32 devices in a mesh: slab: 8 (over z, x), pencil: 4 (over y, core).
Axes of the slice: x: 2, y: 2, z: 4, core: 2. Of those that a mesh axis runs over, the one named last changes fastest.
Arguments:
- potential: float32 [32, 128, 256], P('slab', 'pencil'), may hold values from -2.5 to 2.5
- parent_store: float32 [32, 2, 4, 128], P('slab', None, None, 'pencil'), may hold values from -520 to 520
- face_owner: int32 [8], replicated, may hold values from 0 to 7, as said below
- face_offset: int32 [8], replicated, may hold values from 0 to 3
Outputs:
- second_potential: float32 [32, 128, 256], P('slab', 'pencil')
- source: float32 [32, 128, 256], P('slab', 'pencil')
The draws below stay inside these ranges and needn't reach their ends.
Inputs may be any that keep to these rules, and one draw needn't show every extreme that they name: The pairs (face_owner, face_offset) are all different; in every draw one owner holds exactly 4 slabs' faces.
All inputs are finite; a program needn't handle non-finite values.
Results may differ from the reference program's by a relative error of at most 0.0003.
Values sent between devices are 32-bit elements; how exact they have to be, the bound alone decides.
No kernel may reach another device: no remote copies, remote signals or barrier semaphores. Data moves between devices by JAX's collectives and lax.ppermute only.
A program may use at most 128 MiB of HBM per device.

```python
import math
import jax
import jax.numpy as jnp

CZ = 4
NX = 256
CYCLES = 2
SLOTS = 4
SLABS = 8
NZ = 32
NY = 128


def owner_table(key):
    base = jax.random.fold_in(key, 7)
    key_heavy, key_order, key_rest = jax.random.split(base, 3)
    heavy = jax.random.randint(key_heavy, (), 0, SLABS).astype(jnp.int32)
    order = jax.random.permutation(key_order, SLABS).astype(jnp.int32)
    rest = jax.random.permutation(key_rest, (SLABS - 1) * SLOTS)[:SLABS - SLOTS].astype(jnp.int32)
    rest_owner = rest // SLOTS
    rest_owner = rest_owner + (rest_owner >= heavy).astype(jnp.int32)
    rest_offset = rest % SLOTS
    owners_ranked = jnp.concatenate([jnp.full((SLOTS,), heavy, jnp.int32), rest_owner])
    offsets_ranked = jnp.concatenate([jnp.arange(SLOTS, dtype=jnp.int32), rest_offset])
    owners = jnp.zeros((SLABS,), jnp.int32).at[order].set(owners_ranked)
    offsets = jnp.zeros((SLABS,), jnp.int32).at[order].set(offsets_ranked)
    return (owners, offsets)


def draw_face_owner(key, part):
    return owner_table(key)[0]


def draw_face_offset(key, part):
    return owner_table(key)[1]


def draw_parent_store(key, part):
    base = jax.random.fold_in(key, 11)
    key_level = jax.random.fold_in(base, 0)
    key_phase = jax.random.fold_in(base, 2)
    key_rough = jax.random.fold_in(base, 3)
    row_count = SLOTS * SLABS
    yaxis = jnp.arange(NY, dtype=jnp.float32)[None, None, None, :]
    phase = jax.random.uniform(key_phase, (row_count, 2, 1, 1), jnp.float32, -math.pi, math.pi)
    level = jax.random.uniform(key_level, (row_count, 2, 1, 1), jnp.float32, -100.0, 100.0)
    profile = 1.0 + 0.5 * jnp.cos(2.0 * math.pi * yaxis / NY + phase)
    rough = jax.random.uniform(key_rough, (row_count, 2, CZ, NY), jnp.float32, -3.0, 3.0)
    return (level * profile + rough).astype(jnp.float32)


def levels(rng, extent, shards, smallest, high):
    def one(position, shards_of):
        heights = jax.random.uniform(jax.random.fold_in(jax.random.fold_in(rng, 6), position), (shards_of,), jnp.float32, smallest / len(shards), high / len(shards))
        return jnp.repeat(jnp.exp(heights), extent[position] // shards_of).reshape((-1,) + (1,) * (len(extent) - position - 1))

    gain = one(*shards[0])
    for cut in shards[1:]:
        gain = gain * one(*cut)
    return gain


def normal_values(own_key, shape, width, reach, cuts=(), held_as=jnp.bfloat16):
    values = jax.random.normal(own_key, shape, jnp.float32) * width
    if len(cuts) > 0:
        values = levels(own_key, shape, cuts, -0.22, 0.18) * values
    return jnp.clip(values, min=-reach, max=reach).astype(held_as)


def setup_inputs(seed: int = 0) -> dict:
    key_list = jax.random.split(jax.random.key(seed), 5)
    potential = normal_values(key_list[0], (NZ, NY, NX), 0.4, 2.5, ((0, 8), (1, 4)), jnp.float32)
    parent_store = draw_parent_store(jax.random.fold_in(key_list[4], 71), 0)
    face_owner = draw_face_owner(jax.random.fold_in(key_list[4], 71), 0)
    face_offset = draw_face_offset(jax.random.fold_in(key_list[4], 71), 0)
    return {"potential": potential, "parent_store": parent_store, "face_owner": face_owner, "face_offset": face_offset}


OMEGA = 0.8


def hessian_source(p):
    c = p[1:-1, 1:-1, 1:-1]
    pxx = p[1:-1, 1:-1, 2:] + p[1:-1, 1:-1, :-2] - 2.0 * c
    pyy = p[1:-1, 2:, 1:-1] + p[1:-1, :-2, 1:-1] - 2.0 * c
    pzz = p[2:, 1:-1, 1:-1] + p[:-2, 1:-1, 1:-1] - 2.0 * c
    pxy = 0.25 * (p[1:-1, 2:, 2:] - p[1:-1, :-2, 2:] - p[1:-1, 2:, :-2] + p[1:-1, :-2, :-2])
    pxz = 0.25 * (p[2:, 1:-1, 2:] - p[:-2, 1:-1, 2:] - p[2:, 1:-1, :-2] + p[:-2, 1:-1, :-2])
    pyz = 0.25 * (p[2:, 2:, 1:-1] - p[:-2, 2:, 1:-1] - p[2:, :-2, 1:-1] + p[:-2, :-2, 1:-1])
    return pxx * pyy + pxx * pzz + pyy * pzz - pxy * pxy - pxz * pxz - pyz * pyz


def apply_padded(p, level):
    c = p[1:-1, 1:-1, 1:-1]
    near = p[2:, 1:-1, 1:-1] + p[:-2, 1:-1, 1:-1]
    near = near + p[1:-1, 2:, 1:-1] + p[1:-1, :-2, 1:-1]
    near = near + p[1:-1, 1:-1, 2:] + p[1:-1, 1:-1, :-2]
    return (6.0 * c - near) * (0.25 ** level)


def step_weight(level):
    return OMEGA / 6.0 * 4.0 ** level


def sweep_whole(u, rhs, level):
    return u + step_weight(level) * (rhs - apply_padded(jnp.pad(u, 1), level))


def restrict(r):
    a, b, c = r.shape
    return r.reshape(a // 2, 2, b // 2, 2, c // 2, 2).mean(axis=(1, 3, 5))


def prolong(e):
    a, b, c = e.shape
    return jnp.broadcast_to(e[:, None, :, None, :, None], (a, 2, b, 2, c, 2)).reshape(2 * a, 2 * b, 2 * c)


def is_coarsest(shape):
    return min(shape) <= 4 or any(d % 2 for d in shape)


def vcycle(u, rhs, level):
    if is_coarsest(rhs.shape):
        for sweep_count in range(8):
            u = sweep_whole(u, rhs, level)
        return u
    u = sweep_whole(u, rhs, level)
    u = sweep_whole(u, rhs, level)
    resid = rhs - apply_padded(jnp.pad(u, 1), level)
    coarse = restrict(resid)
    correction = vcycle(jnp.zeros_like(coarse), coarse, level + 1)
    u = u + prolong(correction)
    u = sweep_whole(u, rhs, level)
    u = sweep_whole(u, rhs, level)
    return u


def reference(potential, parent_store, face_owner, face_offset):
    source = hessian_source(jnp.pad(potential, 1))
    rows = face_owner * SLOTS + face_offset
    tiles = jnp.take(parent_store, rows, axis=0)
    low = tiles[:, 0].reshape(NZ, NY)
    high = tiles[:, 1].reshape(NZ, NY)
    rhs = -source
    rhs = rhs.at[:, :, 0].add(low)
    rhs = rhs.at[:, :, NX - 1].add(high)
    solved = jnp.zeros_like(rhs)
    for cycle in range(CYCLES):
        solved = vcycle(solved, rhs, 0)
    return solved, source
```

```python
from functools import partial

import jax
import jax.numpy as jnp
from jax import lax
from jax.experimental import pallas as pl
from jax.experimental.pallas import tpu as pltpu
from jax.sharding import PartitionSpec as P

CYCLES = 2
OMEGA = 0.8
W = OMEGA / 6.0
KEEP = 1.0 - OMEGA
HALO = 8
LANES = 128
HIGHEST = lax.Precision.HIGHEST


def is_coarsest(shape):
    return min(shape) <= 4 or any((d % 2 for d in shape))


def lane_iota(shape):
    return lax.broadcasted_iota(jnp.int32, shape, len(shape) - 1)


def row_iota(shape):
    return lax.broadcasted_iota(jnp.int32, shape, len(shape) - 2)


def halves(plane):
    return plane[:, :LANES], plane[:, LANES:]


def left_right(plane):
    a, b = halves(plane)
    lane = lane_iota(a.shape)
    first = lane == 0
    last = lane == LANES - 1
    a1 = pltpu.roll(a, 1, 1)
    b1 = pltpu.roll(b, 1, 1)
    am = pltpu.roll(a, LANES - 1, 1)
    bm = pltpu.roll(b, LANES - 1, 1)
    left = jnp.concatenate([jnp.where(first, 0.0, a1), jnp.where(first, a1, b1)], axis=1)
    right = jnp.concatenate([jnp.where(last, bm, am), jnp.where(last, 0.0, bm)], axis=1)
    return left, right


def down_up(plane):
    rows = plane.shape[0]
    return pltpu.roll(plane, 1, 0), pltpu.roll(plane, rows - 1, 0)


def swept(below, here, above, q):
    left, right = left_right(here)
    down, up = down_up(here)
    near = (below + above) + (left + right) + (down + up)
    return KEEP * here + W * near + q


def pair_rows(ref, count):
    return ref[pl.ds(0, count, stride=2), :] + ref[pl.ds(1, count, stride=2), :]


def spread_rows(ref, values):
    count = values.shape[0]
    ref[pl.ds(0, count, stride=2), :] = values
    ref[pl.ds(1, count, stride=2), :] = values


def halving_matrix(rows, columns):
    i = lax.broadcasted_iota(jnp.int32, (rows, columns), 0)
    j = lax.broadcasted_iota(jnp.int32, (rows, columns), 1)
    return jnp.where(i // 2 == j, 0.5, 0.0)


def doubling_matrix(rows, columns):
    i = lax.broadcasted_iota(jnp.int32, (rows, columns), 0)
    j = lax.broadcasted_iota(jnp.int32, (rows, columns), 1)
    return jnp.where(i == j // 2, 1.0, 0.0)


def mm(a, b):
    return lax.dot_general(
        a, b, (((1,), (0,)), ((), ())), precision=HIGHEST, preferred_element_type=jnp.float32
    )


def flat_sweep(u, q, shape):
    zs, ys, xs = shape
    rows = zs * ys
    zero = jnp.zeros((ys, LANES), jnp.float32)
    below = jnp.concatenate([zero, u[: rows - ys]], axis=0)
    above = jnp.concatenate([u[ys:], zero], axis=0)
    y = row_iota(u.shape) % ys
    lane = lane_iota(u.shape)
    down = jnp.where(y == 0, 0.0, pltpu.roll(u, 1, 0))
    up = jnp.where(y == ys - 1, 0.0, pltpu.roll(u, rows - 1, 0))
    left = pltpu.roll(u, 1, 1)
    right = pltpu.roll(u, LANES - 1, 1)
    out = KEEP * u + W * ((below + above) + (down + up) + (left + right)) + q
    return jnp.where(lane < xs, out, 0.0)


def flat_vcycle(q, shape, tmp_ref):
    if is_coarsest(shape):
        u = q
        for _ in range(7):
            u = flat_sweep(u, q, shape)
        return u
    zs, ys, xs = shape
    u = flat_sweep(q, q, shape)
    change = flat_sweep(u, q, shape) - u
    pairs = [
        change[2 * z * ys : (2 * z + 1) * ys] + change[(2 * z + 1) * ys : (2 * z + 2) * ys]
        for z in range(zs // 2)
    ]
    half = zs * ys // 2
    tmp_ref[pl.ds(0, half), :] = jnp.concatenate(pairs, axis=0)
    coarse = mm(pair_rows(tmp_ref, half // 2), halving_matrix(LANES, LANES))
    coarse_shape = (zs // 2, ys // 2, xs // 2)
    e = flat_vcycle(coarse, coarse_shape, tmp_ref)
    spread_rows(tmp_ref, mm(e, doubling_matrix(LANES, LANES)))
    wide = tmp_ref[pl.ds(0, half), :]
    planes = []
    for z in range(zs // 2):
        planes += [wide[z * ys : (z + 1) * ys]] * 2
    u = u + jnp.concatenate(planes, axis=0)
    u = flat_sweep(u, q, shape)
    return flat_sweep(u, q, shape)


def solve_level_one(gathered_ref, q_ref, a_ref, b_ref, tmp_ref, shape):
    zs, ys, xs = shape
    pencils, _, part, _ = gathered_ref.shape
    inner = pl.ds(HALO, ys)
    row = row_iota((ys, LANES))
    lane = lane_iota((ys, LANES))
    a_ref[...] = jnp.zeros_like(a_ref)
    b_ref[...] = jnp.zeros_like(b_ref)
    q_ref[pl.ds(0, 1)] = jnp.zeros((1,) + q_ref.shape[1:], jnp.float32)
    q_ref[pl.ds(zs + 1, 1)] = jnp.zeros((1,) + q_ref.shape[1:], jnp.float32)
    for part_index in range(pencils):
        q_ref[pl.ds(1, zs), pl.ds(HALO + part_index * part, part), :] = gathered_ref[part_index]

    def sweep_plane(src, z):
        here = src[z, inner, :]
        below = src[z - 1, inner, :]
        above = src[z + 1, inner, :]
        down = jnp.where(row == 0, 0.0, pltpu.roll(here, 1, 0))
        up = jnp.where(row == ys - 1, 0.0, pltpu.roll(here, ys - 1, 0))
        left = jnp.where(lane == 0, 0.0, pltpu.roll(here, 1, 1))
        right = jnp.where(lane == LANES - 1, 0.0, pltpu.roll(here, LANES - 1, 1))
        near = (below + above) + (down + up) + (left + right)
        return here, KEEP * here + W * near + q_ref[z, inner, :]

    def sweep(src, dst):
        def body(z, carry):
            dst[z, inner, :] = sweep_plane(src, z)[1]
            return carry

        lax.fori_loop(1, zs + 1, body, 0)

    sweep(q_ref, a_ref)

    def restrict(z, carry):
        h0, s0 = sweep_plane(a_ref, 2 * z + 1)
        h1, s1 = sweep_plane(a_ref, 2 * z + 2)
        tmp_ref[pl.ds(pl.multiple_of(z * ys, ys), ys), :] = (s0 - h0) + (s1 - h1)
        return carry

    lax.fori_loop(0, zs // 2, restrict, 0)
    coarse_shape = (zs // 2, ys // 2, xs // 2)
    coarse = mm(
        pair_rows(tmp_ref, coarse_shape[0] * coarse_shape[1]), halving_matrix(LANES, LANES)
    )
    e = flat_vcycle(coarse, coarse_shape, tmp_ref)
    spread_rows(tmp_ref, mm(e, doubling_matrix(LANES, LANES)))

    def correct(z, carry):
        wide = tmp_ref[pl.ds(pl.multiple_of(z * ys, ys), ys), :]
        a_ref[2 * z + 1, inner, :] = a_ref[2 * z + 1, inner, :] + wide
        a_ref[2 * z + 2, inner, :] = a_ref[2 * z + 2, inner, :] + wide
        return carry

    lax.fori_loop(0, zs // 2, correct, 0)
    sweep(a_ref, b_ref)
    sweep(b_ref, a_ref)


def pack_kernel(potential_ref, store_ref, out_ref):
    depth, width, columns = potential_ref.shape
    slots, _, _, _ = store_ref.shape
    for z in range(depth):
        out_ref[pl.ds(z * width, width), :] = potential_ref[z]
    base = depth * width
    out_ref[pl.ds(base, 8), :] = jnp.zeros((8, columns), jnp.float32)
    for slot in range(slots):
        for side in range(2):
            out_ref[pl.ds(base + side * depth, depth), pl.ds(slot * width, width)] = store_ref[
                slot, side
            ]


def blocks_of(own_ref, far_ref, others):
    out = [(0, own_ref, None), (4, far_ref, None)]
    for offset, ref in others:
        out += [(offset, ref, 0), (offset ^ 4, ref, 1)]
    return out


def block_rows(ref, index, start, count):
    if index is None:
        return ref[pl.ds(start, count), :]
    return ref[index, pl.ds(start, count), :]


def edges_kernel(
    where_ref, owner_ref, offset_ref, own_ref, far_ref, r1_ref, r2_ref, r3_ref,
    even_ref, odd_ref, faces_ref, store_ref, rows_ref, *, depth, width
):
    slab = where_ref[0]
    pencil = where_ref[1]
    slabs = owner_ref.shape[0]
    planes = slabs * depth
    is_even = (pencil % 2) == 0
    blocks = blocks_of(own_ref, far_ref, [(1, r1_ref), (2, r2_ref), (3, r3_ref)])
    base = depth * width
    for offset, ref, index in blocks:
        target = slab ^ offset
        store_ref[target] = block_rows(ref, index, base, 8)[:, :LANES]
        for z in range(depth):
            head = block_rows(ref, index, z * width, HALO)
            tail = block_rows(ref, index, (z + 1) * width - HALO, HALO)
            even_ref[target * depth + z] = jnp.where(is_even, tail, head)
            odd_ref[target * depth + z] = jnp.where(is_even, head, tail)
    rows_ref[...] = jnp.zeros_like(rows_ref)
    for s in range(slabs):
        tile = store_ref[owner_ref[s]]
        slot = offset_ref[s]
        picked = jnp.zeros((8, width), jnp.float32)
        for k in range(LANES // width):
            picked = jnp.where(slot == k, tile[:, k * width : (k + 1) * width], picked)
        rows_ref[pl.ds(s * depth, depth), pl.ds(0, width)] = picked[:depth]
        rows_ref[pl.ds(planes + s * depth, depth), pl.ds(0, width)] = picked[depth:]
    faces = rows_ref[...].T
    faces_ref[...] = faces[:width]
    head = faces[:HALO]
    tail = faces[width - HALO : width]
    blank = jnp.zeros((HALO, LANES), jnp.float32)
    even_ref[planes] = jnp.concatenate([jnp.where(is_even, tail, head), blank], axis=1)
    odd_ref[planes] = jnp.concatenate([jnp.where(is_even, head, tail), blank], axis=1)


def first_kernel(
    where_ref, own_ref, far_ref, r1_ref, r2_ref, r3_ref, even_ref, odd_ref, faces_ref,
    source_ref, q_ref, u_ref, coarse_ref, p_ref, f_ref, left_ref, right_ref,
    *, depth, width, height
):
    slab = where_ref[0]
    pencil = where_ref[1]
    planes = p_ref.shape[0] - 2
    rows = width + 2 * HALO
    columns = p_ref.shape[2]
    is_even = (pencil % 2) == 0
    blank = jnp.zeros((rows, columns), jnp.float32)
    p_ref[0] = blank
    p_ref[planes + 1] = blank
    for ref in (q_ref, u_ref):
        for z in (0, 1, planes + 2, planes + 3):
            ref[z] = blank
    for offset, ref, index in blocks_of(own_ref, far_ref, [(1, r1_ref), (2, r2_ref), (3, r3_ref)]):
        target = (slab ^ offset) * depth + 1
        for z in range(depth):
            p_ref[target + z, pl.ds(HALO, width), :] = block_rows(ref, index, z * width, width)

    def edges(z, carry):
        first = even_ref[z]
        second = odd_ref[z]
        p_ref[z + 1, pl.ds(0, HALO), :] = jnp.where(is_even, second, first)
        p_ref[z + 1, pl.ds(HALO + width, HALO), :] = jnp.where(is_even, first, second)
        return carry

    lax.fori_loop(0, planes, edges, 0)
    first = even_ref[planes][:, :LANES]
    second = odd_ref[planes][:, :LANES]
    f_ref[pl.ds(0, HALO), :] = jnp.where(is_even, second, first)
    f_ref[pl.ds(HALO, width), :] = faces_ref[...]
    f_ref[pl.ds(HALO + width, HALO), :] = jnp.where(is_even, first, second)

    y = lax.broadcasted_iota(jnp.int32, (rows, columns), 0) + pencil * width - HALO
    inside = jnp.where((y >= 0) & (y < height), 1.0, 0.0)
    lane = lane_iota((rows, LANES))

    def hessian(z, carry):
        below = p_ref[z]
        here = p_ref[z + 1]
        above = p_ref[z + 2]
        left, right = left_right(here)
        down, up = down_up(here)
        pxx = left + right - 2.0 * here
        pyy = down + up - 2.0 * here
        pzz = below + above - 2.0 * here
        rise = above - below
        left, right = left_right(rise)
        pxz = right - left
        d, u = down_up(rise)
        pyz = u - d
        left, right = left_right(up - down)
        pxy = right - left
        cross = pxy * pxy + pxz * pxz + pyz * pyz
        source = pxx * pyy + (pxx + pyy) * pzz - 0.0625 * cross

        @pl.when(z // depth == slab)
        def _():
            source_ref[z % depth] = source[HALO : HALO + width]

        faces = f_ref[...]
        low = jnp.where(lane == 0, pltpu.roll(faces, (LANES - z) & (LANES - 1), 1), 0.0)
        high = jnp.where(lane == LANES - 1, pltpu.roll(faces, LANES - 1 - planes - z, 1), 0.0)
        q_ref[z + 2] = (W * inside) * (jnp.concatenate([low, high], axis=1) - source)
        return carry

    lax.fori_loop(0, planes, hessian, 0)

    def second_sweep(z, carry):
        here = q_ref[z + 2]
        u_ref[z + 2] = inside * swept(q_ref[z + 1], here, q_ref[z + 3], here)
        return carry

    lax.fori_loop(0, planes, second_sweep, 0)
    restrict_window(u_ref, q_ref, coarse_ref, left_ref, right_ref, planes, width)


def restrict_window(u_ref, q_ref, coarse_ref, left_ref, right_ref, planes, width):
    def change(z):
        here = u_ref[z + 2]
        return swept(u_ref[z + 1], here, u_ref[z + 3], q_ref[z + 2]) - here

    def restrict(z, carry):
        both = (change(2 * z) + change(2 * z + 1))[HALO : HALO + width]
        spot = pl.ds(pl.multiple_of(z * width, width), width)
        left_ref[spot, :] = both[:, :LANES]
        right_ref[spot, :] = both[:, LANES:]
        return carry

    lax.fori_loop(0, planes // 2, restrict, 0)
    count = planes // 2 * width // 2
    wide = jnp.concatenate([pair_rows(left_ref, count), pair_rows(right_ref, count)], axis=1)
    coarse_ref[...] = mm(wide, halving_matrix(2 * LANES, LANES))


def prolong_planes(v_ref, left_ref, right_ref, pencil, width, start, count):
    part = width // 2
    rows = part + 2 * HALO
    spot = pl.ds(pl.multiple_of(pencil * part, part), rows)
    e = v_ref[pl.ds(start, count), spot, :].reshape(count * rows, LANES)
    wide = mm(e, doubling_matrix(LANES, 2 * LANES))
    spread_rows(left_ref, wide[:, :LANES])
    spread_rows(right_ref, wide[:, LANES:])


def prolonged(left_ref, right_ref, z, width):
    rows = width + 4 * HALO
    spot = pl.ds(pl.multiple_of(z * rows + HALO, HALO), width + 2 * HALO)
    return jnp.concatenate([left_ref[spot, :], right_ref[spot, :]], axis=1)


def middle_kernel(
    where_ref, gathered_ref, q_ref, u_ref, qwin_ref, uwin_ref, coarse_ref,
    q1_ref, a1_ref, b1_ref, tmp_ref, left_ref, right_ref, a_ref, b_ref,
    *, depth, width, height, shape
):
    slab = where_ref[0]
    pencil = where_ref[1]
    planes = a_ref.shape[0] - 4
    rows = width + 2 * HALO
    columns = a_ref.shape[2]
    solve_level_one(gathered_ref, q1_ref, a1_ref, b1_ref, tmp_ref, shape)
    prolong_planes(a1_ref, left_ref, right_ref, pencil, width, 1, planes // 2)
    blank = jnp.zeros((rows, columns), jnp.float32)
    for ref in (a_ref, b_ref):
        for z in (0, 1, planes + 2, planes + 3):
            ref[z] = blank

    def correct(z, carry):
        wide = prolonged(left_ref, right_ref, z, width)
        a_ref[2 * z + 2] = u_ref[2 * z + 2] + wide
        a_ref[2 * z + 3] = u_ref[2 * z + 3] + wide
        return carry

    lax.fori_loop(0, planes // 2, correct, 0)
    y = lax.broadcasted_iota(jnp.int32, (rows, columns), 0) + pencil * width - HALO
    inside = jnp.where((y >= 0) & (y < height), 1.0, 0.0)

    def sweep(src, dst):
        def body(z, carry):
            dst[z + 2] = inside * swept(src[z + 1], src[z + 2], src[z + 3], q_ref[z + 2])
            return carry

        lax.fori_loop(0, planes, body, 0)

    sweep(a_ref, b_ref)
    sweep(b_ref, a_ref)
    sweep(a_ref, b_ref)
    sweep(b_ref, a_ref)
    restrict_window(a_ref, q_ref, coarse_ref, left_ref, right_ref, planes, width)
    for z in range(depth + 4):
        qwin_ref[z] = q_ref[slab * depth + z]
        uwin_ref[z] = a_ref[slab * depth + z]


def last_kernel(
    where_ref, gathered_ref, qwin_ref, uwin_ref, out_ref,
    q1_ref, a1_ref, b1_ref, tmp_ref, left_ref, right_ref, a_ref, b_ref,
    *, depth, width, height, shape
):
    slab = where_ref[0]
    pencil = where_ref[1]
    planes = shape[0] * 2
    rows = width + 2 * HALO
    columns = a_ref.shape[2]
    solve_level_one(gathered_ref, q1_ref, a1_ref, b1_ref, tmp_ref, shape)
    coarse = depth // 2 + 2
    prolong_planes(a1_ref, left_ref, right_ref, pencil, width, slab * (depth // 2), coarse)
    for z in range(coarse):
        wide = prolonged(left_ref, right_ref, z, width)
        a_ref[2 * z] = uwin_ref[2 * z] + wide
        a_ref[2 * z + 1] = uwin_ref[2 * z + 1] + wide
    y = lax.broadcasted_iota(jnp.int32, (rows, columns), 0) + pencil * width - HALO
    inside = jnp.where((y >= 0) & (y < height), 1.0, 0.0)
    for z in range(1, depth + 3):
        at = slab * depth - 2 + z
        live = jnp.where((at >= 0) & (at < planes), inside, 0.0)
        b_ref[z] = live * swept(a_ref[z - 1], a_ref[z], a_ref[z + 1], qwin_ref[z])
    for z in range(2, depth + 2):
        new = swept(b_ref[z - 1], b_ref[z], b_ref[z + 1], qwin_ref[z])
        out_ref[z - 2] = new[HALO : HALO + width]


def vmem():
    return pl.BlockSpec(memory_space=pltpu.VMEM)


def smem():
    return pl.BlockSpec(memory_space=pltpu.SMEM)


def arr(*shape):
    return jax.ShapeDtypeStruct(shape, jnp.float32)


def buf(*shape):
    return pltpu.VMEM(shape, jnp.float32)


def call(kernel, name, scalars, args, outs, scratch=()):
    return pl.pallas_call(
        kernel,
        out_shape=outs,
        in_specs=[smem()] * len(scalars) + [vmem()] * len(args),
        out_specs=jax.tree.map(lambda _: vmem(), outs),
        scratch_shapes=list(scratch),
        compiler_params=pltpu.CompilerParams(vmem_limit_bytes=48 << 20),
        name=name,
    )(*scalars, *args)


def windowed(potential, parent_store, face_owner, face_offset):
    depth, width, columns = potential.shape
    slabs = lax.axis_size("slab")
    pencils = lax.axis_size("pencil")
    planes, height = slabs * depth, pencils * width
    rows = width + 2 * HALO
    where = jnp.stack([lax.axis_index("slab"), lax.axis_index("pencil")]).astype(jnp.int32)
    own = call(
        pack_kernel, "pack", [], [potential, parent_store], arr(depth * width + 8, columns)
    )

    def swap(x, bits):
        return lax.ppermute(x, "slab", [(i, i ^ bits) for i in range(slabs)])

    far = swap(own, 4)
    both = jnp.stack([own, far])
    others = [swap(both, bits) for bits in (1, 2, 3)]

    even, odd, faces = call(
        partial(edges_kernel, depth=depth, width=width),
        "edges",
        [where, face_owner, face_offset],
        [own, far, *others],
        (arr(planes + 1, HALO, columns), arr(planes + 1, HALO, columns), arr(width, LANES)),
        [buf(slabs, 8, LANES), buf(LANES, LANES)],
    )
    low_pairs = [(i, i + 1) for i in range(0, pencils - 1, 2)]
    high_pairs = [(i, i + 1) for i in range(1, pencils - 1, 2)]
    even = lax.ppermute(even, "pencil", low_pairs + [(j, i) for i, j in low_pairs])
    odd = lax.ppermute(odd, "pencil", high_pairs + [(j, i) for i, j in high_pairs])
    shape = (planes // 2, height // 2, columns // 2)
    part = arr(planes // 2 * (width // 2), columns // 2)
    field = (planes + 4, rows, columns)
    half_rows = planes // 2 * (width + 4 * HALO)
    source, q, u, coarse = call(
        partial(first_kernel, depth=depth, width=width, height=height),
        "first",
        [where],
        [own, far, *others, even, odd, faces],
        (arr(depth, width, columns), arr(*field), arr(*field), part),
        [
            buf(planes + 2, rows, columns),
            buf(rows, LANES),
            buf(planes // 2 * width, LANES),
            buf(planes // 2 * width, LANES),
        ],
    )
    level = (shape[0] + 2, shape[1] + 2 * HALO, LANES)
    level_scratch = [
        buf(*level),
        buf(*level),
        buf(*level),
        buf(shape[0] * shape[1], LANES),
        buf(half_rows, LANES),
        buf(half_rows, LANES),
    ]

    def gather(x):
        whole = lax.all_gather(x, "pencil", axis=0, tiled=False)
        return whole.reshape(pencils, shape[0], width // 2, columns // 2)

    sizes = dict(depth=depth, width=width, height=height, shape=shape)
    slim = (depth + 4, rows, columns)
    qwin, uwin, coarse = call(
        partial(middle_kernel, **sizes),
        "middle",
        [where],
        [gather(coarse), q, u],
        (arr(*slim), arr(*slim), part),
        level_scratch + [buf(*field), buf(*field)],
    )
    solved = call(
        partial(last_kernel, **sizes),
        "last",
        [where],
        [gather(coarse), qwin, uwin],
        arr(depth, width, columns),
        level_scratch + [buf(*slim), buf(*slim)],
    )
    return solved, source


def fits_window(potential, parent_store):
    depth, width, columns = potential.shape
    slabs = lax.axis_size("slab")
    pencils = lax.axis_size("pencil")
    planes = slabs * depth
    return (
        slabs == 8
        and pencils % 2 == 0
        and depth == 4
        and columns == 2 * LANES
        and width == 32
        and parent_store.shape[0] * width == LANES
        and 2 * planes <= LANES
        and pencils <= 8
    )


def padded(cells, sides, width):
    for axis, dim in sides:
        count = lax.axis_size(axis)
        ends = count - 1
        head = lax.slice_in_dim(cells, 0, width, axis=dim)
        tail = lax.slice_in_dim(cells, cells.shape[dim] - width, cells.shape[dim], axis=dim)
        cells = jnp.concatenate(
            [
                lax.ppermute(tail, axis, [(i, (i + 1) % count) for i in range(ends)]),
                cells,
                lax.ppermute(head, axis, [((i + 1) % count, i) for i in range(ends)]),
            ],
            axis=dim,
        )
    return cells


def hessian_source(p):
    c = p[1:-1, 1:-1, 1:-1]
    pxx = p[1:-1, 1:-1, 2:] + p[1:-1, 1:-1, :-2] - 2.0 * c
    pyy = p[1:-1, 2:, 1:-1] + p[1:-1, :-2, 1:-1] - 2.0 * c
    pzz = p[2:, 1:-1, 1:-1] + p[:-2, 1:-1, 1:-1] - 2.0 * c
    pxy = 0.25 * (p[1:-1, 2:, 2:] - p[1:-1, :-2, 2:] - p[1:-1, 2:, :-2] + p[1:-1, :-2, :-2])
    pxz = 0.25 * (p[2:, 1:-1, 2:] - p[:-2, 1:-1, 2:] - p[2:, 1:-1, :-2] + p[:-2, 1:-1, :-2])
    pyz = 0.25 * (p[2:, 2:, 1:-1] - p[:-2, 2:, 1:-1] - p[2:, :-2, 1:-1] + p[:-2, :-2, 1:-1])
    return pxx * pyy + pxx * pzz + pyy * pzz - pxy * pxy - pxz * pxz - pyz * pyz


def apply_padded(p, level):
    c = p[1:-1, 1:-1, 1:-1]
    near = p[2:, 1:-1, 1:-1] + p[:-2, 1:-1, 1:-1]
    near = near + p[1:-1, 2:, 1:-1] + p[1:-1, :-2, 1:-1]
    near = near + p[1:-1, 1:-1, 2:] + p[1:-1, 1:-1, :-2]
    return (6.0 * c - near) * 0.25**level


def step_weight(level):
    return OMEGA / 6.0 * 4.0**level


def sweep_whole(u, rhs, level):
    return u + step_weight(level) * (rhs - apply_padded(jnp.pad(u, 1), level))


def restrict(r):
    a, b, c = r.shape
    return r.reshape(a // 2, 2, b // 2, 2, c // 2, 2).mean(axis=(1, 3, 5))


def prolong(e):
    a, b, c = e.shape
    return jnp.broadcast_to(e[:, None, :, None, :, None], (a, 2, b, 2, c, 2)).reshape(
        2 * a, 2 * b, 2 * c
    )


def vcycle(u, rhs, level):
    if is_coarsest(rhs.shape):
        for sweep_count in range(8):
            u = sweep_whole(u, rhs, level)
        return u
    u = sweep_whole(u, rhs, level)
    u = sweep_whole(u, rhs, level)
    resid = rhs - apply_padded(jnp.pad(u, 1), level)
    coarse = restrict(resid)
    correction = vcycle(jnp.zeros_like(coarse), coarse, level + 1)
    u = u + prolong(correction)
    u = sweep_whole(u, rhs, level)
    u = sweep_whole(u, rhs, level)
    return u


def widen_x(p):
    return jnp.pad(p, ((0, 0), (0, 0), (1, 1)))


def rim_one(u):
    return widen_x(padded(u, (("slab", 0), ("pencil", 1)), 1))


def coarse_solve(rhs, level):
    width = rhs.shape[1]
    columns = rhs.shape[2]
    whole = lax.all_gather(rhs, ("slab", "pencil"), axis=0, tiled=True)
    whole = whole.reshape(lax.axis_size("slab"), lax.axis_size("pencil") * width, columns)
    solved = vcycle(jnp.zeros_like(whole), whole, level)
    start_y = lax.axis_index("pencil") * width
    return lax.dynamic_slice(
        solved, (lax.axis_index("slab"), start_y, jnp.int32(0)), (1, width, columns)
    )


def split_vcycle(u, rhs, level, from_zero):
    if rhs.shape[0] == 1:
        return coarse_solve(rhs, level)
    weight = step_weight(level)
    if from_zero:
        u = weight * rhs
    else:
        u = u + weight * (rhs - apply_padded(rim_one(u), level))
    u = u + weight * (rhs - apply_padded(rim_one(u), level))
    resid = rhs - apply_padded(rim_one(u), level)
    correction = split_vcycle(None, restrict(resid), level + 1, True)
    u = u + prolong(correction)
    u = u + weight * (rhs - apply_padded(rim_one(u), level))
    u = u + weight * (rhs - apply_padded(rim_one(u), level))
    return u


def plain(potential, parent_store, face_owner, face_offset):
    depth, width, columns = potential.shape
    grown = widen_x(padded(potential, (("slab", 0), ("pencil", 1)), 1))
    source = hessian_source(grown)
    slab_index = lax.axis_index("slab")
    wanted = face_owner[slab_index] * parent_store.shape[0] + face_offset[slab_index]
    piece = lax.all_gather(parent_store, "slab", axis=0, tiled=True)
    labels = jnp.arange(piece.shape[0], dtype=jnp.int32)
    match = labels == wanted
    faces = jnp.sum(jnp.where(match[:, None, None, None], piece, 0.0), axis=0)
    rhs = -source
    rhs = rhs.at[:, :, 0].add(faces[0])
    rhs = rhs.at[:, :, columns - 1].add(faces[1])
    solved = jnp.zeros_like(rhs)
    for cycle in range(CYCLES):
        solved = split_vcycle(solved, rhs, 0, cycle == 0)
    return (solved, source)


def on_device(potential, parent_store, face_owner, face_offset):
    if fits_window(potential, parent_store):
        return windowed(potential, parent_store, face_owner, face_offset)
    return plain(potential, parent_store, face_owner, face_offset)


def solution(mesh):
    in_specs = (P("slab", "pencil", None), P("slab", None, None, "pencil"), P(), P())
    out_specs = (P("slab", "pencil", None), P("slab", "pencil", None))
    return jax.shard_map(
        on_device, mesh=mesh, in_specs=in_specs, out_specs=out_specs, check_vma=False
    )
```

```python
from functools import partial

import jax
import jax.numpy as jnp
from jax import lax
from jax.experimental import pallas as pl
from jax.experimental.pallas import tpu as pltpu
from jax.sharding import PartitionSpec as P

CYCLES = 2
OMEGA = 0.8
W = OMEGA / 6.0
KEEP = 1.0 - OMEGA
HALO = 8
LANES = 128
UNROLL = 4


def is_coarsest(shape):
    return min(shape) <= 4 or any((d % 2 for d in shape))


def lane_iota(shape):
    return lax.broadcasted_iota(jnp.int32, shape, len(shape) - 1)


def row_iota(shape):
    return lax.broadcasted_iota(jnp.int32, shape, len(shape) - 2)


def x_other(values, odd):
    lane = lane_iota(values.shape)
    if odd:
        return jnp.where(lane == LANES - 1, 0.0, pltpu.roll(values, LANES - 1, 1))
    return jnp.where(lane == 0, 0.0, pltpu.roll(values, 1, 1))


def y_other(values, odd):
    return pltpu.roll(values, values.shape[0] - 1 if odd else 1, 0)


def swept(below, here, above, q, c):
    across, along = here[c ^ 1], here[c ^ 2]
    near = (below + above) + (across + x_other(across, c & 1))
    near = near + (along + y_other(along, c >> 1))
    return KEEP * here[c] + W * near + q


def parts(ref, z):
    return [ref[z, c] for c in range(4)]


def halo_mask(pencil, pencils):
    row = row_iota((8, LANES))
    above = jnp.where(pencil < pencils - 1, 1.0, 0.0)
    below = jnp.where(pencil > 0, 1.0, 0.0)
    return jnp.where(row < 4, above, below)


def put(ref, z, c, values, mask):
    own = values.shape[0] - 8
    ref[z, c, pl.ds(0, own), :] = values[:own]
    ref[z, c, pl.ds(own, 8), :] = values[own:] * mask


def pair_rows(ref, count):
    return ref[pl.ds(0, count, stride=2), :] + ref[pl.ds(1, count, stride=2), :]


def spread_rows(ref, values):
    count = values.shape[0]
    ref[pl.ds(0, count, stride=2), :] = values
    ref[pl.ds(1, count, stride=2), :] = values


def index_pair(rows, columns):
    return (
        lax.broadcasted_iota(jnp.int32, (rows, columns), 0),
        lax.broadcasted_iota(jnp.int32, (rows, columns), 1),
    )


def chosen(where, value):
    return jnp.where(where, value, 0.0).astype(jnp.bfloat16)


def halving_matrix():
    i, j = index_pair(LANES, LANES)
    return chosen(i // 2 == j, 0.5)


def doubling_matrix():
    i, j = index_pair(LANES, LANES)
    return chosen(i == j // 2, 1.0)


def splitting_matrix():
    i, j = index_pair(2 * LANES, 2 * LANES)
    return chosen(i == 2 * (j % LANES) + j // LANES, 1.0)


def merging_matrix():
    i, j = index_pair(2 * LANES, 2 * LANES)
    return chosen(j == 2 * (i % LANES) + i // LANES, 1.0)


def mm(a, b):
    high = a.astype(jnp.bfloat16)
    rest = a - high.astype(jnp.float32)
    middle = rest.astype(jnp.bfloat16)
    low = (rest - middle.astype(jnp.float32)).astype(jnp.bfloat16)

    def dot(x):
        return jnp.dot(x, b, preferred_element_type=jnp.float32)

    return dot(high) + (dot(middle) + dot(low))


def flat_sweep(u, q, shape):
    zs, ys, xs = shape
    rows = zs * ys
    zero = jnp.zeros((ys, LANES), jnp.float32)
    below = jnp.concatenate([zero, u[: rows - ys]], axis=0)
    above = jnp.concatenate([u[ys:], zero], axis=0)
    y = row_iota(u.shape) % ys
    lane = lane_iota(u.shape)
    down = jnp.where(y == 0, 0.0, pltpu.roll(u, 1, 0))
    up = jnp.where(y == ys - 1, 0.0, pltpu.roll(u, rows - 1, 0))
    left = pltpu.roll(u, 1, 1)
    right = pltpu.roll(u, LANES - 1, 1)
    out = KEEP * u + W * ((below + above) + (down + up) + (left + right)) + q
    return jnp.where(lane < xs, out, 0.0)


def flat_vcycle(q, shape, tmp_ref):
    if is_coarsest(shape):
        u = q
        for _ in range(7):
            u = flat_sweep(u, q, shape)
        return u
    zs, ys, xs = shape
    u = flat_sweep(q, q, shape)
    change = flat_sweep(u, q, shape) - u
    pairs = [
        change[2 * z * ys : (2 * z + 1) * ys] + change[(2 * z + 1) * ys : (2 * z + 2) * ys]
        for z in range(zs // 2)
    ]
    half = zs * ys // 2
    tmp_ref[pl.ds(0, half), :] = jnp.concatenate(pairs, axis=0)
    coarse = mm(pair_rows(tmp_ref, half // 2), halving_matrix())
    coarse_shape = (zs // 2, ys // 2, xs // 2)
    e = flat_vcycle(coarse, coarse_shape, tmp_ref)
    spread_rows(tmp_ref, mm(e, doubling_matrix()))
    wide = tmp_ref[pl.ds(0, half), :]
    planes = []
    for z in range(zs // 2):
        planes += [wide[z * ys : (z + 1) * ys]] * 2
    u = u + jnp.concatenate(planes, axis=0)
    u = flat_sweep(u, q, shape)
    return flat_sweep(u, q, shape)


def solve_level_one(gathered_ref, q_ref, a_ref, b_ref, tmp_ref, shape):
    zs, ys, xs = shape
    pencils, _, part, _ = gathered_ref.shape
    inner = pl.ds(HALO, ys)
    row = row_iota((ys, LANES))
    lane = lane_iota((ys, LANES))
    a_ref[...] = jnp.zeros_like(a_ref)
    b_ref[...] = jnp.zeros_like(b_ref)
    q_ref[pl.ds(0, 1)] = jnp.zeros((1,) + q_ref.shape[1:], jnp.float32)
    q_ref[pl.ds(zs + 1, 1)] = jnp.zeros((1,) + q_ref.shape[1:], jnp.float32)
    for part_index in range(pencils):
        q_ref[pl.ds(1, zs), pl.ds(HALO + part_index * part, part), :] = gathered_ref[part_index]

    def sweep_plane(src, z):
        here = src[z, inner, :]
        below = src[z - 1, inner, :]
        above = src[z + 1, inner, :]
        down = jnp.where(row == 0, 0.0, pltpu.roll(here, 1, 0))
        up = jnp.where(row == ys - 1, 0.0, pltpu.roll(here, ys - 1, 0))
        left = jnp.where(lane == 0, 0.0, pltpu.roll(here, 1, 1))
        right = jnp.where(lane == LANES - 1, 0.0, pltpu.roll(here, LANES - 1, 1))
        near = (below + above) + (down + up) + (left + right)
        return here, KEEP * here + W * near + q_ref[z, inner, :]

    def sweep(src, dst):
        def body(z, carry):
            dst[z, inner, :] = sweep_plane(src, z)[1]
            return carry

        lax.fori_loop(1, zs + 1, body, 0, unroll=UNROLL)

    sweep(q_ref, a_ref)

    def restrict(z, carry):
        h0, s0 = sweep_plane(a_ref, 2 * z + 1)
        h1, s1 = sweep_plane(a_ref, 2 * z + 2)
        tmp_ref[pl.ds(pl.multiple_of(z * ys, ys), ys), :] = (s0 - h0) + (s1 - h1)
        return carry

    lax.fori_loop(0, zs // 2, restrict, 0, unroll=2)
    coarse_shape = (zs // 2, ys // 2, xs // 2)
    coarse = mm(
        pair_rows(tmp_ref, coarse_shape[0] * coarse_shape[1]), halving_matrix()
    )
    e = flat_vcycle(coarse, coarse_shape, tmp_ref)
    spread_rows(tmp_ref, mm(e, doubling_matrix()))

    def correct(z, carry):
        wide = tmp_ref[pl.ds(pl.multiple_of(z * ys, ys), ys), :]
        a_ref[2 * z + 1, inner, :] = a_ref[2 * z + 1, inner, :] + wide
        a_ref[2 * z + 2, inner, :] = a_ref[2 * z + 2, inner, :] + wide
        return carry

    lax.fori_loop(0, zs // 2, correct, 0, unroll=2)
    sweep(a_ref, b_ref)
    sweep(b_ref, a_ref)


def pack_kernel(potential_ref, store_ref, out_ref, even_ref, odd_ref):
    depth, width, columns = potential_ref.shape
    slots = store_ref.shape[0]
    part = width // 2
    split = mm(potential_ref[...].reshape(depth * width, columns), splitting_matrix())
    even_ref[...] = split[:, :LANES]
    odd_ref[...] = split[:, LANES:]
    for z in range(depth):
        for c in range(4):
            ref = odd_ref if c & 1 else even_ref
            spot = pl.ds((4 * z + c) * part, part)
            out_ref[spot, :] = ref[pl.ds(z * width + (c >> 1), part, stride=2), :]
    base = depth * width * 2
    for slot in range(slots):
        for side in range(2):
            spot = pl.ds(base + side * depth, depth)
            out_ref[spot, pl.ds(slot * width, width)] = store_ref[slot, side]


def blocks_of(own_ref, far_ref, others):
    out = [(0, own_ref, None), (4, far_ref, None)]
    for offset, ref in others:
        out += [(offset, ref, 0), (offset ^ 4, ref, 1)]
    return out


def block_rows(ref, index, start, count):
    if index is None:
        return ref[pl.ds(start, count), :]
    return ref[index, pl.ds(start, count), :]


def ends(load, first, second, part, low_half):
    head = jnp.where(low_half, load(first, 8), pltpu.roll(load(second, 8), 4, 0))
    tail = jnp.where(
        low_half, pltpu.roll(load(first + part - 8, 8), 4, 0), load(second + part - 8, 8)
    )
    return head, tail


def edges_kernel(
    scalar_ref, own_ref, far_ref, r1_ref, r2_ref, r3_ref,
    even_ref, odd_ref, faces_ref, store_ref, rows_ref, *, depth, width, slabs
):
    slab = scalar_ref[0]
    pencil = scalar_ref[1]
    planes = slabs * depth
    part = width // 2
    is_even = (pencil % 2) == 0
    low_half = row_iota((8, LANES)) < 4
    blocks = blocks_of(own_ref, far_ref, [(1, r1_ref), (2, r2_ref), (3, r3_ref)])
    base = depth * width * 2
    for offset, ref, index in blocks:
        target = slab ^ offset
        store_ref[target] = block_rows(ref, index, base, 8)
        for z in range(depth):
            for t in range(2):
                head, tail = ends(
                    partial(block_rows, ref, index),
                    (4 * z + 2 * t) * part, (4 * z + 2 * t + 1) * part, part, low_half,
                )
                even_ref[2 * (target * depth + z) + t] = jnp.where(is_even, tail, head)
                odd_ref[2 * (target * depth + z) + t] = jnp.where(is_even, head, tail)
    rows_ref[...] = jnp.zeros_like(rows_ref)
    for s in range(slabs):
        tile = store_ref[scalar_ref[2 + s]]
        slot = scalar_ref[2 + slabs + s]
        picked = jnp.zeros((8, width), jnp.float32)
        for k in range(LANES // width):
            picked = jnp.where(slot == k, tile[:, k * width : (k + 1) * width], picked)
        rows_ref[pl.ds(s * depth, depth), pl.ds(0, width)] = picked[:depth]
        rows_ref[pl.ds(planes + s * depth, depth), pl.ds(0, width)] = picked[depth:]
    rows_ref[...] = rows_ref[...].T
    faces_ref[pl.ds(0, part), :] = rows_ref[pl.ds(0, part, stride=2), :]
    faces_ref[pl.ds(part, part), :] = rows_ref[pl.ds(1, part, stride=2), :]
    head, tail = ends(partial(block_rows, faces_ref, None), 0, part, part, low_half)
    even_ref[2 * planes] = jnp.where(is_even, tail, head)
    odd_ref[2 * planes] = jnp.where(is_even, head, tail)


def halo_tiles(even_ref, odd_ref, index, is_even, low_half):
    first = even_ref[index]
    second = odd_ref[index]
    above = jnp.where(is_even, first, second)
    below = jnp.where(is_even, second, first)
    return (
        jnp.where(low_half, above, pltpu.roll(below, 4, 0)),
        jnp.where(low_half, pltpu.roll(above, 4, 0), below),
    )


def join_planes(load, out_ref, left_ref, right_ref, depth, width):
    part = width // 2
    for z in range(depth):
        for c in range(4):
            ref = right_ref if c & 1 else left_ref
            ref[pl.ds(z * width + (c >> 1), part, stride=2), :] = load(z, c)
    rows = depth * width
    both = jnp.concatenate([left_ref[pl.ds(0, rows), :], right_ref[pl.ds(0, rows), :]], axis=1)
    out_ref[...] = mm(both, merging_matrix()).reshape(depth, width, 2 * LANES)


def first_kernel(
    scalar_ref, own_ref, far_ref, r1_ref, r2_ref, r3_ref, even_ref, odd_ref, faces_ref,
    source_ref, q_ref, u_ref, coarse_ref, p_ref, f_ref, s_ref, left_ref, right_ref,
    *, depth, width, pencils
):
    slab = scalar_ref[0]
    pencil = scalar_ref[1]
    planes = p_ref.shape[0] - 2
    part = width // 2
    is_even = (pencil % 2) == 0
    low_half = row_iota((8, LANES)) < 4
    mask = halo_mask(pencil, pencils)
    blank = jnp.zeros(p_ref.shape[1:], jnp.float32)
    p_ref[0] = blank
    p_ref[planes + 1] = blank
    for ref in (q_ref, u_ref):
        for z in (0, 1, planes + 2, planes + 3):
            ref[z] = blank
    for offset, ref, index in blocks_of(own_ref, far_ref, [(1, r1_ref), (2, r2_ref), (3, r3_ref)]):
        target = (slab ^ offset) * depth + 1
        for z in range(depth):
            for c in range(4):
                p_ref[target + z, c, pl.ds(0, part), :] = block_rows(
                    ref, index, (4 * z + c) * part, part
                )

    def edges(z, carry):
        for t in range(2):
            first, second = halo_tiles(even_ref, odd_ref, 2 * z + t, is_even, low_half)
            p_ref[z + 1, 2 * t, pl.ds(part, 8), :] = first
            p_ref[z + 1, 2 * t + 1, pl.ds(part, 8), :] = second
        return carry

    lax.fori_loop(0, planes, edges, 0, unroll=UNROLL)
    first, second = halo_tiles(even_ref, odd_ref, 2 * planes, is_even, low_half)
    f_ref[0, pl.ds(0, part), :] = faces_ref[pl.ds(0, part), :]
    f_ref[0, pl.ds(part, 8), :] = first
    f_ref[1, pl.ds(0, part), :] = faces_ref[pl.ds(part, part), :]
    f_ref[1, pl.ds(part, 8), :] = second
    lane = lane_iota((part + 8, LANES))

    def hessian(z, carry):
        below = parts(p_ref, z)
        here = parts(p_ref, z + 1)
        above = parts(p_ref, z + 2)
        rise = [a - b for a, b in zip(above, below)]
        y_sum, y_rise, yz_rise = [], [], []
        for c in range(4):
            odd = c >> 1
            same, other = here[c ^ 2], y_other(here[c ^ 2], odd)
            y_sum.append(same + other)
            y_rise.append(other - same if odd else same - other)
            same, other = rise[c ^ 2], y_other(rise[c ^ 2], odd)
            yz_rise.append(other - same if odd else same - other)
        for c in range(4):
            odd = c & 1
            same, other = here[c ^ 1], x_other(here[c ^ 1], odd)
            twice = 2.0 * here[c]
            pxx = same + other - twice
            pyy = y_sum[c] - twice
            pzz = below[c] + above[c] - twice
            same, other = rise[c ^ 1], x_other(rise[c ^ 1], odd)
            pxz = other - same if odd else same - other
            same, other = y_rise[c ^ 1], x_other(y_rise[c ^ 1], odd)
            pxy = other - same if odd else same - other
            pyz = yz_rise[c]
            cross = pxy * pxy + pxz * pxz + pyz * pyz
            source = pxx * pyy + (pxx + pyy) * pzz - 0.0625 * cross
            s_ref[z, c] = source[:part]
            face = f_ref[c >> 1]
            if odd:
                face = jnp.where(
                    lane == LANES - 1, pltpu.roll(face, LANES - 1 - planes - z, 1), 0.0
                )
            else:
                face = jnp.where(lane == 0, pltpu.roll(face, (LANES - z) & (LANES - 1), 1), 0.0)
            put(q_ref, z + 2, c, W * (face - source), mask)
        return carry

    lax.fori_loop(0, planes, hessian, 0, unroll=2)
    join_planes(
        lambda z, c: s_ref[slab * depth + z, c], source_ref, left_ref, right_ref, depth, width
    )

    def second_sweep(z, carry):
        here = parts(q_ref, z + 2)
        for c in range(4):
            new = swept(q_ref[z + 1, c], here, q_ref[z + 3, c], here[c], c)
            put(u_ref, z + 2, c, new, mask)
        return carry

    lax.fori_loop(0, planes, second_sweep, 0, unroll=UNROLL)
    restrict_window(u_ref, q_ref, coarse_ref, planes, part)


def restrict_window(u_ref, q_ref, coarse_ref, planes, part):
    def restrict(z, carry):
        total = None
        for at in (2 * z + 2, 2 * z + 3):
            here = parts(u_ref, at)
            for c in range(4):
                new = swept(u_ref[at - 1, c], here, u_ref[at + 1, c], q_ref[at, c], c)
                change = (new - here[c])[:part]
                total = change if total is None else total + change
        coarse_ref[pl.ds(pl.multiple_of(z * part, part), part), :] = 0.5 * total
        return carry

    lax.fori_loop(0, planes // 2, restrict, 0, unroll=2)


def coarse_window(v_ref, z, pencil, part):
    start = pl.multiple_of(pencil * part, part)
    own = v_ref[z, pl.ds(start + HALO, part), :]
    above = v_ref[z, pl.ds(start + HALO + part, 8), :]
    below = v_ref[z, pl.ds(start, 8), :]
    tile = jnp.where(row_iota((8, LANES)) < 4, above, below)
    return jnp.concatenate([own, tile], axis=0)


def middle_kernel(
    scalar_ref, gathered_ref, q_ref, u_ref, qwin_ref, uwin_ref, coarse_ref,
    q1_ref, a1_ref, b1_ref, tmp_ref, a_ref, b_ref, *, depth, width, pencils, shape
):
    slab = scalar_ref[0]
    pencil = scalar_ref[1]
    planes = a_ref.shape[0] - 4
    part = width // 2
    mask = halo_mask(pencil, pencils)
    solve_level_one(gathered_ref, q1_ref, a1_ref, b1_ref, tmp_ref, shape)
    blank = jnp.zeros(a_ref.shape[1:], jnp.float32)
    for ref in (a_ref, b_ref):
        for z in (0, 1, planes + 2, planes + 3):
            ref[z] = blank

    def correct(z, carry):
        wide = coarse_window(a1_ref, z + 1, pencil, part)
        for at in (2 * z + 2, 2 * z + 3):
            for c in range(4):
                a_ref[at, c] = u_ref[at, c] + wide
        return carry

    lax.fori_loop(0, planes // 2, correct, 0, unroll=2)

    def sweep(src, dst):
        def body(z, carry):
            here = parts(src, z + 2)
            for c in range(4):
                new = swept(src[z + 1, c], here, src[z + 3, c], q_ref[z + 2, c], c)
                put(dst, z + 2, c, new, mask)
            return carry

        lax.fori_loop(0, planes, body, 0, unroll=UNROLL)

    sweep(a_ref, b_ref)
    sweep(b_ref, a_ref)
    sweep(a_ref, b_ref)
    sweep(b_ref, a_ref)
    restrict_window(a_ref, q_ref, coarse_ref, planes, part)
    for z in range(depth + 4):
        qwin_ref[z] = q_ref[slab * depth + z]
        uwin_ref[z] = a_ref[slab * depth + z]


def last_kernel(
    scalar_ref, gathered_ref, qwin_ref, uwin_ref, out_ref,
    q1_ref, a1_ref, b1_ref, tmp_ref, a_ref, b_ref, left_ref, right_ref,
    *, depth, width, pencils, shape
):
    slab = scalar_ref[0]
    pencil = scalar_ref[1]
    planes = shape[0] * 2
    part = width // 2
    mask = halo_mask(pencil, pencils)
    solve_level_one(gathered_ref, q1_ref, a1_ref, b1_ref, tmp_ref, shape)
    for z in range(depth // 2 + 2):
        wide = coarse_window(a1_ref, slab * (depth // 2) + z, pencil, part)
        for at in (2 * z, 2 * z + 1):
            for c in range(4):
                a_ref[at, c] = uwin_ref[at, c] + wide
    for z in range(1, depth + 3):
        at = slab * depth - 2 + z
        live = jnp.where((at >= 0) & (at < planes), 1.0, 0.0)
        here = parts(a_ref, z)
        for c in range(4):
            new = swept(a_ref[z - 1, c], here, a_ref[z + 1, c], qwin_ref[z, c], c)
            put(b_ref, z, c, live * new, mask)
    done = {}
    for z in range(2, depth + 2):
        here = parts(b_ref, z)
        for c in range(4):
            new = swept(b_ref[z - 1, c], here, b_ref[z + 1, c], qwin_ref[z, c], c)
            done[z - 2, c] = new[:part]
    join_planes(lambda z, c: done[z, c], out_ref, left_ref, right_ref, depth, width)


def vmem():
    return pl.BlockSpec(memory_space=pltpu.VMEM)


def smem():
    return pl.BlockSpec(memory_space=pltpu.SMEM)


def arr(*shape):
    return jax.ShapeDtypeStruct(shape, jnp.float32)


def buf(*shape):
    return pltpu.VMEM(shape, jnp.float32)


def call(kernel, name, scalars, args, outs, scratch=()):
    return pl.pallas_call(
        kernel,
        out_shape=outs,
        in_specs=[smem()] * len(scalars) + [vmem()] * len(args),
        out_specs=jax.tree.map(lambda _: vmem(), outs),
        scratch_shapes=list(scratch),
        compiler_params=pltpu.CompilerParams(vmem_limit_bytes=48 << 20),
        name=name,
    )(*scalars, *args)


def windowed(potential, parent_store, face_owner, face_offset):
    depth, width, columns = potential.shape
    slabs = lax.axis_size("slab")
    pencils = lax.axis_size("pencil")
    planes, height = slabs * depth, pencils * width
    part = width // 2
    rows = part + 8
    where = jnp.stack([lax.axis_index("slab"), lax.axis_index("pencil")]).astype(jnp.int32)
    scalars = jnp.concatenate([where, face_owner, face_offset])
    own = call(
        pack_kernel,
        "pack",
        [],
        [potential, parent_store],
        arr(depth * width * 2 + 8, LANES),
        [buf(depth * width, LANES), buf(depth * width, LANES)],
    )

    def swap(x, bits):
        return lax.ppermute(x, "slab", [(i, i ^ bits) for i in range(slabs)])

    far = swap(own, 4)
    both = jnp.stack([own, far])
    others = [swap(both, bits) for bits in (1, 2, 3)]
    message = arr(2 * planes + 1, 8, LANES)
    even, odd, faces = call(
        partial(edges_kernel, depth=depth, width=width, slabs=slabs),
        "edges",
        [scalars],
        [own, far, *others],
        (message, message, arr(width, LANES)),
        [buf(slabs, 8, LANES), buf(LANES, LANES)],
    )
    low_pairs = [(i, i + 1) for i in range(0, pencils - 1, 2)]
    high_pairs = [(i, i + 1) for i in range(1, pencils - 1, 2)]
    even = lax.ppermute(even, "pencil", low_pairs + [(j, i) for i, j in low_pairs])
    odd = lax.ppermute(odd, "pencil", high_pairs + [(j, i) for i, j in high_pairs])
    shape = (planes // 2, height // 2, columns // 2)
    coarse_part = arr(planes // 2 * part, LANES)
    field = (planes + 4, 4, rows, LANES)
    source, q, u, coarse = call(
        partial(first_kernel, depth=depth, width=width, pencils=pencils),
        "first",
        [scalars],
        [own, far, *others, even, odd, faces],
        (arr(depth, width, columns), arr(*field), arr(*field), coarse_part),
        [
            buf(planes + 2, 4, rows, LANES),
            buf(2, rows, LANES),
            buf(planes, 4, part, LANES),
            buf(depth * width, LANES),
            buf(depth * width, LANES),
        ],
    )
    level = (shape[0] + 2, shape[1] + 2 * HALO, LANES)
    level_scratch = [buf(*level), buf(*level), buf(*level), buf(shape[0] * shape[1], LANES)]

    def gather(x):
        whole = lax.all_gather(x, "pencil", axis=0, tiled=False)
        return whole.reshape(pencils, shape[0], part, LANES)

    sizes = dict(depth=depth, width=width, pencils=pencils, shape=shape)
    slim = (depth + 4, 4, rows, LANES)
    qwin, uwin, coarse = call(
        partial(middle_kernel, **sizes),
        "middle",
        [scalars],
        [gather(coarse), q, u],
        (arr(*slim), arr(*slim), coarse_part),
        level_scratch + [buf(*field), buf(*field)],
    )
    solved = call(
        partial(last_kernel, **sizes),
        "last",
        [scalars],
        [gather(coarse), qwin, uwin],
        arr(depth, width, columns),
        level_scratch
        + [buf(*slim), buf(*slim), buf(depth * width, LANES), buf(depth * width, LANES)],
    )
    return solved, source


def fits_window(potential, parent_store):
    depth, width, columns = potential.shape
    slabs = lax.axis_size("slab")
    pencils = lax.axis_size("pencil")
    planes = slabs * depth
    return (
        slabs == 8
        and pencils % 2 == 0
        and depth == 4
        and columns == 2 * LANES
        and width == 32
        and parent_store.shape[0] * width == LANES
        and 2 * planes <= LANES
        and pencils <= 8
    )


def padded(cells, sides, width):
    for axis, dim in sides:
        count = lax.axis_size(axis)
        ends = count - 1
        head = lax.slice_in_dim(cells, 0, width, axis=dim)
        tail = lax.slice_in_dim(cells, cells.shape[dim] - width, cells.shape[dim], axis=dim)
        cells = jnp.concatenate(
            [
                lax.ppermute(tail, axis, [(i, (i + 1) % count) for i in range(ends)]),
                cells,
                lax.ppermute(head, axis, [((i + 1) % count, i) for i in range(ends)]),
            ],
            axis=dim,
        )
    return cells


def hessian_source(p):
    c = p[1:-1, 1:-1, 1:-1]
    pxx = p[1:-1, 1:-1, 2:] + p[1:-1, 1:-1, :-2] - 2.0 * c
    pyy = p[1:-1, 2:, 1:-1] + p[1:-1, :-2, 1:-1] - 2.0 * c
    pzz = p[2:, 1:-1, 1:-1] + p[:-2, 1:-1, 1:-1] - 2.0 * c
    pxy = 0.25 * (p[1:-1, 2:, 2:] - p[1:-1, :-2, 2:] - p[1:-1, 2:, :-2] + p[1:-1, :-2, :-2])
    pxz = 0.25 * (p[2:, 1:-1, 2:] - p[:-2, 1:-1, 2:] - p[2:, 1:-1, :-2] + p[:-2, 1:-1, :-2])
    pyz = 0.25 * (p[2:, 2:, 1:-1] - p[:-2, 2:, 1:-1] - p[2:, :-2, 1:-1] + p[:-2, :-2, 1:-1])
    return pxx * pyy + pxx * pzz + pyy * pzz - pxy * pxy - pxz * pxz - pyz * pyz


def apply_padded(p, level):
    c = p[1:-1, 1:-1, 1:-1]
    near = p[2:, 1:-1, 1:-1] + p[:-2, 1:-1, 1:-1]
    near = near + p[1:-1, 2:, 1:-1] + p[1:-1, :-2, 1:-1]
    near = near + p[1:-1, 1:-1, 2:] + p[1:-1, 1:-1, :-2]
    return (6.0 * c - near) * 0.25**level


def step_weight(level):
    return OMEGA / 6.0 * 4.0**level


def sweep_whole(u, rhs, level):
    return u + step_weight(level) * (rhs - apply_padded(jnp.pad(u, 1), level))


def restrict(r):
    a, b, c = r.shape
    return r.reshape(a // 2, 2, b // 2, 2, c // 2, 2).mean(axis=(1, 3, 5))


def prolong(e):
    a, b, c = e.shape
    return jnp.broadcast_to(e[:, None, :, None, :, None], (a, 2, b, 2, c, 2)).reshape(
        2 * a, 2 * b, 2 * c
    )


def vcycle(u, rhs, level):
    if is_coarsest(rhs.shape):
        for sweep_count in range(8):
            u = sweep_whole(u, rhs, level)
        return u
    u = sweep_whole(u, rhs, level)
    u = sweep_whole(u, rhs, level)
    resid = rhs - apply_padded(jnp.pad(u, 1), level)
    coarse = restrict(resid)
    correction = vcycle(jnp.zeros_like(coarse), coarse, level + 1)
    u = u + prolong(correction)
    u = sweep_whole(u, rhs, level)
    u = sweep_whole(u, rhs, level)
    return u


def widen_x(p):
    return jnp.pad(p, ((0, 0), (0, 0), (1, 1)))


def rim_one(u):
    return widen_x(padded(u, (("slab", 0), ("pencil", 1)), 1))


def coarse_solve(rhs, level):
    width = rhs.shape[1]
    columns = rhs.shape[2]
    whole = lax.all_gather(rhs, ("slab", "pencil"), axis=0, tiled=True)
    whole = whole.reshape(lax.axis_size("slab"), lax.axis_size("pencil") * width, columns)
    solved = vcycle(jnp.zeros_like(whole), whole, level)
    start_y = lax.axis_index("pencil") * width
    return lax.dynamic_slice(
        solved, (lax.axis_index("slab"), start_y, jnp.int32(0)), (1, width, columns)
    )


def split_vcycle(u, rhs, level, from_zero):
    if rhs.shape[0] == 1:
        return coarse_solve(rhs, level)
    weight = step_weight(level)
    if from_zero:
        u = weight * rhs
    else:
        u = u + weight * (rhs - apply_padded(rim_one(u), level))
    u = u + weight * (rhs - apply_padded(rim_one(u), level))
    resid = rhs - apply_padded(rim_one(u), level)
    correction = split_vcycle(None, restrict(resid), level + 1, True)
    u = u + prolong(correction)
    u = u + weight * (rhs - apply_padded(rim_one(u), level))
    u = u + weight * (rhs - apply_padded(rim_one(u), level))
    return u


def plain(potential, parent_store, face_owner, face_offset):
    depth, width, columns = potential.shape
    grown = widen_x(padded(potential, (("slab", 0), ("pencil", 1)), 1))
    source = hessian_source(grown)
    slab_index = lax.axis_index("slab")
    wanted = face_owner[slab_index] * parent_store.shape[0] + face_offset[slab_index]
    piece = lax.all_gather(parent_store, "slab", axis=0, tiled=True)
    labels = jnp.arange(piece.shape[0], dtype=jnp.int32)
    match = labels == wanted
    faces = jnp.sum(jnp.where(match[:, None, None, None], piece, 0.0), axis=0)
    rhs = -source
    rhs = rhs.at[:, :, 0].add(faces[0])
    rhs = rhs.at[:, :, columns - 1].add(faces[1])
    solved = jnp.zeros_like(rhs)
    for cycle in range(CYCLES):
        solved = split_vcycle(solved, rhs, 0, cycle == 0)
    return (solved, source)


def on_device(potential, parent_store, face_owner, face_offset):
    if fits_window(potential, parent_store):
        return windowed(potential, parent_store, face_owner, face_offset)
    return plain(potential, parent_store, face_owner, face_offset)


def solution(mesh):
    in_specs = (P("slab", "pencil", None), P("slab", None, None, "pencil"), P(), P())
    out_specs = (P("slab", "pencil", None), P("slab", "pencil", None))
    return jax.shard_map(
        on_device, mesh=mesh, in_specs=in_specs, out_specs=out_specs, check_vma=False
    )
```

```python
from functools import partial

import jax
import jax.numpy as jnp
import numpy as np
from jax import lax
from jax.experimental import pallas as pl
from jax.experimental.pallas import tpu as pltpu
from jax.sharding import PartitionSpec as P

CYCLES = 2
OMEGA = 0.8
W = float(np.float32(OMEGA / 6.0))
KEEP = 1.0 - 6.0 * W
HALO = 8
LANES = 128
UNROLL = 4


def is_coarsest(shape):
    return min(shape) <= 4 or any((d % 2 for d in shape))


def lane_iota(shape):
    return lax.broadcasted_iota(jnp.int32, shape, len(shape) - 1)


def row_iota(shape):
    return lax.broadcasted_iota(jnp.int32, shape, len(shape) - 2)


def x_other(values, odd):
    lane = lane_iota(values.shape)
    if odd:
        return jnp.where(lane == LANES - 1, 0.0, pltpu.roll(values, LANES - 1, 1))
    return jnp.where(lane == 0, 0.0, pltpu.roll(values, 1, 1))


def y_other(values, odd):
    return pltpu.roll(values, values.shape[0] - 1 if odd else 1, 0)


def swept(below, here, above, q, c):
    across, along = here[c ^ 1], here[c ^ 2]
    near = (below + above) + (across + x_other(across, c & 1))
    near = near + (along + y_other(along, c >> 1))
    return KEEP * here[c] + W * near + q


def parts(ref, z):
    return [ref[z, c] for c in range(4)]


def halo_mask(pencil, pencils):
    row = row_iota((8, LANES))
    above = jnp.where(pencil < pencils - 1, 1.0, 0.0)
    below = jnp.where(pencil > 0, 1.0, 0.0)
    return jnp.where(row < 4, above, below)


def put(ref, z, c, values, mask):
    own = values.shape[0] - 8
    ref[z, c, pl.ds(0, own), :] = values[:own]
    ref[z, c, pl.ds(own, 8), :] = values[own:] * mask


def index_pair(rows, columns):
    return (
        lax.broadcasted_iota(jnp.int32, (rows, columns), 0),
        lax.broadcasted_iota(jnp.int32, (rows, columns), 1),
    )


def chosen(where, value):
    return jnp.where(where, value, 0.0).astype(jnp.bfloat16)


def splitting_matrix():
    i, j = index_pair(2 * LANES, 2 * LANES)
    return chosen(i == 2 * (j & (LANES - 1)) + (j >= LANES).astype(jnp.int32), 1.0)


def merging_matrix():
    i, j = index_pair(2 * LANES, 2 * LANES)
    return chosen(j == 2 * (i & (LANES - 1)) + (i >= LANES).astype(jnp.int32), 1.0)


def mm(a, b):
    high = a.astype(jnp.bfloat16)
    rest = a - high.astype(jnp.float32)
    middle = rest.astype(jnp.bfloat16)
    low = (rest - middle.astype(jnp.float32)).astype(jnp.bfloat16)

    def dot(x):
        return jnp.dot(x, b, preferred_element_type=jnp.float32)

    return dot(high) + (dot(middle) + dot(low))


def pair_sum(values, distance, axis):
    size = values.shape[axis]
    at = lax.broadcasted_iota(jnp.int32, values.shape, axis)
    ahead = pltpu.roll(values, size - distance, axis)
    behind = pltpu.roll(values, distance, axis)
    return values + jnp.where((at & distance) == 0, ahead, behind)


def x_sides(values, distance):
    lane = lane_iota(values.shape)
    left = jnp.where(lane < distance, 0.0, pltpu.roll(values, distance, 1))
    right = jnp.where(lane >= LANES - distance, 0.0, pltpu.roll(values, LANES - distance, 1))
    return left + right


def flat_sweep(u, q, rows, yd, xd):
    total = u.shape[0]
    zero = jnp.zeros((rows, LANES), jnp.float32)
    below = jnp.concatenate([zero, u[: total - rows]], axis=0)
    above = jnp.concatenate([u[rows:], zero], axis=0)
    y = row_iota(u.shape) & (rows - 1)
    down = jnp.where(y < yd, 0.0, pltpu.roll(u, yd, 0))
    up = jnp.where(y >= rows - yd, 0.0, pltpu.roll(u, total - yd, 0))
    return KEEP * u + W * ((below + above) + (down + up) + x_sides(u, xd)) + q


def flat_vcycle(q, shape, rows, yd, xd):
    if is_coarsest(shape):
        u = q
        for _ in range(7):
            u = flat_sweep(u, q, rows, yd, xd)
        return u
    zs, ys, xs = shape
    u = flat_sweep(q, q, rows, yd, xd)
    change = flat_sweep(u, q, rows, yd, xd) - u
    pairs = [
        change[2 * z * rows : (2 * z + 1) * rows] + change[(2 * z + 1) * rows : (2 * z + 2) * rows]
        for z in range(zs // 2)
    ]
    coarse = 0.5 * pair_sum(pair_sum(jnp.concatenate(pairs, axis=0), yd, 0), xd, 1)
    e = flat_vcycle(coarse, (zs // 2, ys // 2, xs // 2), rows, 2 * yd, 2 * xd)
    planes = []
    for z in range(zs // 2):
        planes += [e[z * rows : (z + 1) * rows]] * 2
    u = u + jnp.concatenate(planes, axis=0)
    u = flat_sweep(u, q, rows, yd, xd)
    return flat_sweep(u, q, rows, yd, xd)


def solve_level_one(gathered_ref, v_ref, q_ref, a_ref, b_ref, tmp_ref, shape):
    zs, ys, xs = shape
    pencils = gathered_ref.shape[0]
    rows = ys // 2
    piece = rows // pencils
    row = row_iota((rows, LANES))
    blank = jnp.zeros((rows, LANES), jnp.float32)
    for ref in (q_ref, a_ref, b_ref):
        for z in (0, zs + 1):
            for c in range(2):
                ref[z, c] = blank
    edge = jnp.zeros((HALO, LANES), jnp.float32)
    for z in range(zs + 2):
        v_ref[z, pl.ds(0, HALO), :] = edge
        v_ref[z, pl.ds(HALO + ys, HALO), :] = edge
    for z in (0, zs + 1):
        for c in range(2):
            v_ref[z, pl.ds(HALO + c * rows, rows), :] = blank
    for z in range(zs):
        for c in range(2):
            for p in range(pencils):
                spot = pl.ds(2 * piece * z + c, piece, stride=2)
                q_ref[z + 1, c, pl.ds(p * piece, piece), :] = gathered_ref[p, spot, :]

    def sweep_plane(src, z):
        here = [src[z, 0], src[z, 1]]
        new = []
        for c in range(2):
            other = here[1 - c]
            if c:
                beyond = jnp.where(row == rows - 1, 0.0, pltpu.roll(other, rows - 1, 0))
            else:
                beyond = jnp.where(row == 0, 0.0, pltpu.roll(other, 1, 0))
            near = (src[z - 1, c] + src[z + 1, c]) + (other + beyond) + x_sides(here[c], 1)
            new.append(KEEP * here[c] + W * near + q_ref[z, c])
        return here, new

    def sweep(src, dst):
        def body(z, carry):
            _, new = sweep_plane(src, z)
            for c in range(2):
                dst[z, c] = new[c]
            return carry

        lax.fori_loop(1, zs + 1, body, 0, unroll=UNROLL)

    sweep(q_ref, a_ref)

    def restrict(z, carry):
        total = None
        for at in (2 * z + 1, 2 * z + 2):
            here, new = sweep_plane(a_ref, at)
            change = (new[0] - here[0]) + (new[1] - here[1])
            total = change if total is None else total + change
        tmp_ref[pl.ds(pl.multiple_of(z * rows, rows), rows), :] = 0.5 * pair_sum(total, 1, 1)
        return carry

    lax.fori_loop(0, zs // 2, restrict, 0, unroll=2)
    tmp_ref[...] = flat_vcycle(tmp_ref[...], (zs // 2, ys // 2, xs // 2), rows, 1, 2)

    def correct(z, carry):
        e = tmp_ref[pl.ds(pl.multiple_of(z * rows, rows), rows), :]
        for at in (2 * z + 1, 2 * z + 2):
            for c in range(2):
                a_ref[at, c] = a_ref[at, c] + e
        return carry

    lax.fori_loop(0, zs // 2, correct, 0, unroll=2)
    sweep(a_ref, b_ref)

    def last_sweep(z, carry):
        _, new = sweep_plane(b_ref, z)
        for c in range(2):
            v_ref[z, pl.ds(HALO + c, rows, stride=2), :] = new[c]
        return carry

    lax.fori_loop(1, zs + 1, last_sweep, 0, unroll=UNROLL)


def pack_kernel(
    potential_hbm, store_hbm, out_ref, even_ref, odd_ref, potential_ref, store_ref, sems
):
    copies = [
        pltpu.make_async_copy(potential_hbm, potential_ref, sems.at[0]),
        pltpu.make_async_copy(store_hbm, store_ref, sems.at[1]),
    ]
    for copy in copies:
        copy.start()
    for copy in copies:
        copy.wait()
    depth, width, columns = potential_ref.shape
    slots = store_ref.shape[0]
    part = width // 2
    split = mm(potential_ref[...].reshape(depth * width, columns), splitting_matrix())
    even_ref[...] = split[:, :LANES]
    odd_ref[...] = split[:, LANES:]
    for z in range(depth):
        for c in range(4):
            ref = odd_ref if c & 1 else even_ref
            spot = pl.ds((4 * z + c) * part, part)
            out_ref[spot, :] = ref[pl.ds(z * width + (c >> 1), part, stride=2), :]
    base = depth * width * 2
    for slot in range(slots):
        for side in range(2):
            spot = pl.ds(base + side * depth, depth)
            out_ref[spot, pl.ds(slot * width, width)] = store_ref[slot, side]


OFFSETS = (0, 4, 3, 1, 2, 7, 5, 6)
EARLY = 5


def block_rows(ref, start, count):
    return ref[pl.ds(start, count), :]


def ends(load, first, second, part, low_half):
    head = jnp.where(low_half, load(first, 8), pltpu.roll(load(second, 8), 4, 0))
    tail = jnp.where(
        low_half, pltpu.roll(load(first + part - 8, 8), 4, 0), load(second + part - 8, 8)
    )
    return head, tail


def store_ends(ref, pencil, out_refs, at, depth, part):
    even_ref, odd_ref = out_refs
    is_even = (pencil % 2) == 0
    low_half = row_iota((8, LANES)) < 4
    for z in range(depth):
        for t in range(2):
            head, tail = ends(
                partial(block_rows, ref),
                (4 * z + 2 * t) * part, (4 * z + 2 * t + 1) * part, part, low_half,
            )
            even_ref[at + 2 * z + t] = jnp.where(is_even, tail, head)
            odd_ref[at + 2 * z + t] = jnp.where(is_even, head, tail)


def early_edges_kernel(scalar_ref, *refs, depth, width):
    blocks, out_refs = refs[:EARLY], refs[EARLY:]
    for k, ref in enumerate(blocks):
        store_ends(ref, scalar_ref[1], out_refs, 2 * depth * k, depth, width // 2)


def late_edges_kernel(scalar_ref, *refs, depth, width):
    slabs = len(OFFSETS)
    even_ref, odd_ref, faces_ref, store_ref, rows_ref = refs[slabs:]
    slab = scalar_ref[0]
    pencil = scalar_ref[1]
    planes = slabs * depth
    part = width // 2
    is_even = (pencil % 2) == 0
    low_half = row_iota((8, LANES)) < 4
    base = depth * width * 2
    late = refs[EARLY:slabs]
    for k, ref in enumerate(late):
        store_ends(ref, pencil, (even_ref, odd_ref), 2 * depth * k, depth, part)
    for offset, ref in zip(OFFSETS, refs):
        store_ref[slab ^ offset] = block_rows(ref, base, 8)
    rest = LANES - 2 * planes
    rows_ref[pl.ds(2 * planes, rest), :] = jnp.zeros((rest, LANES), jnp.float32)
    for s in range(slabs):
        tile = store_ref[scalar_ref[2 + s]]
        slot = scalar_ref[2 + slabs + s]
        picked = pltpu.roll(tile, (LANES - slot * width) & (LANES - 1), 1)
        rows_ref[pl.ds(s * depth, depth), :] = picked[:depth]
        rows_ref[pl.ds(planes + s * depth, depth), :] = picked[depth:]
    rows_ref[...] = rows_ref[...].T
    faces_ref[pl.ds(0, part), :] = rows_ref[pl.ds(0, part, stride=2), :]
    faces_ref[pl.ds(part, part), :] = rows_ref[pl.ds(1, part, stride=2), :]
    head, tail = ends(partial(block_rows, faces_ref), 0, part, part, low_half)
    even_ref[2 * depth * len(late)] = jnp.where(is_even, tail, head)
    odd_ref[2 * depth * len(late)] = jnp.where(is_even, head, tail)


def halo_tiles(even_ref, odd_ref, index, is_even, low_half):
    first = even_ref[index]
    second = odd_ref[index]
    above = jnp.where(is_even, first, second)
    below = jnp.where(is_even, second, first)
    return (
        jnp.where(low_half, above, pltpu.roll(below, 4, 0)),
        jnp.where(low_half, pltpu.roll(above, 4, 0), below),
    )


def join_planes(load, out_ref, left_ref, right_ref, depth, width):
    part = width // 2
    for z in range(depth):
        for c in range(4):
            ref = right_ref if c & 1 else left_ref
            ref[pl.ds(z * width + (c >> 1), part, stride=2), :] = load(z, c)
    rows = depth * width
    both = jnp.concatenate([left_ref[pl.ds(0, rows), :], right_ref[pl.ds(0, rows), :]], axis=1)
    out_ref[...] = mm(both, merging_matrix()).reshape(depth, width, 2 * LANES)


def hessian_parts(below, here, above):
    rise = [a - b for a, b in zip(above, below)]
    y_sum, y_rise, yz_rise = [], [], []
    for c in range(4):
        odd = c >> 1
        same, other = here[c ^ 2], y_other(here[c ^ 2], odd)
        y_sum.append(same + other)
        y_rise.append(other - same if odd else same - other)
        same, other = rise[c ^ 2], y_other(rise[c ^ 2], odd)
        yz_rise.append(other - same if odd else same - other)
    out = []
    for c in range(4):
        odd = c & 1
        same, other = here[c ^ 1], x_other(here[c ^ 1], odd)
        twice = 2.0 * here[c]
        pxx = same + other - twice
        pyy = y_sum[c] - twice
        pzz = below[c] + above[c] - twice
        same, other = rise[c ^ 1], x_other(rise[c ^ 1], odd)
        pxz = other - same if odd else same - other
        same, other = y_rise[c ^ 1], x_other(y_rise[c ^ 1], odd)
        pxy = other - same if odd else same - other
        cross = pxy * pxy + pxz * pxz + yz_rise[c] * yz_rise[c]
        out.append(pxx * pyy + (pxx + pyy) * pzz - 0.0625 * cross)
    return out


def face_part(face, c, z, planes):
    lane = lane_iota(face.shape)
    if c & 1:
        turned = pltpu.roll(face, LANES - 1 - planes - z, 1)
        return jnp.where(lane == LANES - 1, turned, 0.0)
    turned = pltpu.roll(face, (LANES - z) & (LANES - 1), 1)
    return jnp.where(lane == 0, turned, 0.0)


def fill_block(p_ref, at, ref, edge_refs, tile, pencil, depth, part):
    is_even = (pencil % 2) == 0
    low_half = row_iota((8, LANES)) < 4
    for z in range(depth):
        for c in range(4):
            p_ref[at + z, c, pl.ds(0, part), :] = block_rows(ref, (4 * z + c) * part, part)
        for t in range(2):
            first, second = halo_tiles(*edge_refs, tile + 2 * z + t, is_even, low_half)
            p_ref[at + z, 2 * t, pl.ds(part, 8), :] = first
            p_ref[at + z, 2 * t + 1, pl.ds(part, 8), :] = second


def near_half_kernel(scalar_ref, *refs, depth, width, pencils):
    near = [k for k in range(EARLY) if OFFSETS[k] < 4]
    blocks = refs[: len(near)]
    even_ref, odd_ref, faces_ref, p_ref, s_ref, q_ref = refs[len(near) :]
    slab = scalar_ref[0]
    pencil = scalar_ref[1]
    part = width // 2
    half = 4 * depth
    first_plane = (slab // 4) * half
    mask = halo_mask(pencil, pencils)
    blank = jnp.zeros(p_ref.shape[1:], jnp.float32)
    p_ref[0] = blank
    p_ref[half + 1] = blank
    for k, ref in zip(near, blocks):
        at = ((slab ^ OFFSETS[k]) % 4) * depth + 1
        fill_block(p_ref, at, ref, (even_ref, odd_ref), 2 * depth * k, pencil, depth, part)

    def body(j, carry):
        source = hessian_parts(parts(p_ref, j), parts(p_ref, j + 1), parts(p_ref, j + 2))
        for c in range(4):
            s_ref[j, c] = source[c][:part]
            face = faces_ref[pl.ds((c >> 1) * part, part), :]
            face = face_part(face, c, first_plane + j, 2 * half)
            q_ref[j, c, pl.ds(0, part), :] = W * (face - source[c][:part])
            q_ref[j, c, pl.ds(part, 8), :] = (-W * mask) * source[c][part:]
        return carry

    lax.fori_loop(0, half, body, 0, unroll=2)


def far_half_kernel(scalar_ref, *refs, depth, width, pencils):
    far = [k for k in range(len(OFFSETS)) if OFFSETS[k] >= 4]
    blocks = refs[: len(far)]
    early_refs = refs[len(far) : len(far) + 2]
    late_refs = refs[len(far) + 2 : len(far) + 4]
    faces_ref, pn_ref, sn_ref, qn_ref = refs[len(far) + 4 : len(far) + 8]
    source_hbm, q_ref, u_ref, coarse_ref = refs[len(far) + 8 : len(far) + 12]
    p_ref, f_ref, s_ref, left_ref, right_ref, source_ref, sem = refs[len(far) + 12 :]
    slab = scalar_ref[0]
    pencil = scalar_ref[1]
    part = width // 2
    half = 4 * depth
    planes = 2 * half
    lower = slab < 4
    near_first = jnp.where(lower, 0, half)
    far_first = half - near_first
    is_even = (pencil % 2) == 0
    low_half = row_iota((8, LANES)) < 4
    mask = halo_mask(pencil, pencils)
    blank = jnp.zeros(p_ref.shape[1:], jnp.float32)
    for ref in (q_ref, u_ref):
        for z in (0, 1, planes + 2, planes + 3):
            ref[z] = blank
    p_ref[jnp.where(lower, half + 1, 0)] = blank
    p_ref[jnp.where(lower, 0, half + 1)] = pn_ref[jnp.where(lower, half, 1)]
    for k, ref in zip(far, blocks):
        at = ((slab ^ OFFSETS[k]) % 4) * depth + 1
        early = k < EARLY
        tile = 2 * depth * (k if early else k - EARLY)
        edge_refs = early_refs if early else late_refs
        fill_block(p_ref, at, ref, edge_refs, tile, pencil, depth, part)
    face_tile = 2 * depth * (len(OFFSETS) - EARLY)
    first, second = halo_tiles(*late_refs, face_tile, is_even, low_half)
    f_ref[0, pl.ds(0, part), :] = faces_ref[pl.ds(0, part), :]
    f_ref[0, pl.ds(part, 8), :] = first
    f_ref[1, pl.ds(0, part), :] = faces_ref[pl.ds(part, part), :]
    f_ref[1, pl.ds(part, 8), :] = second

    def finish(source, z):
        for c in range(4):
            face = face_part(f_ref[c >> 1], c, z, planes)
            put(q_ref, z + 2, c, W * (face - source[c]), mask)

    def copy(j, carry):
        z = near_first + j
        for c in range(4):
            face = face_part(f_ref[c >> 1, pl.ds(part, 8), :], c, z, planes)
            q_ref[z + 2, c, pl.ds(0, part), :] = qn_ref[j, c, pl.ds(0, part), :]
            q_ref[z + 2, c, pl.ds(part, 8), :] = (
                qn_ref[j, c, pl.ds(part, 8), :] + (W * mask) * face
            )
        return carry

    lax.fori_loop(0, half, copy, 0, unroll=UNROLL)

    def body(j, carry):
        source = hessian_parts(parts(p_ref, j), parts(p_ref, j + 1), parts(p_ref, j + 2))
        finish(source, far_first + j)
        return carry

    lax.fori_loop(0, half, body, 0, unroll=2)
    seam = jnp.where(lower, half, 1)
    here = parts(pn_ref, seam)
    inner = parts(pn_ref, jnp.where(lower, half - 1, 2))
    outer = parts(p_ref, jnp.where(lower, 1, half))
    below = [jnp.where(lower, a, b) for a, b in zip(inner, outer)]
    above = [jnp.where(lower, b, a) for a, b in zip(inner, outer)]
    source = hessian_parts(below, here, above)
    finish(source, near_first + seam - 1)
    own = (slab % 4) * depth
    for z in range(depth):
        is_seam = own + z == seam - 1
        for c in range(4):
            s_ref[z, c] = jnp.where(is_seam, source[c][:part], sn_ref[own + z, c])
    join_planes(lambda z, c: s_ref[z, c], source_ref, left_ref, right_ref, depth, width)
    copy_out = pltpu.make_async_copy(source_ref, source_hbm, sem)
    copy_out.start()

    def second_sweep(z, carry):
        here = parts(q_ref, z + 2)
        for c in range(4):
            new = swept(q_ref[z + 1, c], here, q_ref[z + 3, c], here[c], c)
            put(u_ref, z + 2, c, new, mask)
        return carry

    lax.fori_loop(0, planes, second_sweep, 0, unroll=UNROLL)
    restrict_window(u_ref, q_ref, coarse_ref, planes, part)
    copy_out.wait()


def restrict_window(u_ref, q_ref, coarse_ref, planes, part):
    def restrict(z, carry):
        total = None
        for at in (2 * z + 2, 2 * z + 3):
            here = parts(u_ref, at)
            for c in range(4):
                new = swept(u_ref[at - 1, c], here, u_ref[at + 1, c], q_ref[at, c], c)
                change = (new - here[c])[:part]
                total = change if total is None else total + change
        coarse_ref[pl.ds(pl.multiple_of(z * part, part), part), :] = 0.5 * total
        return carry

    lax.fori_loop(0, planes // 2, restrict, 0, unroll=2)


def coarse_window(v_ref, z, pencil, part):
    start = pl.multiple_of(pencil * part, part)
    own = v_ref[z, pl.ds(start + HALO, part), :]
    above = v_ref[z, pl.ds(start + HALO + part, 8), :]
    below = v_ref[z, pl.ds(start, 8), :]
    tile = jnp.where(row_iota((8, LANES)) < 4, above, below)
    return jnp.concatenate([own, tile], axis=0)


def middle_kernel(
    scalar_ref, gathered_ref, q_ref, u_ref, qwin_ref, uwin_ref, coarse_ref,
    v_ref, q1_ref, a1_ref, b1_ref, tmp_ref, a_ref, b_ref, *, depth, width, pencils, shape
):
    slab = scalar_ref[0]
    pencil = scalar_ref[1]
    planes = a_ref.shape[0] - 4
    part = width // 2
    mask = halo_mask(pencil, pencils)
    solve_level_one(gathered_ref, v_ref, q1_ref, a1_ref, b1_ref, tmp_ref, shape)
    blank = jnp.zeros(a_ref.shape[1:], jnp.float32)
    for ref in (a_ref, b_ref):
        for z in (0, 1, planes + 2, planes + 3):
            ref[z] = blank

    def correct(z, carry):
        wide = coarse_window(v_ref, z + 1, pencil, part)
        for at in (2 * z + 2, 2 * z + 3):
            for c in range(4):
                a_ref[at, c] = u_ref[at, c] + wide
        return carry

    lax.fori_loop(0, planes // 2, correct, 0, unroll=2)

    def sweep(src, dst):
        def body(z, carry):
            here = parts(src, z + 2)
            for c in range(4):
                new = swept(src[z + 1, c], here, src[z + 3, c], q_ref[z + 2, c], c)
                put(dst, z + 2, c, new, mask)
            return carry

        lax.fori_loop(0, planes, body, 0, unroll=UNROLL)

    sweep(a_ref, b_ref)
    sweep(b_ref, a_ref)
    sweep(a_ref, b_ref)
    sweep(b_ref, a_ref)
    restrict_window(a_ref, q_ref, coarse_ref, planes, part)
    for z in range(depth + 4):
        qwin_ref[z] = q_ref[slab * depth + z]
        uwin_ref[z] = a_ref[slab * depth + z]


def last_kernel(
    scalar_ref, gathered_ref, qwin_ref, uwin_ref, out_ref,
    v_ref, q1_ref, a1_ref, b1_ref, tmp_ref, a_ref, b_ref, left_ref, right_ref,
    *, depth, width, pencils, shape
):
    slab = scalar_ref[0]
    pencil = scalar_ref[1]
    planes = shape[0] * 2
    part = width // 2
    mask = halo_mask(pencil, pencils)
    solve_level_one(gathered_ref, v_ref, q1_ref, a1_ref, b1_ref, tmp_ref, shape)
    for z in range(depth // 2 + 2):
        wide = coarse_window(v_ref, slab * (depth // 2) + z, pencil, part)
        for at in (2 * z, 2 * z + 1):
            for c in range(4):
                a_ref[at, c] = uwin_ref[at, c] + wide
    for z in range(1, depth + 3):
        at = slab * depth - 2 + z
        live = jnp.where((at >= 0) & (at < planes), 1.0, 0.0)
        here = parts(a_ref, z)
        for c in range(4):
            new = swept(a_ref[z - 1, c], here, a_ref[z + 1, c], qwin_ref[z, c], c)
            put(b_ref, z, c, live * new, mask)
    done = {}
    for z in range(2, depth + 2):
        here = parts(b_ref, z)
        for c in range(4):
            new = swept(b_ref[z - 1, c], here, b_ref[z + 1, c], qwin_ref[z, c], c)
            done[z - 2, c] = new[:part]
    join_planes(lambda z, c: done[z, c], out_ref, left_ref, right_ref, depth, width)


def vmem():
    return pl.BlockSpec(memory_space=pltpu.VMEM)


def smem():
    return pl.BlockSpec(memory_space=pltpu.SMEM)


def arr(*shape):
    return jax.ShapeDtypeStruct(shape, jnp.float32)


def buf(*shape):
    return pltpu.VMEM(shape, jnp.float32)


def call(kernel, name, scalars, args, outs, scratch=(), space=pltpu.VMEM, out_space=None):
    out_specs = jax.tree.map(lambda _: vmem(), outs)
    if out_space is not None:
        out_specs = tuple(pl.BlockSpec(memory_space=one) for one in out_space)
    return pl.pallas_call(
        kernel,
        out_shape=outs,
        in_specs=[smem()] * len(scalars) + [pl.BlockSpec(memory_space=space)] * len(args),
        out_specs=out_specs,
        scratch_shapes=list(scratch),
        compiler_params=pltpu.CompilerParams(vmem_limit_bytes=16 << 20),
        name=name,
    )(*scalars, *args)


def windowed(potential, parent_store, face_owner, face_offset):
    depth, width, columns = potential.shape
    slabs = lax.axis_size("slab")
    pencils = lax.axis_size("pencil")
    planes, height = slabs * depth, pencils * width
    part = width // 2
    rows = part + 8
    where = jnp.stack([lax.axis_index("slab"), lax.axis_index("pencil")]).astype(jnp.int32)
    scalars = jnp.concatenate([where, face_owner, face_offset])
    own = call(
        pack_kernel,
        "pack",
        [],
        [pltpu.with_memory_space_constraint(x, pltpu.HBM) for x in (potential, parent_store)],
        arr(depth * width * 2 + 8, LANES),
        [
            buf(depth * width, LANES),
            buf(depth * width, LANES),
            buf(*potential.shape),
            buf(*parent_store.shape),
            pltpu.SemaphoreType.DMA((2,)),
        ],
        space=pltpu.HBM,
    )

    def swap(x, bits):
        return lax.ppermute(x, "slab", [(i, i ^ bits) for i in range(slabs)])

    near = [swap(own, bits) for bits in OFFSETS[1:5]]
    blocks = [own, *near] + [swap(near[0], bits) for bits in OFFSETS[2:5]]
    low_pairs = [(i, i + 1) for i in range(0, pencils - 1, 2)]
    high_pairs = [(i, i + 1) for i in range(1, pencils - 1, 2)]

    def beside(even, odd):
        return (
            lax.ppermute(even, "pencil", low_pairs + [(j, i) for i, j in low_pairs]),
            lax.ppermute(odd, "pencil", high_pairs + [(j, i) for i, j in high_pairs]),
        )

    message = arr(2 * depth * EARLY, 8, LANES)
    early = call(
        partial(early_edges_kernel, depth=depth, width=width),
        "early_edges",
        [scalars],
        blocks[:EARLY],
        (message, message),
    )
    early = beside(*early)
    message = arr(2 * depth * (slabs - EARLY) + 1, 8, LANES)
    even, odd, faces = call(
        partial(late_edges_kernel, depth=depth, width=width),
        "late_edges",
        [scalars],
        blocks,
        (message, message, arr(width, LANES)),
        [buf(slabs, 8, LANES), buf(LANES, LANES)],
    )
    late = beside(even, odd)
    shape = (planes // 2, height // 2, columns // 2)
    coarse_part = arr(planes // 2 * part, LANES)
    field = (planes + 4, 4, rows, LANES)
    half = planes // 2
    near = call(
        partial(near_half_kernel, depth=depth, width=width, pencils=pencils),
        "near_half",
        [scalars],
        [b for b, offset in zip(blocks, OFFSETS) if offset < 4] + [*early, faces],
        (arr(half + 2, 4, rows, LANES), arr(half, 4, part, LANES), arr(half, 4, rows, LANES)),
    )
    source, q, u, coarse = call(
        partial(far_half_kernel, depth=depth, width=width, pencils=pencils),
        "far_half",
        [scalars],
        [b for b, offset in zip(blocks, OFFSETS) if offset >= 4] + [*early, *late, faces, *near],
        (arr(depth, width, columns), arr(*field), arr(*field), coarse_part),
        [
            buf(half + 2, 4, rows, LANES),
            buf(2, rows, LANES),
            buf(depth, 4, part, LANES),
            buf(depth * width, LANES),
            buf(depth * width, LANES),
            buf(depth, width, columns),
            pltpu.SemaphoreType.DMA,
        ],
        out_space=[pl.ANY] + [pltpu.VMEM] * 3,
    )
    level = (shape[0] + 2, 2, shape[1] // 2, LANES)
    level_scratch = [
        buf(shape[0] + 2, shape[1] + 2 * HALO, LANES),
        buf(*level),
        buf(*level),
        buf(*level),
        buf(shape[0] * shape[1] // 4, LANES),
    ]

    def gather(x):
        return lax.all_gather(x, "pencil", axis=0, tiled=False)

    sizes = dict(depth=depth, width=width, pencils=pencils, shape=shape)
    slim = (depth + 4, 4, rows, LANES)
    qwin, uwin, coarse = call(
        partial(middle_kernel, **sizes),
        "middle",
        [scalars],
        [gather(coarse), q, u],
        (arr(*slim), arr(*slim), coarse_part),
        level_scratch + [buf(*field), buf(*field)],
    )
    solved = call(
        partial(last_kernel, **sizes),
        "last",
        [scalars],
        [gather(coarse), qwin, uwin],
        arr(depth, width, columns),
        level_scratch
        + [buf(*slim), buf(*slim), buf(depth * width, LANES), buf(depth * width, LANES)],
    )
    return solved, source


def fits_window(potential, parent_store):
    depth, width, columns = potential.shape
    slabs = lax.axis_size("slab")
    pencils = lax.axis_size("pencil")
    planes = slabs * depth
    return (
        slabs == 8
        and pencils % 2 == 0
        and depth == 4
        and columns == 2 * LANES
        and width == 32
        and parent_store.shape[0] * width == LANES
        and 2 * planes < LANES
        and pencils in (2, 4, 8)
    )


def padded(cells, sides, width):
    for axis, dim in sides:
        count = lax.axis_size(axis)
        ends = count - 1
        head = lax.slice_in_dim(cells, 0, width, axis=dim)
        tail = lax.slice_in_dim(cells, cells.shape[dim] - width, cells.shape[dim], axis=dim)
        cells = jnp.concatenate(
            [
                lax.ppermute(tail, axis, [(i, (i + 1) % count) for i in range(ends)]),
                cells,
                lax.ppermute(head, axis, [((i + 1) % count, i) for i in range(ends)]),
            ],
            axis=dim,
        )
    return cells


def hessian_source(p):
    c = p[1:-1, 1:-1, 1:-1]
    pxx = p[1:-1, 1:-1, 2:] + p[1:-1, 1:-1, :-2] - 2.0 * c
    pyy = p[1:-1, 2:, 1:-1] + p[1:-1, :-2, 1:-1] - 2.0 * c
    pzz = p[2:, 1:-1, 1:-1] + p[:-2, 1:-1, 1:-1] - 2.0 * c
    pxy = 0.25 * (p[1:-1, 2:, 2:] - p[1:-1, :-2, 2:] - p[1:-1, 2:, :-2] + p[1:-1, :-2, :-2])
    pxz = 0.25 * (p[2:, 1:-1, 2:] - p[:-2, 1:-1, 2:] - p[2:, 1:-1, :-2] + p[:-2, 1:-1, :-2])
    pyz = 0.25 * (p[2:, 2:, 1:-1] - p[:-2, 2:, 1:-1] - p[2:, :-2, 1:-1] + p[:-2, :-2, 1:-1])
    return pxx * pyy + pxx * pzz + pyy * pzz - pxy * pxy - pxz * pxz - pyz * pyz


def apply_padded(p, level):
    c = p[1:-1, 1:-1, 1:-1]
    near = p[2:, 1:-1, 1:-1] + p[:-2, 1:-1, 1:-1]
    near = near + p[1:-1, 2:, 1:-1] + p[1:-1, :-2, 1:-1]
    near = near + p[1:-1, 1:-1, 2:] + p[1:-1, 1:-1, :-2]
    return (6.0 * c - near) * 0.25**level


def step_weight(level):
    return OMEGA / 6.0 * 4.0**level


def sweep_whole(u, rhs, level):
    return u + step_weight(level) * (rhs - apply_padded(jnp.pad(u, 1), level))


def restrict(r):
    a, b, c = r.shape
    return r.reshape(a // 2, 2, b // 2, 2, c // 2, 2).mean(axis=(1, 3, 5))


def prolong(e):
    a, b, c = e.shape
    return jnp.broadcast_to(e[:, None, :, None, :, None], (a, 2, b, 2, c, 2)).reshape(
        2 * a, 2 * b, 2 * c
    )


def vcycle(u, rhs, level):
    if is_coarsest(rhs.shape):
        for sweep_count in range(8):
            u = sweep_whole(u, rhs, level)
        return u
    u = sweep_whole(u, rhs, level)
    u = sweep_whole(u, rhs, level)
    resid = rhs - apply_padded(jnp.pad(u, 1), level)
    coarse = restrict(resid)
    correction = vcycle(jnp.zeros_like(coarse), coarse, level + 1)
    u = u + prolong(correction)
    u = sweep_whole(u, rhs, level)
    u = sweep_whole(u, rhs, level)
    return u


def widen_x(p):
    return jnp.pad(p, ((0, 0), (0, 0), (1, 1)))


def rim_one(u):
    return widen_x(padded(u, (("slab", 0), ("pencil", 1)), 1))


def coarse_solve(rhs, level):
    width = rhs.shape[1]
    columns = rhs.shape[2]
    whole = lax.all_gather(rhs, ("slab", "pencil"), axis=0, tiled=True)
    whole = whole.reshape(lax.axis_size("slab"), lax.axis_size("pencil") * width, columns)
    solved = vcycle(jnp.zeros_like(whole), whole, level)
    start_y = lax.axis_index("pencil") * width
    return lax.dynamic_slice(
        solved, (lax.axis_index("slab"), start_y, jnp.int32(0)), (1, width, columns)
    )


def split_vcycle(u, rhs, level, from_zero):
    if rhs.shape[0] == 1:
        return coarse_solve(rhs, level)
    weight = step_weight(level)
    if from_zero:
        u = weight * rhs
    else:
        u = u + weight * (rhs - apply_padded(rim_one(u), level))
    u = u + weight * (rhs - apply_padded(rim_one(u), level))
    resid = rhs - apply_padded(rim_one(u), level)
    correction = split_vcycle(None, restrict(resid), level + 1, True)
    u = u + prolong(correction)
    u = u + weight * (rhs - apply_padded(rim_one(u), level))
    u = u + weight * (rhs - apply_padded(rim_one(u), level))
    return u


def plain(potential, parent_store, face_owner, face_offset):
    depth, width, columns = potential.shape
    grown = widen_x(padded(potential, (("slab", 0), ("pencil", 1)), 1))
    source = hessian_source(grown)
    slab_index = lax.axis_index("slab")
    wanted = face_owner[slab_index] * parent_store.shape[0] + face_offset[slab_index]
    piece = lax.all_gather(parent_store, "slab", axis=0, tiled=True)
    labels = jnp.arange(piece.shape[0], dtype=jnp.int32)
    match = labels == wanted
    faces = jnp.sum(jnp.where(match[:, None, None, None], piece, 0.0), axis=0)
    rhs = -source
    rhs = rhs.at[:, :, 0].add(faces[0])
    rhs = rhs.at[:, :, columns - 1].add(faces[1])
    solved = jnp.zeros_like(rhs)
    for cycle in range(CYCLES):
        solved = split_vcycle(solved, rhs, 0, cycle == 0)
    return (solved, source)


def on_device(potential, parent_store, face_owner, face_offset):
    if fits_window(potential, parent_store):
        return windowed(potential, parent_store, face_owner, face_offset)
    return plain(potential, parent_store, face_owner, face_offset)


def solution(mesh):
    in_specs = (P("slab", "pencil", None), P("slab", None, None, "pencil"), P(), P())
    out_specs = (P("slab", "pencil", None), P("slab", "pencil", None))
    return jax.shard_map(
        on_device, mesh=mesh, in_specs=in_specs, out_specs=out_specs, check_vma=False
    )
```

```python
from functools import partial

import jax
import jax.numpy as jnp
import numpy as np
from jax import lax
from jax.experimental import pallas as pl
from jax.experimental.pallas import tpu as pltpu
from jax.sharding import PartitionSpec as P

CYCLES = 2
OMEGA = 0.8
W = float(np.float32(OMEGA / 6.0))
KEEP = 1.0 - 6.0 * W
HALO = 8
LANES = 128
UNROLL = 16
PAIRS = 8
HESS = 8
LEVEL = 16
LPAIRS = 4


def is_coarsest(shape):
    return min(shape) <= 4 or any((d % 2 for d in shape))


def lane_iota(shape):
    return lax.broadcasted_iota(jnp.int32, shape, len(shape) - 1)


def row_iota(shape):
    return lax.broadcasted_iota(jnp.int32, shape, len(shape) - 2)


def x_other(values, odd):
    lane = lane_iota(values.shape)
    if odd:
        return jnp.where(lane == LANES - 1, 0.0, pltpu.roll(values, LANES - 1, 1))
    return jnp.where(lane == 0, 0.0, pltpu.roll(values, 1, 1))


def y_other(values, odd):
    return pltpu.roll(values, values.shape[0] - 1 if odd else 1, 0)


def swept(below, here, above, q, c):
    across, along = here[c ^ 1], here[c ^ 2]
    near = (below + above) + (across + x_other(across, c & 1))
    near = near + (along + y_other(along, c >> 1))
    return KEEP * here[c] + W * near + q


def parts(ref, z):
    return [ref[z, c] for c in range(4)]


def halo_mask(pencil, pencils):
    row = row_iota((8, LANES))
    above = jnp.where(pencil < pencils - 1, 1.0, 0.0)
    below = jnp.where(pencil > 0, 1.0, 0.0)
    return jnp.where(row < 4, above, below)


def put(ref, z, c, values, mask):
    own = values.shape[0] - 8
    ref[z, c, pl.ds(0, own), :] = values[:own]
    ref[z, c, pl.ds(own, 8), :] = values[own:] * mask


def index_pair(rows, columns):
    return (
        lax.broadcasted_iota(jnp.int32, (rows, columns), 0),
        lax.broadcasted_iota(jnp.int32, (rows, columns), 1),
    )


def chosen(where, value):
    return jnp.where(where, value, 0.0).astype(jnp.bfloat16)


def splitting_matrix():
    i, j = index_pair(2 * LANES, 2 * LANES)
    return chosen(i == 2 * (j & (LANES - 1)) + (j >= LANES).astype(jnp.int32), 1.0)


def merging_matrix():
    i, j = index_pair(2 * LANES, 2 * LANES)
    return chosen(j == 2 * (i & (LANES - 1)) + (i >= LANES).astype(jnp.int32), 1.0)


def mm(a, b):
    high = a.astype(jnp.bfloat16)
    rest = a - high.astype(jnp.float32)
    middle = rest.astype(jnp.bfloat16)
    low = (rest - middle.astype(jnp.float32)).astype(jnp.bfloat16)

    def dot(x):
        return jnp.dot(x, b, preferred_element_type=jnp.float32)

    return dot(high) + (dot(middle) + dot(low))


def pair_sum(values, distance, axis):
    size = values.shape[axis]
    at = lax.broadcasted_iota(jnp.int32, values.shape, axis)
    ahead = pltpu.roll(values, size - distance, axis)
    behind = pltpu.roll(values, distance, axis)
    return values + jnp.where((at & distance) == 0, ahead, behind)


def x_sides(values, distance):
    lane = lane_iota(values.shape)
    left = jnp.where(lane < distance, 0.0, pltpu.roll(values, distance, 1))
    right = jnp.where(lane >= LANES - distance, 0.0, pltpu.roll(values, LANES - distance, 1))
    return left + right


def flat_sweep(u, q, rows, yd, xd):
    total = u.shape[0]
    zero = jnp.zeros((rows, LANES), jnp.float32)
    below = jnp.concatenate([zero, u[: total - rows]], axis=0)
    above = jnp.concatenate([u[rows:], zero], axis=0)
    y = row_iota(u.shape) & (rows - 1)
    down = jnp.where(y < yd, 0.0, pltpu.roll(u, yd, 0))
    up = jnp.where(y >= rows - yd, 0.0, pltpu.roll(u, total - yd, 0))
    return KEEP * u + W * ((below + above) + (down + up) + x_sides(u, xd)) + q


def flat_vcycle(q, shape, rows, yd, xd):
    if is_coarsest(shape):
        u = q
        for _ in range(7):
            u = flat_sweep(u, q, rows, yd, xd)
        return u
    zs, ys, xs = shape
    u = flat_sweep(q, q, rows, yd, xd)
    change = flat_sweep(u, q, rows, yd, xd) - u
    pairs = [
        change[2 * z * rows : (2 * z + 1) * rows] + change[(2 * z + 1) * rows : (2 * z + 2) * rows]
        for z in range(zs // 2)
    ]
    coarse = 0.5 * pair_sum(pair_sum(jnp.concatenate(pairs, axis=0), yd, 0), xd, 1)
    e = flat_vcycle(coarse, (zs // 2, ys // 2, xs // 2), rows, 2 * yd, 2 * xd)
    planes = []
    for z in range(zs // 2):
        planes += [e[z * rows : (z + 1) * rows]] * 2
    u = u + jnp.concatenate(planes, axis=0)
    u = flat_sweep(u, q, rows, yd, xd)
    return flat_sweep(u, q, rows, yd, xd)


def solve_level_one(gathered_ref, v_ref, q_ref, a_ref, b_ref, tmp_ref, shape):
    zs, ys, xs = shape
    pencils = gathered_ref.shape[0]
    rows = ys // 2
    piece = rows // pencils
    row = row_iota((rows, LANES))
    blank = jnp.zeros((rows, LANES), jnp.float32)
    for ref in (q_ref, a_ref, b_ref):
        for z in (0, zs + 1):
            for c in range(2):
                ref[z, c] = blank
    edge = jnp.zeros((HALO, LANES), jnp.float32)
    for z in range(zs + 2):
        v_ref[z, pl.ds(0, HALO), :] = edge
        v_ref[z, pl.ds(HALO + ys, HALO), :] = edge
    for z in (0, zs + 1):
        for c in range(2):
            v_ref[z, pl.ds(HALO + c * rows, rows), :] = blank
    for z in range(zs):
        for c in range(2):
            for p in range(pencils):
                spot = pl.ds(2 * piece * z + c, piece, stride=2)
                q_ref[z + 1, c, pl.ds(p * piece, piece), :] = gathered_ref[p, spot, :]

    def sweep_plane(src, z):
        here = [src[z, 0], src[z, 1]]
        new = []
        for c in range(2):
            other = here[1 - c]
            if c:
                beyond = jnp.where(row == rows - 1, 0.0, pltpu.roll(other, rows - 1, 0))
            else:
                beyond = jnp.where(row == 0, 0.0, pltpu.roll(other, 1, 0))
            near = (src[z - 1, c] + src[z + 1, c]) + (other + beyond) + x_sides(here[c], 1)
            new.append(KEEP * here[c] + W * near + q_ref[z, c])
        return here, new

    def sweep(src, dst):
        def body(z, carry):
            _, new = sweep_plane(src, z)
            for c in range(2):
                dst[z, c] = new[c]
            return carry

        lax.fori_loop(1, zs + 1, body, 0, unroll=LEVEL)

    sweep(q_ref, a_ref)

    def restrict(z, carry):
        total = None
        for at in (2 * z + 1, 2 * z + 2):
            here, new = sweep_plane(a_ref, at)
            change = (new[0] - here[0]) + (new[1] - here[1])
            total = change if total is None else total + change
        tmp_ref[pl.ds(pl.multiple_of(z * rows, rows), rows), :] = 0.5 * pair_sum(total, 1, 1)
        return carry

    lax.fori_loop(0, zs // 2, restrict, 0, unroll=LPAIRS)
    tmp_ref[...] = flat_vcycle(tmp_ref[...], (zs // 2, ys // 2, xs // 2), rows, 1, 2)

    def correct(z, carry):
        e = tmp_ref[pl.ds(pl.multiple_of(z * rows, rows), rows), :]
        for at in (2 * z + 1, 2 * z + 2):
            for c in range(2):
                a_ref[at, c] = a_ref[at, c] + e
        return carry

    lax.fori_loop(0, zs // 2, correct, 0, unroll=LPAIRS)
    sweep(a_ref, b_ref)

    def last_sweep(z, carry):
        _, new = sweep_plane(b_ref, z)
        for c in range(2):
            v_ref[z, pl.ds(HALO + c, rows, stride=2), :] = new[c]
        return carry

    lax.fori_loop(1, zs + 1, last_sweep, 0, unroll=LEVEL)


def pack_kernel(
    potential_hbm, store_hbm, out_ref, even_ref, odd_ref, potential_ref, store_ref, sems
):
    copies = [
        pltpu.make_async_copy(potential_hbm, potential_ref, sems.at[0]),
        pltpu.make_async_copy(store_hbm, store_ref, sems.at[1]),
    ]
    for copy in copies:
        copy.start()
    for copy in copies:
        copy.wait()
    depth, width, columns = potential_ref.shape
    slots = store_ref.shape[0]
    part = width // 2
    split = mm(potential_ref[...].reshape(depth * width, columns), splitting_matrix())
    even_ref[...] = split[:, :LANES]
    odd_ref[...] = split[:, LANES:]
    for z in range(depth):
        for c in range(4):
            ref = odd_ref if c & 1 else even_ref
            spot = pl.ds((4 * z + c) * part, part)
            out_ref[spot, :] = ref[pl.ds(z * width + (c >> 1), part, stride=2), :]
    base = depth * width * 2
    for slot in range(slots):
        for side in range(2):
            spot = pl.ds(base + side * depth, depth)
            out_ref[spot, pl.ds(slot * width, width)] = store_ref[slot, side]


OFFSETS = (0, 4, 3, 1, 2, 7, 5, 6)
EARLY = 5


def block_rows(ref, start, count):
    return ref[pl.ds(start, count), :]


def ends(load, first, second, part, low_half):
    head = jnp.where(low_half, load(first, 8), pltpu.roll(load(second, 8), 4, 0))
    tail = jnp.where(
        low_half, pltpu.roll(load(first + part - 8, 8), 4, 0), load(second + part - 8, 8)
    )
    return head, tail


def store_ends(ref, pencil, out_refs, at, depth, part):
    even_ref, odd_ref = out_refs
    is_even = (pencil % 2) == 0
    low_half = row_iota((8, LANES)) < 4
    for z in range(depth):
        for t in range(2):
            head, tail = ends(
                partial(block_rows, ref),
                (4 * z + 2 * t) * part, (4 * z + 2 * t + 1) * part, part, low_half,
            )
            even_ref[at + 2 * z + t] = jnp.where(is_even, tail, head)
            odd_ref[at + 2 * z + t] = jnp.where(is_even, head, tail)


def early_edges_kernel(scalar_ref, *refs, depth, width):
    blocks, out_refs = refs[:EARLY], refs[EARLY:]
    for k, ref in enumerate(blocks):
        store_ends(ref, scalar_ref[1], out_refs, 2 * depth * k, depth, width // 2)


def late_edges_kernel(scalar_ref, *refs, depth, width):
    slabs = len(OFFSETS)
    even_ref, odd_ref, faces_ref, store_ref, rows_ref = refs[slabs:]
    slab = scalar_ref[0]
    pencil = scalar_ref[1]
    planes = slabs * depth
    part = width // 2
    is_even = (pencil % 2) == 0
    low_half = row_iota((8, LANES)) < 4
    base = depth * width * 2
    late = refs[EARLY:slabs]
    for k, ref in enumerate(late):
        store_ends(ref, pencil, (even_ref, odd_ref), 2 * depth * k, depth, part)
    for offset, ref in zip(OFFSETS, refs):
        store_ref[slab ^ offset] = block_rows(ref, base, 8)
    rest = LANES - 2 * planes
    rows_ref[pl.ds(2 * planes, rest), :] = jnp.zeros((rest, LANES), jnp.float32)
    for s in range(slabs):
        tile = store_ref[scalar_ref[2 + s]]
        slot = scalar_ref[2 + slabs + s]
        picked = pltpu.roll(tile, (LANES - slot * width) & (LANES - 1), 1)
        rows_ref[pl.ds(s * depth, depth), :] = picked[:depth]
        rows_ref[pl.ds(planes + s * depth, depth), :] = picked[depth:]
    rows_ref[...] = rows_ref[...].T
    faces_ref[pl.ds(0, part), :] = rows_ref[pl.ds(0, part, stride=2), :]
    faces_ref[pl.ds(part, part), :] = rows_ref[pl.ds(1, part, stride=2), :]
    head, tail = ends(partial(block_rows, faces_ref), 0, part, part, low_half)
    even_ref[2 * depth * len(late)] = jnp.where(is_even, tail, head)
    odd_ref[2 * depth * len(late)] = jnp.where(is_even, head, tail)


def halo_tiles(even_ref, odd_ref, index, is_even, low_half):
    first = even_ref[index]
    second = odd_ref[index]
    above = jnp.where(is_even, first, second)
    below = jnp.where(is_even, second, first)
    return (
        jnp.where(low_half, above, pltpu.roll(below, 4, 0)),
        jnp.where(low_half, pltpu.roll(above, 4, 0), below),
    )


def join_planes(load, out_ref, left_ref, right_ref, depth, width):
    part = width // 2
    for z in range(depth):
        for c in range(4):
            ref = right_ref if c & 1 else left_ref
            ref[pl.ds(z * width + (c >> 1), part, stride=2), :] = load(z, c)
    rows = depth * width
    both = jnp.concatenate([left_ref[pl.ds(0, rows), :], right_ref[pl.ds(0, rows), :]], axis=1)
    out_ref[...] = mm(both, merging_matrix()).reshape(depth, width, 2 * LANES)


def hessian_parts(below, here, above):
    rise = [a - b for a, b in zip(above, below)]
    y_sum, y_rise, yz_rise = [], [], []
    for c in range(4):
        odd = c >> 1
        same, other = here[c ^ 2], y_other(here[c ^ 2], odd)
        y_sum.append(same + other)
        y_rise.append(other - same if odd else same - other)
        same, other = rise[c ^ 2], y_other(rise[c ^ 2], odd)
        yz_rise.append(other - same if odd else same - other)
    out = []
    for c in range(4):
        odd = c & 1
        same, other = here[c ^ 1], x_other(here[c ^ 1], odd)
        twice = 2.0 * here[c]
        pxx = same + other - twice
        pyy = y_sum[c] - twice
        pzz = below[c] + above[c] - twice
        same, other = rise[c ^ 1], x_other(rise[c ^ 1], odd)
        pxz = other - same if odd else same - other
        same, other = y_rise[c ^ 1], x_other(y_rise[c ^ 1], odd)
        pxy = other - same if odd else same - other
        cross = pxy * pxy + pxz * pxz + yz_rise[c] * yz_rise[c]
        out.append(pxx * pyy + (pxx + pyy) * pzz - 0.0625 * cross)
    return out


def face_part(face, c, z, planes):
    lane = lane_iota(face.shape)
    if c & 1:
        turned = pltpu.roll(face, LANES - 1 - planes - z, 1)
        return jnp.where(lane == LANES - 1, turned, 0.0)
    turned = pltpu.roll(face, (LANES - z) & (LANES - 1), 1)
    return jnp.where(lane == 0, turned, 0.0)


def fill_block(p_ref, at, ref, edge_refs, tile, pencil, depth, part):
    is_even = (pencil % 2) == 0
    low_half = row_iota((8, LANES)) < 4
    for z in range(depth):
        for c in range(4):
            p_ref[at + z, c, pl.ds(0, part), :] = block_rows(ref, (4 * z + c) * part, part)
        for t in range(2):
            first, second = halo_tiles(*edge_refs, tile + 2 * z + t, is_even, low_half)
            p_ref[at + z, 2 * t, pl.ds(part, 8), :] = first
            p_ref[at + z, 2 * t + 1, pl.ds(part, 8), :] = second


def near_half_kernel(scalar_ref, *refs, depth, width, pencils):
    near = [k for k in range(EARLY) if OFFSETS[k] < 4]
    blocks = refs[: len(near)]
    even_ref, odd_ref, faces_ref, p_ref, s_ref, q_ref = refs[len(near) :]
    slab = scalar_ref[0]
    pencil = scalar_ref[1]
    part = width // 2
    half = 4 * depth
    first_plane = (slab // 4) * half
    mask = halo_mask(pencil, pencils)
    blank = jnp.zeros(p_ref.shape[1:], jnp.float32)
    p_ref[0] = blank
    p_ref[half + 1] = blank
    for k, ref in zip(near, blocks):
        at = ((slab ^ OFFSETS[k]) % 4) * depth + 1
        fill_block(p_ref, at, ref, (even_ref, odd_ref), 2 * depth * k, pencil, depth, part)

    def body(j, carry):
        source = hessian_parts(parts(p_ref, j), parts(p_ref, j + 1), parts(p_ref, j + 2))
        for c in range(4):
            s_ref[j, c] = source[c][:part]
            face = faces_ref[pl.ds((c >> 1) * part, part), :]
            face = face_part(face, c, first_plane + j, 2 * half)
            q_ref[j, c, pl.ds(0, part), :] = W * (face - source[c][:part])
            q_ref[j, c, pl.ds(part, 8), :] = (-W * mask) * source[c][part:]
        return carry

    lax.fori_loop(0, half, body, 0, unroll=HESS)


def far_half_kernel(scalar_ref, *refs, depth, width, pencils):
    far = [k for k in range(len(OFFSETS)) if OFFSETS[k] >= 4]
    blocks = refs[: len(far)]
    early_refs = refs[len(far) : len(far) + 2]
    late_refs = refs[len(far) + 2 : len(far) + 4]
    faces_ref, pn_ref, sn_ref, qn_ref = refs[len(far) + 4 : len(far) + 8]
    source_hbm, q_ref, u_ref, coarse_ref = refs[len(far) + 8 : len(far) + 12]
    p_ref, f_ref, s_ref, left_ref, right_ref, source_ref, sem = refs[len(far) + 12 :]
    slab = scalar_ref[0]
    pencil = scalar_ref[1]
    part = width // 2
    half = 4 * depth
    planes = 2 * half
    lower = slab < 4
    near_first = jnp.where(lower, 0, half)
    far_first = half - near_first
    is_even = (pencil % 2) == 0
    low_half = row_iota((8, LANES)) < 4
    mask = halo_mask(pencil, pencils)
    blank = jnp.zeros(p_ref.shape[1:], jnp.float32)
    for ref in (q_ref, u_ref):
        for z in (0, 1, planes + 2, planes + 3):
            ref[z] = blank
    p_ref[jnp.where(lower, half + 1, 0)] = blank
    p_ref[jnp.where(lower, 0, half + 1)] = pn_ref[jnp.where(lower, half, 1)]
    for k, ref in zip(far, blocks):
        at = ((slab ^ OFFSETS[k]) % 4) * depth + 1
        early = k < EARLY
        tile = 2 * depth * (k if early else k - EARLY)
        edge_refs = early_refs if early else late_refs
        fill_block(p_ref, at, ref, edge_refs, tile, pencil, depth, part)
    face_tile = 2 * depth * (len(OFFSETS) - EARLY)
    first, second = halo_tiles(*late_refs, face_tile, is_even, low_half)
    f_ref[0, pl.ds(0, part), :] = faces_ref[pl.ds(0, part), :]
    f_ref[0, pl.ds(part, 8), :] = first
    f_ref[1, pl.ds(0, part), :] = faces_ref[pl.ds(part, part), :]
    f_ref[1, pl.ds(part, 8), :] = second

    def finish(source, z):
        for c in range(4):
            face = face_part(f_ref[c >> 1], c, z, planes)
            put(q_ref, z + 2, c, W * (face - source[c]), mask)

    def copy(j, carry):
        z = near_first + j
        for c in range(4):
            face = face_part(f_ref[c >> 1, pl.ds(part, 8), :], c, z, planes)
            q_ref[z + 2, c, pl.ds(0, part), :] = qn_ref[j, c, pl.ds(0, part), :]
            q_ref[z + 2, c, pl.ds(part, 8), :] = (
                qn_ref[j, c, pl.ds(part, 8), :] + (W * mask) * face
            )
        return carry

    lax.fori_loop(0, half, copy, 0, unroll=UNROLL)

    def body(j, carry):
        source = hessian_parts(parts(p_ref, j), parts(p_ref, j + 1), parts(p_ref, j + 2))
        finish(source, far_first + j)
        return carry

    lax.fori_loop(0, half, body, 0, unroll=HESS)
    seam = jnp.where(lower, half, 1)
    here = parts(pn_ref, seam)
    inner = parts(pn_ref, jnp.where(lower, half - 1, 2))
    outer = parts(p_ref, jnp.where(lower, 1, half))
    below = [jnp.where(lower, a, b) for a, b in zip(inner, outer)]
    above = [jnp.where(lower, b, a) for a, b in zip(inner, outer)]
    source = hessian_parts(below, here, above)
    finish(source, near_first + seam - 1)
    own = (slab % 4) * depth
    for z in range(depth):
        is_seam = own + z == seam - 1
        for c in range(4):
            s_ref[z, c] = jnp.where(is_seam, source[c][:part], sn_ref[own + z, c])
    join_planes(lambda z, c: s_ref[z, c], source_ref, left_ref, right_ref, depth, width)
    copy_out = pltpu.make_async_copy(source_ref, source_hbm, sem)
    copy_out.start()

    def second_sweep(z, carry):
        here = parts(q_ref, z + 2)
        for c in range(4):
            new = swept(q_ref[z + 1, c], here, q_ref[z + 3, c], here[c], c)
            put(u_ref, z + 2, c, new, mask)
        return carry

    lax.fori_loop(0, planes, second_sweep, 0, unroll=UNROLL)
    restrict_window(u_ref, q_ref, coarse_ref, planes, part)
    copy_out.wait()


def restrict_window(u_ref, q_ref, coarse_ref, planes, part):
    def restrict(z, carry):
        total = None
        for at in (2 * z + 2, 2 * z + 3):
            here = parts(u_ref, at)
            for c in range(4):
                new = swept(u_ref[at - 1, c], here, u_ref[at + 1, c], q_ref[at, c], c)
                change = (new - here[c])[:part]
                total = change if total is None else total + change
        coarse_ref[pl.ds(pl.multiple_of(z * part, part), part), :] = 0.5 * total
        return carry

    lax.fori_loop(0, planes // 2, restrict, 0, unroll=PAIRS)


def coarse_window(v_ref, z, pencil, part):
    start = pl.multiple_of(pencil * part, part)
    own = v_ref[z, pl.ds(start + HALO, part), :]
    above = v_ref[z, pl.ds(start + HALO + part, 8), :]
    below = v_ref[z, pl.ds(start, 8), :]
    tile = jnp.where(row_iota((8, LANES)) < 4, above, below)
    return jnp.concatenate([own, tile], axis=0)


def middle_kernel(
    scalar_ref, gathered_ref, q_ref, u_ref, qwin_ref, uwin_ref, coarse_ref,
    v_ref, q1_ref, a1_ref, b1_ref, tmp_ref, a_ref, b_ref, *, depth, width, pencils, shape
):
    slab = scalar_ref[0]
    pencil = scalar_ref[1]
    planes = a_ref.shape[0] - 4
    part = width // 2
    mask = halo_mask(pencil, pencils)
    solve_level_one(gathered_ref, v_ref, q1_ref, a1_ref, b1_ref, tmp_ref, shape)
    blank = jnp.zeros(a_ref.shape[1:], jnp.float32)
    for ref in (a_ref, b_ref):
        for z in (0, 1, planes + 2, planes + 3):
            ref[z] = blank

    def correct(z, carry):
        wide = coarse_window(v_ref, z + 1, pencil, part)
        for at in (2 * z + 2, 2 * z + 3):
            for c in range(4):
                a_ref[at, c] = u_ref[at, c] + wide
        return carry

    lax.fori_loop(0, planes // 2, correct, 0, unroll=PAIRS)

    def sweep(src, dst):
        def body(z, carry):
            here = parts(src, z + 2)
            for c in range(4):
                new = swept(src[z + 1, c], here, src[z + 3, c], q_ref[z + 2, c], c)
                put(dst, z + 2, c, new, mask)
            return carry

        lax.fori_loop(0, planes, body, 0, unroll=UNROLL)

    sweep(a_ref, b_ref)
    sweep(b_ref, a_ref)
    sweep(a_ref, b_ref)
    sweep(b_ref, a_ref)
    restrict_window(a_ref, q_ref, coarse_ref, planes, part)
    for z in range(depth + 4):
        qwin_ref[z] = q_ref[slab * depth + z]
        uwin_ref[z] = a_ref[slab * depth + z]


def last_kernel(
    scalar_ref, gathered_ref, qwin_ref, uwin_ref, out_ref,
    v_ref, q1_ref, a1_ref, b1_ref, tmp_ref, a_ref, b_ref, left_ref, right_ref,
    *, depth, width, pencils, shape
):
    slab = scalar_ref[0]
    pencil = scalar_ref[1]
    planes = shape[0] * 2
    part = width // 2
    mask = halo_mask(pencil, pencils)
    solve_level_one(gathered_ref, v_ref, q1_ref, a1_ref, b1_ref, tmp_ref, shape)
    for z in range(depth // 2 + 2):
        wide = coarse_window(v_ref, slab * (depth // 2) + z, pencil, part)
        for at in (2 * z, 2 * z + 1):
            for c in range(4):
                a_ref[at, c] = uwin_ref[at, c] + wide
    for z in range(1, depth + 3):
        at = slab * depth - 2 + z
        live = jnp.where((at >= 0) & (at < planes), 1.0, 0.0)
        here = parts(a_ref, z)
        for c in range(4):
            new = swept(a_ref[z - 1, c], here, a_ref[z + 1, c], qwin_ref[z, c], c)
            put(b_ref, z, c, live * new, mask)
    done = {}
    for z in range(2, depth + 2):
        here = parts(b_ref, z)
        for c in range(4):
            new = swept(b_ref[z - 1, c], here, b_ref[z + 1, c], qwin_ref[z, c], c)
            done[z - 2, c] = new[:part]
    join_planes(lambda z, c: done[z, c], out_ref, left_ref, right_ref, depth, width)


def vmem():
    return pl.BlockSpec(memory_space=pltpu.VMEM)


def smem():
    return pl.BlockSpec(memory_space=pltpu.SMEM)


def arr(*shape):
    return jax.ShapeDtypeStruct(shape, jnp.float32)


def buf(*shape):
    return pltpu.VMEM(shape, jnp.float32)


def call(kernel, name, scalars, args, outs, scratch=(), space=pltpu.VMEM, out_space=None):
    out_specs = jax.tree.map(lambda _: vmem(), outs)
    if out_space is not None:
        out_specs = tuple(pl.BlockSpec(memory_space=one) for one in out_space)
    return pl.pallas_call(
        kernel,
        out_shape=outs,
        in_specs=[smem()] * len(scalars) + [pl.BlockSpec(memory_space=space)] * len(args),
        out_specs=out_specs,
        scratch_shapes=list(scratch),
        compiler_params=pltpu.CompilerParams(vmem_limit_bytes=16 << 20),
        name=name,
    )(*scalars, *args)


def windowed(potential, parent_store, face_owner, face_offset):
    depth, width, columns = potential.shape
    slabs = lax.axis_size("slab")
    pencils = lax.axis_size("pencil")
    planes, height = slabs * depth, pencils * width
    part = width // 2
    rows = part + 8
    where = jnp.stack([lax.axis_index("slab"), lax.axis_index("pencil")]).astype(jnp.int32)
    scalars = jnp.concatenate([where, face_owner, face_offset])
    own = call(
        pack_kernel,
        "pack",
        [],
        [pltpu.with_memory_space_constraint(x, pltpu.HBM) for x in (potential, parent_store)],
        arr(depth * width * 2 + 8, LANES),
        [
            buf(depth * width, LANES),
            buf(depth * width, LANES),
            buf(*potential.shape),
            buf(*parent_store.shape),
            pltpu.SemaphoreType.DMA((2,)),
        ],
        space=pltpu.HBM,
    )

    def swap(x, bits):
        return lax.ppermute(x, "slab", [(i, i ^ bits) for i in range(slabs)])

    near = [swap(own, bits) for bits in OFFSETS[1:5]]
    blocks = [own, *near] + [swap(near[0], bits) for bits in OFFSETS[2:5]]
    low_pairs = [(i, i + 1) for i in range(0, pencils - 1, 2)]
    high_pairs = [(i, i + 1) for i in range(1, pencils - 1, 2)]

    def beside(even, odd):
        return (
            lax.ppermute(even, "pencil", low_pairs + [(j, i) for i, j in low_pairs]),
            lax.ppermute(odd, "pencil", high_pairs + [(j, i) for i, j in high_pairs]),
        )

    message = arr(2 * depth * EARLY, 8, LANES)
    early = call(
        partial(early_edges_kernel, depth=depth, width=width),
        "early_edges",
        [scalars],
        blocks[:EARLY],
        (message, message),
    )
    early = beside(*early)
    message = arr(2 * depth * (slabs - EARLY) + 1, 8, LANES)
    even, odd, faces = call(
        partial(late_edges_kernel, depth=depth, width=width),
        "late_edges",
        [scalars],
        blocks,
        (message, message, arr(width, LANES)),
        [buf(slabs, 8, LANES), buf(LANES, LANES)],
    )
    late = beside(even, odd)
    shape = (planes // 2, height // 2, columns // 2)
    coarse_part = arr(planes // 2 * part, LANES)
    field = (planes + 4, 4, rows, LANES)
    half = planes // 2
    near = call(
        partial(near_half_kernel, depth=depth, width=width, pencils=pencils),
        "near_half",
        [scalars],
        [b for b, offset in zip(blocks, OFFSETS) if offset < 4] + [*early, faces],
        (arr(half + 2, 4, rows, LANES), arr(half, 4, part, LANES), arr(half, 4, rows, LANES)),
    )
    source, q, u, coarse = call(
        partial(far_half_kernel, depth=depth, width=width, pencils=pencils),
        "far_half",
        [scalars],
        [b for b, offset in zip(blocks, OFFSETS) if offset >= 4] + [*early, *late, faces, *near],
        (arr(depth, width, columns), arr(*field), arr(*field), coarse_part),
        [
            buf(half + 2, 4, rows, LANES),
            buf(2, rows, LANES),
            buf(depth, 4, part, LANES),
            buf(depth * width, LANES),
            buf(depth * width, LANES),
            buf(depth, width, columns),
            pltpu.SemaphoreType.DMA,
        ],
        out_space=[pl.ANY] + [pltpu.VMEM] * 3,
    )
    level = (shape[0] + 2, 2, shape[1] // 2, LANES)
    level_scratch = [
        buf(shape[0] + 2, shape[1] + 2 * HALO, LANES),
        buf(*level),
        buf(*level),
        buf(*level),
        buf(shape[0] * shape[1] // 4, LANES),
    ]

    def gather(x):
        return lax.all_gather(x, "pencil", axis=0, tiled=False)

    sizes = dict(depth=depth, width=width, pencils=pencils, shape=shape)
    slim = (depth + 4, 4, rows, LANES)
    qwin, uwin, coarse = call(
        partial(middle_kernel, **sizes),
        "middle",
        [scalars],
        [gather(coarse), q, u],
        (arr(*slim), arr(*slim), coarse_part),
        level_scratch + [buf(*field), buf(*field)],
    )
    solved = call(
        partial(last_kernel, **sizes),
        "last",
        [scalars],
        [gather(coarse), qwin, uwin],
        arr(depth, width, columns),
        level_scratch
        + [buf(*slim), buf(*slim), buf(depth * width, LANES), buf(depth * width, LANES)],
    )
    return solved, source


def fits_window(potential, parent_store):
    depth, width, columns = potential.shape
    slabs = lax.axis_size("slab")
    pencils = lax.axis_size("pencil")
    planes = slabs * depth
    return (
        slabs == 8
        and pencils % 2 == 0
        and depth == 4
        and columns == 2 * LANES
        and width == 32
        and parent_store.shape[0] * width == LANES
        and 2 * planes < LANES
        and pencils in (2, 4, 8)
    )


def padded(cells, sides, width):
    for axis, dim in sides:
        count = lax.axis_size(axis)
        ends = count - 1
        head = lax.slice_in_dim(cells, 0, width, axis=dim)
        tail = lax.slice_in_dim(cells, cells.shape[dim] - width, cells.shape[dim], axis=dim)
        cells = jnp.concatenate(
            [
                lax.ppermute(tail, axis, [(i, (i + 1) % count) for i in range(ends)]),
                cells,
                lax.ppermute(head, axis, [((i + 1) % count, i) for i in range(ends)]),
            ],
            axis=dim,
        )
    return cells


def hessian_source(p):
    c = p[1:-1, 1:-1, 1:-1]
    pxx = p[1:-1, 1:-1, 2:] + p[1:-1, 1:-1, :-2] - 2.0 * c
    pyy = p[1:-1, 2:, 1:-1] + p[1:-1, :-2, 1:-1] - 2.0 * c
    pzz = p[2:, 1:-1, 1:-1] + p[:-2, 1:-1, 1:-1] - 2.0 * c
    pxy = 0.25 * (p[1:-1, 2:, 2:] - p[1:-1, :-2, 2:] - p[1:-1, 2:, :-2] + p[1:-1, :-2, :-2])
    pxz = 0.25 * (p[2:, 1:-1, 2:] - p[:-2, 1:-1, 2:] - p[2:, 1:-1, :-2] + p[:-2, 1:-1, :-2])
    pyz = 0.25 * (p[2:, 2:, 1:-1] - p[:-2, 2:, 1:-1] - p[2:, :-2, 1:-1] + p[:-2, :-2, 1:-1])
    return pxx * pyy + pxx * pzz + pyy * pzz - pxy * pxy - pxz * pxz - pyz * pyz


def apply_padded(p, level):
    c = p[1:-1, 1:-1, 1:-1]
    near = p[2:, 1:-1, 1:-1] + p[:-2, 1:-1, 1:-1]
    near = near + p[1:-1, 2:, 1:-1] + p[1:-1, :-2, 1:-1]
    near = near + p[1:-1, 1:-1, 2:] + p[1:-1, 1:-1, :-2]
    return (6.0 * c - near) * 0.25**level


def step_weight(level):
    return OMEGA / 6.0 * 4.0**level


def sweep_whole(u, rhs, level):
    return u + step_weight(level) * (rhs - apply_padded(jnp.pad(u, 1), level))


def restrict(r):
    a, b, c = r.shape
    return r.reshape(a // 2, 2, b // 2, 2, c // 2, 2).mean(axis=(1, 3, 5))


def prolong(e):
    a, b, c = e.shape
    return jnp.broadcast_to(e[:, None, :, None, :, None], (a, 2, b, 2, c, 2)).reshape(
        2 * a, 2 * b, 2 * c
    )


def vcycle(u, rhs, level):
    if is_coarsest(rhs.shape):
        for sweep_count in range(8):
            u = sweep_whole(u, rhs, level)
        return u
    u = sweep_whole(u, rhs, level)
    u = sweep_whole(u, rhs, level)
    resid = rhs - apply_padded(jnp.pad(u, 1), level)
    coarse = restrict(resid)
    correction = vcycle(jnp.zeros_like(coarse), coarse, level + 1)
    u = u + prolong(correction)
    u = sweep_whole(u, rhs, level)
    u = sweep_whole(u, rhs, level)
    return u


def widen_x(p):
    return jnp.pad(p, ((0, 0), (0, 0), (1, 1)))


def rim_one(u):
    return widen_x(padded(u, (("slab", 0), ("pencil", 1)), 1))


def coarse_solve(rhs, level):
    width = rhs.shape[1]
    columns = rhs.shape[2]
    whole = lax.all_gather(rhs, ("slab", "pencil"), axis=0, tiled=True)
    whole = whole.reshape(lax.axis_size("slab"), lax.axis_size("pencil") * width, columns)
    solved = vcycle(jnp.zeros_like(whole), whole, level)
    start_y = lax.axis_index("pencil") * width
    return lax.dynamic_slice(
        solved, (lax.axis_index("slab"), start_y, jnp.int32(0)), (1, width, columns)
    )


def split_vcycle(u, rhs, level, from_zero):
    if rhs.shape[0] == 1:
        return coarse_solve(rhs, level)
    weight = step_weight(level)
    if from_zero:
        u = weight * rhs
    else:
        u = u + weight * (rhs - apply_padded(rim_one(u), level))
    u = u + weight * (rhs - apply_padded(rim_one(u), level))
    resid = rhs - apply_padded(rim_one(u), level)
    correction = split_vcycle(None, restrict(resid), level + 1, True)
    u = u + prolong(correction)
    u = u + weight * (rhs - apply_padded(rim_one(u), level))
    u = u + weight * (rhs - apply_padded(rim_one(u), level))
    return u


def plain(potential, parent_store, face_owner, face_offset):
    depth, width, columns = potential.shape
    grown = widen_x(padded(potential, (("slab", 0), ("pencil", 1)), 1))
    source = hessian_source(grown)
    slab_index = lax.axis_index("slab")
    wanted = face_owner[slab_index] * parent_store.shape[0] + face_offset[slab_index]
    piece = lax.all_gather(parent_store, "slab", axis=0, tiled=True)
    labels = jnp.arange(piece.shape[0], dtype=jnp.int32)
    match = labels == wanted
    faces = jnp.sum(jnp.where(match[:, None, None, None], piece, 0.0), axis=0)
    rhs = -source
    rhs = rhs.at[:, :, 0].add(faces[0])
    rhs = rhs.at[:, :, columns - 1].add(faces[1])
    solved = jnp.zeros_like(rhs)
    for cycle in range(CYCLES):
        solved = split_vcycle(solved, rhs, 0, cycle == 0)
    return (solved, source)


def on_device(potential, parent_store, face_owner, face_offset):
    if fits_window(potential, parent_store):
        return windowed(potential, parent_store, face_owner, face_offset)
    return plain(potential, parent_store, face_owner, face_offset)


def solution(mesh):
    in_specs = (P("slab", "pencil", None), P("slab", None, None, "pencil"), P(), P())
    out_specs = (P("slab", "pencil", None), P("slab", "pencil", None))
    return jax.shard_map(
        on_device, mesh=mesh, in_specs=in_specs, out_specs=out_specs, check_vma=False
    )
```

```python
from functools import partial

import jax
import jax.numpy as jnp
import numpy as np
from jax import lax
from jax.experimental import pallas as pl
from jax.experimental.pallas import tpu as pltpu
from jax.sharding import PartitionSpec as P

CYCLES = 2
OMEGA = 0.8
W = float(np.float32(OMEGA / 6.0))
KEEP = 1.0 - 6.0 * W
HALO = 8
LANES = 128
UNROLL = 16
PAIRS = 8
HESS = 8
LEVEL = 16
LPAIRS = 4


def is_coarsest(shape):
    return min(shape) <= 4 or any((d % 2 for d in shape))


def lane_iota(shape):
    return lax.broadcasted_iota(jnp.int32, shape, len(shape) - 1)


def row_iota(shape):
    return lax.broadcasted_iota(jnp.int32, shape, len(shape) - 2)


def x_other(values, odd):
    lane = lane_iota(values.shape)
    if odd:
        return jnp.where(lane == LANES - 1, 0.0, pltpu.roll(values, LANES - 1, 1))
    return jnp.where(lane == 0, 0.0, pltpu.roll(values, 1, 1))


def y_other(values, odd):
    return pltpu.roll(values, values.shape[0] - 1 if odd else 1, 0)


def neighbours(below, here, above, c):
    across, along = here[c ^ 1], here[c ^ 2]
    near = (below + above) + (across + x_other(across, c & 1))
    return near + (along + y_other(along, c >> 1))


def swept(below, here, above, q, c):
    return KEEP * here[c] + W * neighbours(below, here, above, c) + q


def swept_children(below, here, above):
    here = W * here
    base = ((1.0 - 3.0 * W) / W) * here
    beyond = [W * below, W * above]
    across = [base + x_other(here, odd) for odd in range(2)]
    along = [y_other(here, odd) for odd in range(2)]
    flat = [across[c & 1] + along[c >> 1] for c in range(4)]
    return [[one + beyond[k] for one in flat] for k in range(2)]


def parts(ref, z):
    return [ref[z, c] for c in range(4)]


def halo_mask(pencil, pencils):
    row = row_iota((8, LANES))
    above = jnp.where(pencil < pencils - 1, 1.0, 0.0)
    below = jnp.where(pencil > 0, 1.0, 0.0)
    return jnp.where(row < 4, above, below)


def put(ref, z, c, values, mask):
    own = values.shape[0] - 8
    ref[z, c, pl.ds(0, own), :] = values[:own]
    ref[z, c, pl.ds(own, 8), :] = values[own:] * mask


def index_pair(rows, columns):
    return (
        lax.broadcasted_iota(jnp.int32, (rows, columns), 0),
        lax.broadcasted_iota(jnp.int32, (rows, columns), 1),
    )


def chosen(where, value):
    return jnp.where(where, value, 0.0).astype(jnp.bfloat16)


def splitting_matrix():
    i, j = index_pair(2 * LANES, 2 * LANES)
    return chosen(i == 2 * (j & (LANES - 1)) + (j >= LANES).astype(jnp.int32), 1.0)


def merging_matrix():
    i, j = index_pair(2 * LANES, 2 * LANES)
    return chosen(j == 2 * (i & (LANES - 1)) + (i >= LANES).astype(jnp.int32), 1.0)


def mm(a, b):
    high = a.astype(jnp.bfloat16)
    rest = a - high.astype(jnp.float32)
    middle = rest.astype(jnp.bfloat16)
    low = (rest - middle.astype(jnp.float32)).astype(jnp.bfloat16)

    def dot(x):
        return jnp.dot(x, b, preferred_element_type=jnp.float32)

    return dot(high) + (dot(middle) + dot(low))


def pair_sum(values, distance, axis):
    size = values.shape[axis]
    at = lax.broadcasted_iota(jnp.int32, values.shape, axis)
    ahead = pltpu.roll(values, size - distance, axis)
    behind = pltpu.roll(values, distance, axis)
    return values + jnp.where((at & distance) == 0, ahead, behind)


def x_sides(values, distance):
    lane = lane_iota(values.shape)
    left = jnp.where(lane < distance, 0.0, pltpu.roll(values, distance, 1))
    right = jnp.where(lane >= LANES - distance, 0.0, pltpu.roll(values, LANES - distance, 1))
    return left + right


def flat_sweep(u, q, rows, yd, xd):
    total = u.shape[0]
    zero = jnp.zeros((rows, LANES), jnp.float32)
    below = jnp.concatenate([zero, u[: total - rows]], axis=0)
    above = jnp.concatenate([u[rows:], zero], axis=0)
    y = row_iota(u.shape) & (rows - 1)
    down = jnp.where(y < yd, 0.0, pltpu.roll(u, yd, 0))
    up = jnp.where(y >= rows - yd, 0.0, pltpu.roll(u, total - yd, 0))
    return KEEP * u + W * ((below + above) + (down + up) + x_sides(u, xd)) + q


def flat_vcycle(q, shape, rows, yd, xd):
    if is_coarsest(shape):
        u = q
        for _ in range(7):
            u = flat_sweep(u, q, rows, yd, xd)
        return u
    zs, ys, xs = shape
    u = flat_sweep(q, q, rows, yd, xd)
    change = flat_sweep(u, q, rows, yd, xd) - u
    pairs = [
        change[2 * z * rows : (2 * z + 1) * rows] + change[(2 * z + 1) * rows : (2 * z + 2) * rows]
        for z in range(zs // 2)
    ]
    coarse = 0.5 * pair_sum(pair_sum(jnp.concatenate(pairs, axis=0), yd, 0), xd, 1)
    e = flat_vcycle(coarse, (zs // 2, ys // 2, xs // 2), rows, 2 * yd, 2 * xd)
    planes = []
    for z in range(zs // 2):
        planes += [e[z * rows : (z + 1) * rows]] * 2
    u = u + jnp.concatenate(planes, axis=0)
    u = flat_sweep(u, q, rows, yd, xd)
    return flat_sweep(u, q, rows, yd, xd)


def solve_level_one(gathered_ref, v_ref, q_ref, a_ref, b_ref, tmp_ref, shape, near=None):
    zs, ys, xs = shape
    pencils = gathered_ref.shape[0]
    rows = ys // 2
    half = zs // 2
    piece = rows // pencils
    row = row_iota((rows, LANES))
    blank = jnp.zeros((rows, LANES), jnp.float32)
    for ref in (q_ref, a_ref, b_ref):
        for z in (0, 1, zs + 2, zs + 3):
            for c in range(2):
                ref[z, c] = blank
    for z in (0, 1, half + 2, half + 3):
        tmp_ref[pl.ds(z * rows, rows), :] = blank
    edge = jnp.zeros((HALO, LANES), jnp.float32)
    for z in range(zs + 2):
        v_ref[z, pl.ds(0, HALO), :] = edge
        v_ref[z, pl.ds(HALO + ys, HALO), :] = edge
    if near is None:
        for z in (0, zs + 1):
            for c in range(2):
                v_ref[z, pl.ds(HALO + c * rows, rows), :] = blank
    for z in range(zs):
        for c in range(2):
            for p in range(pencils):
                spot = pl.ds(2 * piece * z + c, piece, stride=2)
                q_ref[z + 2, c, pl.ds(p * piece, piece), :] = gathered_ref[p, spot, :]

    def y_beyond(other, c):
        if c:
            return jnp.where(row == rows - 1, 0.0, pltpu.roll(other, rows - 1, 0))
        return jnp.where(row == 0, 0.0, pltpu.roll(other, 1, 0))

    def around(src, z):
        here = [src[z, 0], src[z, 1]]
        near = []
        for c in range(2):
            other = here[1 - c]
            sides = (other + y_beyond(other, c)) + x_sides(here[c], 1)
            near.append((src[z - 1, c] + src[z + 1, c]) + sides)
        return here, near

    def second(z, carry):
        here, sides = around(q_ref, z)
        for c in range(2):
            a_ref[z, c] = (1.0 + KEEP) * here[c] + W * sides[c]
        return carry

    lax.fori_loop(2, zs + 2, second, 0, unroll=LEVEL)

    def restrict(z, carry):
        total = None
        for at in (2 * z + 2, 2 * z + 3):
            here, sides = around(a_ref, at)
            for c in range(2):
                new = KEEP * here[c] + W * sides[c] + q_ref[at, c]
                b_ref[at, c] = new
                change = new - here[c]
                total = change if total is None else total + change
        spot = pl.ds(pl.multiple_of((z + 2) * rows, rows), rows)
        tmp_ref[spot, :] = 0.5 * pair_sum(total, 1, 1)
        return carry

    pairs_unroll = LPAIRS if near is None else half
    lax.fori_loop(0, half, restrict, 0, unroll=pairs_unroll)
    inner = pl.ds(2 * rows, half * rows)
    tmp_ref[inner, :] = flat_vcycle(tmp_ref[inner, :], (half, ys // 2, xs // 2), rows, 1, 2)

    def live(at, count):
        return jnp.where((at >= 0) & (at < count), 1.0, 0.0)

    def third(z):
        e = [tmp_ref[pl.ds(pl.multiple_of((z + k) * rows, rows), rows), :] for k in (1, 2, 3)]
        here = W * e[1]
        base = ((1.0 - 4.0 * W) / W) * here + x_sides(here, 1)
        for c in range(2):
            flat = base + y_beyond(here, c)
            for k in range(2):
                new = b_ref[2 * z + 2 + k, c] + (flat + W * e[2 * k])
                a_ref[2 * z + 2 + k, c] = new if near is None else live(z, half) * new

    def fourth(z):
        here, sides = around(a_ref, z + 2)
        for c in range(2):
            new = KEEP * here[c] + W * sides[c] + q_ref[z + 2, c]
            if near is not None:
                new = live(z, zs) * new
            v_ref[z + 1, pl.ds(HALO + c, rows, stride=2), :] = new

    def loop(step, start, count, unroll):
        def body(i, carry):
            step(start + i)
            return carry

        lax.fori_loop(0, count, body, 0, unroll=unroll)

    if near is None:
        loop(third, 0, half, LPAIRS)
        loop(fourth, 0, zs, LEVEL)
    else:
        loop(third, near - 1, 3, 3)
        loop(fourth, 2 * near - 1, 4, 4)


def pack_kernel(
    potential_hbm, store_hbm, out_ref, even_ref, odd_ref, potential_ref, store_ref, sems
):
    copies = [
        pltpu.make_async_copy(potential_hbm, potential_ref, sems.at[0]),
        pltpu.make_async_copy(store_hbm, store_ref, sems.at[1]),
    ]
    for copy in copies:
        copy.start()
    for copy in copies:
        copy.wait()
    depth, width, columns = potential_ref.shape
    slots = store_ref.shape[0]
    part = width // 2
    split = mm(potential_ref[...].reshape(depth * width, columns), splitting_matrix())
    even_ref[...] = split[:, :LANES]
    odd_ref[...] = split[:, LANES:]
    for z in range(depth):
        for c in range(4):
            ref = odd_ref if c & 1 else even_ref
            spot = pl.ds((4 * z + c) * part, part)
            out_ref[spot, :] = ref[pl.ds(z * width + (c >> 1), part, stride=2), :]
    base = depth * width * 2
    for slot in range(slots):
        for side in range(2):
            spot = pl.ds(base + side * depth, depth)
            out_ref[spot, pl.ds(slot * width, width)] = store_ref[slot, side]


OFFSETS = (0, 4, 3, 1, 2, 7, 5, 6)
EARLY = 5


def block_rows(ref, start, count):
    return ref[pl.ds(start, count), :]


def ends(load, first, second, part, low_half):
    head = jnp.where(low_half, load(first, 8), pltpu.roll(load(second, 8), 4, 0))
    tail = jnp.where(
        low_half, pltpu.roll(load(first + part - 8, 8), 4, 0), load(second + part - 8, 8)
    )
    return head, tail


def store_ends(ref, pencil, out_refs, at, depth, part):
    even_ref, odd_ref = out_refs
    is_even = (pencil % 2) == 0
    low_half = row_iota((8, LANES)) < 4
    for z in range(depth):
        for t in range(2):
            head, tail = ends(
                partial(block_rows, ref),
                (4 * z + 2 * t) * part, (4 * z + 2 * t + 1) * part, part, low_half,
            )
            even_ref[at + 2 * z + t] = jnp.where(is_even, tail, head)
            odd_ref[at + 2 * z + t] = jnp.where(is_even, head, tail)


def early_edges_kernel(scalar_ref, *refs, depth, width):
    blocks, out_refs = refs[:EARLY], refs[EARLY:]
    for k, ref in enumerate(blocks):
        store_ends(ref, scalar_ref[1], out_refs, 2 * depth * k, depth, width // 2)


def late_edges_kernel(scalar_ref, *refs, depth, width):
    slabs = len(OFFSETS)
    even_ref, odd_ref, faces_ref, store_ref, rows_ref = refs[slabs:]
    slab = scalar_ref[0]
    pencil = scalar_ref[1]
    planes = slabs * depth
    part = width // 2
    is_even = (pencil % 2) == 0
    low_half = row_iota((8, LANES)) < 4
    base = depth * width * 2
    late = refs[EARLY:slabs]
    for k, ref in enumerate(late):
        store_ends(ref, pencil, (even_ref, odd_ref), 2 * depth * k, depth, part)
    for offset, ref in zip(OFFSETS, refs):
        store_ref[slab ^ offset] = block_rows(ref, base, 8)
    rest = LANES - 2 * planes
    rows_ref[pl.ds(2 * planes, rest), :] = jnp.zeros((rest, LANES), jnp.float32)
    for s in range(slabs):
        tile = store_ref[scalar_ref[2 + s]]
        slot = scalar_ref[2 + slabs + s]
        picked = pltpu.roll(tile, (LANES - slot * width) & (LANES - 1), 1)
        rows_ref[pl.ds(s * depth, depth), :] = picked[:depth]
        rows_ref[pl.ds(planes + s * depth, depth), :] = picked[depth:]
    rows_ref[...] = rows_ref[...].T
    faces_ref[pl.ds(0, part), :] = rows_ref[pl.ds(0, part, stride=2), :]
    faces_ref[pl.ds(part, part), :] = rows_ref[pl.ds(1, part, stride=2), :]
    head, tail = ends(partial(block_rows, faces_ref), 0, part, part, low_half)
    even_ref[2 * depth * len(late)] = jnp.where(is_even, tail, head)
    odd_ref[2 * depth * len(late)] = jnp.where(is_even, head, tail)


def halo_tiles(even_ref, odd_ref, index, is_even, low_half):
    first = even_ref[index]
    second = odd_ref[index]
    above = jnp.where(is_even, first, second)
    below = jnp.where(is_even, second, first)
    return (
        jnp.where(low_half, above, pltpu.roll(below, 4, 0)),
        jnp.where(low_half, pltpu.roll(above, 4, 0), below),
    )


def join_planes(load, out_ref, left_ref, right_ref, depth, width):
    part = width // 2
    for z in range(depth):
        for c in range(4):
            ref = right_ref if c & 1 else left_ref
            ref[pl.ds(z * width + (c >> 1), part, stride=2), :] = load(z, c)
    rows = depth * width
    both = jnp.concatenate([left_ref[pl.ds(0, rows), :], right_ref[pl.ds(0, rows), :]], axis=1)
    out_ref[...] = mm(both, merging_matrix()).reshape(depth, width, 2 * LANES)


def hessian_parts(below, here, above):
    rise = [a - b for a, b in zip(above, below)]
    y_sum, y_rise, yz_rise = [], [], []
    for c in range(4):
        odd = c >> 1
        same, other = here[c ^ 2], y_other(here[c ^ 2], odd)
        y_sum.append(same + other)
        y_rise.append(other - same if odd else same - other)
        same, other = rise[c ^ 2], y_other(rise[c ^ 2], odd)
        yz_rise.append(other - same if odd else same - other)
    out = []
    for c in range(4):
        odd = c & 1
        same, other = here[c ^ 1], x_other(here[c ^ 1], odd)
        twice = 2.0 * here[c]
        pxx = same + other - twice
        pyy = y_sum[c] - twice
        pzz = below[c] + above[c] - twice
        same, other = rise[c ^ 1], x_other(rise[c ^ 1], odd)
        pxz = other - same if odd else same - other
        same, other = y_rise[c ^ 1], x_other(y_rise[c ^ 1], odd)
        pxy = other - same if odd else same - other
        cross = pxy * pxy + pxz * pxz + yz_rise[c] * yz_rise[c]
        out.append(pxx * pyy + (pxx + pyy) * pzz - 0.0625 * cross)
    return out


def face_part(face, c, z, planes):
    lane = lane_iota(face.shape)
    if c & 1:
        turned = pltpu.roll(face, LANES - 1 - planes - z, 1)
        return jnp.where(lane == LANES - 1, turned, 0.0)
    turned = pltpu.roll(face, (LANES - z) & (LANES - 1), 1)
    return jnp.where(lane == 0, turned, 0.0)


def fill_block(p_ref, at, ref, edge_refs, tile, pencil, depth, part):
    is_even = (pencil % 2) == 0
    low_half = row_iota((8, LANES)) < 4
    for z in range(depth):
        for c in range(4):
            p_ref[at + z, c, pl.ds(0, part), :] = block_rows(ref, (4 * z + c) * part, part)
        for t in range(2):
            first, second = halo_tiles(*edge_refs, tile + 2 * z + t, is_even, low_half)
            p_ref[at + z, 2 * t, pl.ds(part, 8), :] = first
            p_ref[at + z, 2 * t + 1, pl.ds(part, 8), :] = second


def near_half_kernel(scalar_ref, *refs, depth, width, pencils):
    near = [k for k in range(EARLY) if OFFSETS[k] < 4]
    blocks = refs[: len(near)]
    even_ref, odd_ref, faces_ref, p_ref, s_ref, q_ref = refs[len(near) :]
    slab = scalar_ref[0]
    pencil = scalar_ref[1]
    part = width // 2
    half = 4 * depth
    first_plane = (slab // 4) * half
    mask = halo_mask(pencil, pencils)
    blank = jnp.zeros(p_ref.shape[1:], jnp.float32)
    p_ref[0] = blank
    p_ref[half + 1] = blank
    for k, ref in zip(near, blocks):
        at = ((slab ^ OFFSETS[k]) % 4) * depth + 1
        fill_block(p_ref, at, ref, (even_ref, odd_ref), 2 * depth * k, pencil, depth, part)

    def body(j, carry):
        source = hessian_parts(parts(p_ref, j), parts(p_ref, j + 1), parts(p_ref, j + 2))
        for c in range(4):
            s_ref[j, c] = source[c][:part]
            face = faces_ref[pl.ds((c >> 1) * part, part), :]
            face = face_part(face, c, first_plane + j, 2 * half)
            q_ref[j, c, pl.ds(0, part), :] = W * (face - source[c][:part])
            q_ref[j, c, pl.ds(part, 8), :] = (-W * mask) * source[c][part:]
        return carry

    lax.fori_loop(0, half, body, 0, unroll=HESS)


def far_half_kernel(scalar_ref, *refs, depth, width, pencils):
    far = [k for k in range(len(OFFSETS)) if OFFSETS[k] >= 4]
    blocks = refs[: len(far)]
    early_refs = refs[len(far) : len(far) + 2]
    late_refs = refs[len(far) + 2 : len(far) + 4]
    faces_ref, pn_ref, sn_ref, qn_ref = refs[len(far) + 4 : len(far) + 8]
    source_hbm, q_ref, swept_ref, coarse_ref = refs[len(far) + 8 : len(far) + 12]
    p_ref, f_ref, s_ref, u_ref, left_ref, right_ref, source_ref, sem = refs[len(far) + 12 :]
    slab = scalar_ref[0]
    pencil = scalar_ref[1]
    part = width // 2
    half = 4 * depth
    planes = 2 * half
    lower = slab < 4
    near_first = jnp.where(lower, 0, half)
    far_first = half - near_first
    is_even = (pencil % 2) == 0
    low_half = row_iota((8, LANES)) < 4
    mask = halo_mask(pencil, pencils)
    blank = jnp.zeros(p_ref.shape[1:], jnp.float32)
    for ref in (q_ref, u_ref):
        for z in (1, planes + 2):
            ref[z] = blank
    p_ref[jnp.where(lower, half + 1, 0)] = blank
    p_ref[jnp.where(lower, 0, half + 1)] = pn_ref[jnp.where(lower, half, 1)]
    for k, ref in zip(far, blocks):
        at = ((slab ^ OFFSETS[k]) % 4) * depth + 1
        early = k < EARLY
        tile = 2 * depth * (k if early else k - EARLY)
        edge_refs = early_refs if early else late_refs
        fill_block(p_ref, at, ref, edge_refs, tile, pencil, depth, part)
    face_tile = 2 * depth * (len(OFFSETS) - EARLY)
    first, second = halo_tiles(*late_refs, face_tile, is_even, low_half)
    f_ref[0, pl.ds(0, part), :] = faces_ref[pl.ds(0, part), :]
    f_ref[0, pl.ds(part, 8), :] = first
    f_ref[1, pl.ds(0, part), :] = faces_ref[pl.ds(part, part), :]
    f_ref[1, pl.ds(part, 8), :] = second

    def finish(source, z):
        for c in range(4):
            face = face_part(f_ref[c >> 1], c, z, planes)
            put(q_ref, z + 2, c, W * (face - source[c]), mask)

    def copy(j, carry):
        z = near_first + j
        for c in range(4):
            face = face_part(f_ref[c >> 1, pl.ds(part, 8), :], c, z, planes)
            q_ref[z + 2, c, pl.ds(0, part), :] = qn_ref[j, c, pl.ds(0, part), :]
            q_ref[z + 2, c, pl.ds(part, 8), :] = (
                qn_ref[j, c, pl.ds(part, 8), :] + (W * mask) * face
            )
        return carry

    lax.fori_loop(0, half, copy, 0, unroll=UNROLL)

    def body(j, carry):
        source = hessian_parts(parts(p_ref, j), parts(p_ref, j + 1), parts(p_ref, j + 2))
        finish(source, far_first + j)
        return carry

    lax.fori_loop(0, half, body, 0, unroll=HESS)
    seam = jnp.where(lower, half, 1)
    here = parts(pn_ref, seam)
    inner = parts(pn_ref, jnp.where(lower, half - 1, 2))
    outer = parts(p_ref, jnp.where(lower, 1, half))
    below = [jnp.where(lower, a, b) for a, b in zip(inner, outer)]
    above = [jnp.where(lower, b, a) for a, b in zip(inner, outer)]
    source = hessian_parts(below, here, above)
    finish(source, near_first + seam - 1)
    own = (slab % 4) * depth
    for z in range(depth):
        is_seam = own + z == seam - 1
        for c in range(4):
            s_ref[z, c] = jnp.where(is_seam, source[c][:part], sn_ref[own + z, c])
    join_planes(lambda z, c: s_ref[z, c], source_ref, left_ref, right_ref, depth, width)
    copy_out = pltpu.make_async_copy(source_ref, source_hbm, sem)
    copy_out.start()

    def second_sweep(z, carry):
        here = parts(q_ref, z + 2)
        for c in range(4):
            sides = neighbours(q_ref[z + 1, c], here, q_ref[z + 3, c], c)
            put(u_ref, z + 2, c, (1.0 + KEEP) * here[c] + W * sides, mask)
        return carry

    lax.fori_loop(0, planes, second_sweep, 0, unroll=UNROLL)
    restrict_window(u_ref, q_ref, coarse_ref, swept_ref, mask, planes, part)
    copy_out.wait()


def restrict_window(u_ref, q_ref, coarse_ref, swept_ref, mask, planes, part):
    def restrict(z, carry):
        total = None
        for at in (2 * z + 2, 2 * z + 3):
            here = parts(u_ref, at)
            for c in range(4):
                new = swept(u_ref[at - 1, c], here, u_ref[at + 1, c], q_ref[at, c], c)
                put(swept_ref, at, c, new, mask)
                change = new[:part] - here[c][:part]
                total = change if total is None else total + change
        coarse_ref[pl.ds(pl.multiple_of(z * part, part), part), :] = 0.5 * total
        return carry

    lax.fori_loop(0, planes // 2, restrict, 0, unroll=PAIRS)


def coarse_window(v_ref, z, pencil, part):
    start = pl.multiple_of(pencil * part, part)
    own = v_ref[z, pl.ds(start + HALO, part), :]
    above = v_ref[z, pl.ds(start + HALO + part, 8), :]
    below = v_ref[z, pl.ds(start, 8), :]
    tile = jnp.where(row_iota((8, LANES)) < 4, above, below)
    return jnp.concatenate([own, tile], axis=0)


def middle_kernel(
    scalar_ref, gathered_ref, q_ref, swept_ref, qwin_ref, win_ref, coarse_ref,
    v_ref, q1_ref, a1_ref, b1_ref, tmp_ref, a_ref, b_ref, *, depth, width, pencils, shape
):
    slab = scalar_ref[0]
    pencil = scalar_ref[1]
    planes = a_ref.shape[0] - 4
    part = width // 2
    mask = halo_mask(pencil, pencils)
    solve_level_one(gathered_ref, v_ref, q1_ref, a1_ref, b1_ref, tmp_ref, shape)
    blank = jnp.zeros(a_ref.shape[1:], jnp.float32)
    for ref in (a_ref, b_ref):
        for z in (1, planes + 2):
            ref[z] = blank

    def third_sweep(z, carry):
        v = [coarse_window(v_ref, z + k, pencil, part) for k in range(3)]
        for k, children in enumerate(swept_children(*v)):
            at = 2 * z + 2 + k
            for c in range(4):
                put(a_ref, at, c, swept_ref[at, c] + children[c], mask)
        return carry

    lax.fori_loop(0, planes // 2, third_sweep, 0, unroll=PAIRS)

    def sweep(src, dst):
        def body(z, carry):
            here = parts(src, z + 2)
            for c in range(4):
                new = swept(src[z + 1, c], here, src[z + 3, c], q_ref[z + 2, c], c)
                put(dst, z + 2, c, new, mask)
            return carry

        lax.fori_loop(0, planes, body, 0, unroll=UNROLL)

    sweep(a_ref, b_ref)
    sweep(b_ref, a_ref)
    sweep(a_ref, b_ref)
    restrict_window(b_ref, q_ref, coarse_ref, a_ref, mask, planes, part)
    for z in range(depth):
        qwin_ref[z] = q_ref[slab * depth + z + 2]
    for z in range(depth + 2):
        win_ref[z] = a_ref[slab * depth + z + 1]


def last_kernel(
    scalar_ref, gathered_ref, qwin_ref, win_ref, out_hbm,
    v_ref, q1_ref, a1_ref, b1_ref, tmp_ref, a_ref, left_ref, right_ref, out_ref, sems,
    *, depth, width, pencils, shape
):
    slab = scalar_ref[0]
    pencil = scalar_ref[1]
    planes = shape[0] * 2
    part = width // 2
    mask = halo_mask(pencil, pencils)
    solve_level_one(gathered_ref, v_ref, q1_ref, a1_ref, b1_ref, tmp_ref, shape, slab)
    blank = jnp.zeros((part + 8, LANES), jnp.float32)
    v = [coarse_window(v_ref, slab * (depth // 2) + k, pencil, part) for k in range(4)]
    v = [blank] + v + [blank]
    for k in range(4):
        for side, children in enumerate(swept_children(*v[k : k + 3])):
            z = 2 * k + side - 1
            if 0 <= z < depth + 2:
                at = slab * depth - 1 + z
                live = jnp.where((at >= 0) & (at < planes), 1.0, 0.0)
                for c in range(4):
                    put(a_ref, z, c, live * (win_ref[z, c] + children[c]), mask)
    matrix = merging_matrix()
    copies = []
    for z in range(depth):
        here = parts(a_ref, z + 1)
        for c in range(4):
            new = swept(a_ref[z, c], here, a_ref[z + 2, c], qwin_ref[z, c], c)
            ref = right_ref if c & 1 else left_ref
            ref[z, pl.ds(c >> 1, part, stride=2), :] = new[:part]
        out_ref[z] = mm(jnp.concatenate([left_ref[z], right_ref[z]], axis=1), matrix)
        copies.append(pltpu.make_async_copy(out_ref.at[z], out_hbm.at[z], sems.at[z]))
        copies[-1].start()
    for copy in copies:
        copy.wait()


def vmem():
    return pl.BlockSpec(memory_space=pltpu.VMEM)


def smem():
    return pl.BlockSpec(memory_space=pltpu.SMEM)


def arr(*shape):
    return jax.ShapeDtypeStruct(shape, jnp.float32)


def buf(*shape):
    return pltpu.VMEM(shape, jnp.float32)


def call(kernel, name, scalars, args, outs, scratch=(), space=pltpu.VMEM, out_space=None):
    out_specs = jax.tree.map(lambda _: vmem(), outs)
    if out_space is not None:
        out_specs = tuple(pl.BlockSpec(memory_space=one) for one in out_space)
    return pl.pallas_call(
        kernel,
        out_shape=outs,
        in_specs=[smem()] * len(scalars) + [pl.BlockSpec(memory_space=space)] * len(args),
        out_specs=out_specs,
        scratch_shapes=list(scratch),
        compiler_params=pltpu.CompilerParams(vmem_limit_bytes=16 << 20),
        name=name,
    )(*scalars, *args)


def windowed(potential, parent_store, face_owner, face_offset):
    depth, width, columns = potential.shape
    slabs = lax.axis_size("slab")
    pencils = lax.axis_size("pencil")
    planes, height = slabs * depth, pencils * width
    part = width // 2
    rows = part + 8
    where = jnp.stack([lax.axis_index("slab"), lax.axis_index("pencil")]).astype(jnp.int32)
    scalars = jnp.concatenate([where, face_owner, face_offset])
    own = call(
        pack_kernel,
        "pack",
        [],
        [pltpu.with_memory_space_constraint(x, pltpu.HBM) for x in (potential, parent_store)],
        arr(depth * width * 2 + 8, LANES),
        [
            buf(depth * width, LANES),
            buf(depth * width, LANES),
            buf(*potential.shape),
            buf(*parent_store.shape),
            pltpu.SemaphoreType.DMA((2,)),
        ],
        space=pltpu.HBM,
    )

    def swap(x, bits):
        return lax.ppermute(x, "slab", [(i, i ^ bits) for i in range(slabs)])

    near = [swap(own, bits) for bits in OFFSETS[1:5]]
    blocks = [own, *near] + [swap(near[0], bits) for bits in OFFSETS[2:5]]
    low_pairs = [(i, i + 1) for i in range(0, pencils - 1, 2)]
    high_pairs = [(i, i + 1) for i in range(1, pencils - 1, 2)]

    def beside(even, odd):
        return (
            lax.ppermute(even, "pencil", low_pairs + [(j, i) for i, j in low_pairs]),
            lax.ppermute(odd, "pencil", high_pairs + [(j, i) for i, j in high_pairs]),
        )

    message = arr(2 * depth * EARLY, 8, LANES)
    early = call(
        partial(early_edges_kernel, depth=depth, width=width),
        "early_edges",
        [scalars],
        blocks[:EARLY],
        (message, message),
    )
    early = beside(*early)
    message = arr(2 * depth * (slabs - EARLY) + 1, 8, LANES)
    even, odd, faces = call(
        partial(late_edges_kernel, depth=depth, width=width),
        "late_edges",
        [scalars],
        blocks,
        (message, message, arr(width, LANES)),
        [buf(slabs, 8, LANES), buf(LANES, LANES)],
    )
    late = beside(even, odd)
    shape = (planes // 2, height // 2, columns // 2)
    coarse_part = arr(planes // 2 * part, LANES)
    field = (planes + 4, 4, rows, LANES)
    half = planes // 2
    near = call(
        partial(near_half_kernel, depth=depth, width=width, pencils=pencils),
        "near_half",
        [scalars],
        [b for b, offset in zip(blocks, OFFSETS) if offset < 4] + [*early, faces],
        (arr(half + 2, 4, rows, LANES), arr(half, 4, part, LANES), arr(half, 4, rows, LANES)),
    )
    source, q, swept_once, coarse = call(
        partial(far_half_kernel, depth=depth, width=width, pencils=pencils),
        "far_half",
        [scalars],
        [b for b, offset in zip(blocks, OFFSETS) if offset >= 4] + [*early, *late, faces, *near],
        (arr(depth, width, columns), arr(*field), arr(*field), coarse_part),
        [
            buf(half + 2, 4, rows, LANES),
            buf(2, rows, LANES),
            buf(depth, 4, part, LANES),
            buf(*field),
            buf(depth * width, LANES),
            buf(depth * width, LANES),
            buf(depth, width, columns),
            pltpu.SemaphoreType.DMA,
        ],
        out_space=[pl.ANY] + [pltpu.VMEM] * 3,
    )
    level = (shape[0] + 4, 2, shape[1] // 2, LANES)
    level_scratch = [
        buf(shape[0] + 2, shape[1] + 2 * HALO, LANES),
        buf(*level),
        buf(*level),
        buf(*level),
        buf((shape[0] // 2 + 4) * shape[1] // 2, LANES),
    ]

    def gather(x):
        return lax.all_gather(x, "pencil", axis=0, tiled=False)

    sizes = dict(depth=depth, width=width, pencils=pencils, shape=shape)
    qwin, win, coarse = call(
        partial(middle_kernel, **sizes),
        "middle",
        [scalars],
        [gather(coarse), q, swept_once],
        (arr(depth, 4, rows, LANES), arr(depth + 2, 4, rows, LANES), coarse_part),
        level_scratch + [buf(*field), buf(*field)],
    )
    (solved,) = call(
        partial(last_kernel, **sizes),
        "last",
        [scalars],
        [gather(coarse), qwin, win],
        (arr(depth, width, columns),),
        level_scratch
        + [
            buf(depth + 2, 4, rows, LANES),
            buf(depth, width, LANES),
            buf(depth, width, LANES),
            buf(depth, width, columns),
            pltpu.SemaphoreType.DMA((depth,)),
        ],
        out_space=[pl.ANY],
    )
    return solved, source


def fits_window(potential, parent_store):
    depth, width, columns = potential.shape
    slabs = lax.axis_size("slab")
    pencils = lax.axis_size("pencil")
    planes = slabs * depth
    return (
        slabs == 8
        and pencils % 2 == 0
        and depth == 4
        and columns == 2 * LANES
        and width == 32
        and parent_store.shape[0] * width == LANES
        and 2 * planes < LANES
        and pencils in (2, 4, 8)
    )


def padded(cells, sides, width):
    for axis, dim in sides:
        count = lax.axis_size(axis)
        ends = count - 1
        head = lax.slice_in_dim(cells, 0, width, axis=dim)
        tail = lax.slice_in_dim(cells, cells.shape[dim] - width, cells.shape[dim], axis=dim)
        cells = jnp.concatenate(
            [
                lax.ppermute(tail, axis, [(i, (i + 1) % count) for i in range(ends)]),
                cells,
                lax.ppermute(head, axis, [((i + 1) % count, i) for i in range(ends)]),
            ],
            axis=dim,
        )
    return cells


def hessian_source(p):
    c = p[1:-1, 1:-1, 1:-1]
    pxx = p[1:-1, 1:-1, 2:] + p[1:-1, 1:-1, :-2] - 2.0 * c
    pyy = p[1:-1, 2:, 1:-1] + p[1:-1, :-2, 1:-1] - 2.0 * c
    pzz = p[2:, 1:-1, 1:-1] + p[:-2, 1:-1, 1:-1] - 2.0 * c
    pxy = 0.25 * (p[1:-1, 2:, 2:] - p[1:-1, :-2, 2:] - p[1:-1, 2:, :-2] + p[1:-1, :-2, :-2])
    pxz = 0.25 * (p[2:, 1:-1, 2:] - p[:-2, 1:-1, 2:] - p[2:, 1:-1, :-2] + p[:-2, 1:-1, :-2])
    pyz = 0.25 * (p[2:, 2:, 1:-1] - p[:-2, 2:, 1:-1] - p[2:, :-2, 1:-1] + p[:-2, :-2, 1:-1])
    return pxx * pyy + pxx * pzz + pyy * pzz - pxy * pxy - pxz * pxz - pyz * pyz


def apply_padded(p, level):
    c = p[1:-1, 1:-1, 1:-1]
    near = p[2:, 1:-1, 1:-1] + p[:-2, 1:-1, 1:-1]
    near = near + p[1:-1, 2:, 1:-1] + p[1:-1, :-2, 1:-1]
    near = near + p[1:-1, 1:-1, 2:] + p[1:-1, 1:-1, :-2]
    return (6.0 * c - near) * 0.25**level


def step_weight(level):
    return OMEGA / 6.0 * 4.0**level


def sweep_whole(u, rhs, level):
    return u + step_weight(level) * (rhs - apply_padded(jnp.pad(u, 1), level))


def restrict(r):
    a, b, c = r.shape
    return r.reshape(a // 2, 2, b // 2, 2, c // 2, 2).mean(axis=(1, 3, 5))


def prolong(e):
    a, b, c = e.shape
    return jnp.broadcast_to(e[:, None, :, None, :, None], (a, 2, b, 2, c, 2)).reshape(
        2 * a, 2 * b, 2 * c
    )


def vcycle(u, rhs, level):
    if is_coarsest(rhs.shape):
        for sweep_count in range(8):
            u = sweep_whole(u, rhs, level)
        return u
    u = sweep_whole(u, rhs, level)
    u = sweep_whole(u, rhs, level)
    resid = rhs - apply_padded(jnp.pad(u, 1), level)
    coarse = restrict(resid)
    correction = vcycle(jnp.zeros_like(coarse), coarse, level + 1)
    u = u + prolong(correction)
    u = sweep_whole(u, rhs, level)
    u = sweep_whole(u, rhs, level)
    return u


def widen_x(p):
    return jnp.pad(p, ((0, 0), (0, 0), (1, 1)))


def rim_one(u):
    return widen_x(padded(u, (("slab", 0), ("pencil", 1)), 1))


def coarse_solve(rhs, level):
    width = rhs.shape[1]
    columns = rhs.shape[2]
    whole = lax.all_gather(rhs, ("slab", "pencil"), axis=0, tiled=True)
    whole = whole.reshape(lax.axis_size("slab"), lax.axis_size("pencil") * width, columns)
    solved = vcycle(jnp.zeros_like(whole), whole, level)
    start_y = lax.axis_index("pencil") * width
    return lax.dynamic_slice(
        solved, (lax.axis_index("slab"), start_y, jnp.int32(0)), (1, width, columns)
    )


def split_vcycle(u, rhs, level, from_zero):
    if rhs.shape[0] == 1:
        return coarse_solve(rhs, level)
    weight = step_weight(level)
    if from_zero:
        u = weight * rhs
    else:
        u = u + weight * (rhs - apply_padded(rim_one(u), level))
    u = u + weight * (rhs - apply_padded(rim_one(u), level))
    resid = rhs - apply_padded(rim_one(u), level)
    correction = split_vcycle(None, restrict(resid), level + 1, True)
    u = u + prolong(correction)
    u = u + weight * (rhs - apply_padded(rim_one(u), level))
    u = u + weight * (rhs - apply_padded(rim_one(u), level))
    return u


def plain(potential, parent_store, face_owner, face_offset):
    depth, width, columns = potential.shape
    grown = widen_x(padded(potential, (("slab", 0), ("pencil", 1)), 1))
    source = hessian_source(grown)
    slab_index = lax.axis_index("slab")
    wanted = face_owner[slab_index] * parent_store.shape[0] + face_offset[slab_index]
    piece = lax.all_gather(parent_store, "slab", axis=0, tiled=True)
    labels = jnp.arange(piece.shape[0], dtype=jnp.int32)
    match = labels == wanted
    faces = jnp.sum(jnp.where(match[:, None, None, None], piece, 0.0), axis=0)
    rhs = -source
    rhs = rhs.at[:, :, 0].add(faces[0])
    rhs = rhs.at[:, :, columns - 1].add(faces[1])
    solved = jnp.zeros_like(rhs)
    for cycle in range(CYCLES):
        solved = split_vcycle(solved, rhs, 0, cycle == 0)
    return (solved, source)


def on_device(potential, parent_store, face_owner, face_offset):
    if fits_window(potential, parent_store):
        return windowed(potential, parent_store, face_owner, face_offset)
    return plain(potential, parent_store, face_owner, face_offset)


def solution(mesh):
    in_specs = (P("slab", "pencil", None), P("slab", None, None, "pencil"), P(), P())
    out_specs = (P("slab", "pencil", None), P("slab", "pencil", None))
    return jax.shard_map(
        on_device, mesh=mesh, in_specs=in_specs, out_specs=out_specs, check_vma=False
    )
```

```python
from functools import partial

import jax
import jax.numpy as jnp
import numpy as np
from jax import lax
from jax.experimental import pallas as pl
from jax.experimental.pallas import tpu as pltpu
from jax.sharding import PartitionSpec as P

CYCLES = 2
OMEGA = 0.8
W = float(np.float32(OMEGA / 6.0))
KEEP = 1.0 - 6.0 * W
HALO = 8
LANES = 128
UNROLL = 16
PAIRS = 8
HESS = 8
LEVEL = 16
LPAIRS = 4


def is_coarsest(shape):
    return min(shape) <= 4 or any((d % 2 for d in shape))


def lane_iota(shape):
    return lax.broadcasted_iota(jnp.int32, shape, len(shape) - 1)


def row_iota(shape):
    return lax.broadcasted_iota(jnp.int32, shape, len(shape) - 2)


def x_other(values, odd):
    lane = lane_iota(values.shape)
    if odd:
        return jnp.where(lane == LANES - 1, 0.0, pltpu.roll(values, LANES - 1, 1))
    return jnp.where(lane == 0, 0.0, pltpu.roll(values, 1, 1))


def y_other(values, odd):
    return pltpu.roll(values, values.shape[0] - 1 if odd else 1, 0)


def neighbours(below, here, above, c):
    across, along = here[c ^ 1], here[c ^ 2]
    near = (below + above) + (across + x_other(across, c & 1))
    return near + (along + y_other(along, c >> 1))


def swept(below, here, above, q, c):
    return KEEP * here[c] + W * neighbours(below, here, above, c) + q


def swept_children(below, here, above):
    here = W * here
    base = ((1.0 - 3.0 * W) / W) * here
    beyond = [W * below, W * above]
    across = [base + x_other(here, odd) for odd in range(2)]
    along = [y_other(here, odd) for odd in range(2)]
    flat = [across[c & 1] + along[c >> 1] for c in range(4)]
    return [[one + beyond[k] for one in flat] for k in range(2)]


def parts(ref, z):
    return [ref[z, c] for c in range(4)]


def halo_mask(pencil, pencils):
    row = row_iota((8, LANES))
    above = jnp.where(pencil < pencils - 1, 1.0, 0.0)
    below = jnp.where(pencil > 0, 1.0, 0.0)
    return jnp.where(row < 4, above, below)


def put(ref, z, c, values, mask):
    own = values.shape[0] - 8
    ref[z, c, pl.ds(0, own), :] = values[:own]
    ref[z, c, pl.ds(own, 8), :] = values[own:] * mask


def index_pair(rows, columns):
    return (
        lax.broadcasted_iota(jnp.int32, (rows, columns), 0),
        lax.broadcasted_iota(jnp.int32, (rows, columns), 1),
    )


def chosen(where, value):
    return jnp.where(where, value, 0.0).astype(jnp.bfloat16)


def splitting_matrix():
    i, j = index_pair(2 * LANES, 2 * LANES)
    return chosen(i == 2 * (j & (LANES - 1)) + (j >= LANES).astype(jnp.int32), 1.0)


def merging_matrix():
    i, j = index_pair(2 * LANES, 2 * LANES)
    return chosen(j == 2 * (i & (LANES - 1)) + (i >= LANES).astype(jnp.int32), 1.0)


def mm(a, b):
    high = a.astype(jnp.bfloat16)
    rest = a - high.astype(jnp.float32)
    middle = rest.astype(jnp.bfloat16)
    low = (rest - middle.astype(jnp.float32)).astype(jnp.bfloat16)

    def dot(x):
        return jnp.dot(x, b, preferred_element_type=jnp.float32)

    return dot(high) + (dot(middle) + dot(low))


def pair_sum(values, distance, axis):
    size = values.shape[axis]
    at = lax.broadcasted_iota(jnp.int32, values.shape, axis)
    ahead = pltpu.roll(values, size - distance, axis)
    behind = pltpu.roll(values, distance, axis)
    return values + jnp.where((at & distance) == 0, ahead, behind)


def x_sides(values, distance):
    lane = lane_iota(values.shape)
    left = jnp.where(lane < distance, 0.0, pltpu.roll(values, distance, 1))
    right = jnp.where(lane >= LANES - distance, 0.0, pltpu.roll(values, LANES - distance, 1))
    return left + right


def flat_sweep(u, q, rows, yd, xd):
    total = u.shape[0]
    zero = jnp.zeros((rows, LANES), jnp.float32)
    below = jnp.concatenate([zero, u[: total - rows]], axis=0)
    above = jnp.concatenate([u[rows:], zero], axis=0)
    y = row_iota(u.shape) & (rows - 1)
    down = jnp.where(y < yd, 0.0, pltpu.roll(u, yd, 0))
    up = jnp.where(y >= rows - yd, 0.0, pltpu.roll(u, total - yd, 0))
    return KEEP * u + W * ((below + above) + (down + up) + x_sides(u, xd)) + q


def flat_vcycle(q, shape, rows, yd, xd):
    if is_coarsest(shape):
        u = q
        for _ in range(7):
            u = flat_sweep(u, q, rows, yd, xd)
        return u
    zs, ys, xs = shape
    u = flat_sweep(q, q, rows, yd, xd)
    change = flat_sweep(u, q, rows, yd, xd) - u
    pairs = [
        change[2 * z * rows : (2 * z + 1) * rows] + change[(2 * z + 1) * rows : (2 * z + 2) * rows]
        for z in range(zs // 2)
    ]
    coarse = 0.5 * pair_sum(pair_sum(jnp.concatenate(pairs, axis=0), yd, 0), xd, 1)
    e = flat_vcycle(coarse, (zs // 2, ys // 2, xs // 2), rows, 2 * yd, 2 * xd)
    planes = []
    for z in range(zs // 2):
        planes += [e[z * rows : (z + 1) * rows]] * 2
    u = u + jnp.concatenate(planes, axis=0)
    u = flat_sweep(u, q, rows, yd, xd)
    return flat_sweep(u, q, rows, yd, xd)


def solve_level_one(piece_refs, pencil, v_ref, q_ref, a_ref, b_ref, tmp_ref, shape, near=None):
    zs, ys, xs = shape
    rows = ys // 2
    half = zs // 2
    piece = rows // len(piece_refs)
    row = row_iota((rows, LANES))
    blank = jnp.zeros((rows, LANES), jnp.float32)
    for ref in (q_ref, a_ref, b_ref):
        for z in (0, 1, zs + 2, zs + 3):
            for c in range(2):
                ref[z, c] = blank
    for z in (0, 1, half + 2, half + 3):
        tmp_ref[pl.ds(z * rows, rows), :] = blank
    edge = jnp.zeros((HALO, LANES), jnp.float32)
    for z in range(zs + 2):
        v_ref[z, pl.ds(0, HALO), :] = edge
        v_ref[z, pl.ds(HALO + ys, HALO), :] = edge
    if near is None:
        for z in (0, zs + 1):
            for c in range(2):
                v_ref[z, pl.ds(HALO + c * rows, rows), :] = blank
    for z in range(zs):
        for c in range(2):
            for k, ref in enumerate(piece_refs):
                spot = pl.ds(2 * piece * z + c, piece, stride=2)
                to = pl.ds(pl.multiple_of((pencil ^ k) * piece, piece), piece)
                q_ref[z + 2, c, to, :] = ref[spot, :]

    def y_beyond(other, c):
        if c:
            return jnp.where(row == rows - 1, 0.0, pltpu.roll(other, rows - 1, 0))
        return jnp.where(row == 0, 0.0, pltpu.roll(other, 1, 0))

    def around(src, z):
        here = [src[z, 0], src[z, 1]]
        near = []
        for c in range(2):
            other = here[1 - c]
            sides = (other + y_beyond(other, c)) + x_sides(here[c], 1)
            near.append((src[z - 1, c] + src[z + 1, c]) + sides)
        return here, near

    def second(z, carry):
        here, sides = around(q_ref, z)
        for c in range(2):
            a_ref[z, c] = (1.0 + KEEP) * here[c] + W * sides[c]
        return carry

    lax.fori_loop(2, zs + 2, second, 0, unroll=LEVEL)

    def restrict(z, carry):
        total = None
        for at in (2 * z + 2, 2 * z + 3):
            here, sides = around(a_ref, at)
            for c in range(2):
                new = KEEP * here[c] + W * sides[c] + q_ref[at, c]
                b_ref[at, c] = new
                change = new - here[c]
                total = change if total is None else total + change
        spot = pl.ds(pl.multiple_of((z + 2) * rows, rows), rows)
        tmp_ref[spot, :] = 0.5 * pair_sum(total, 1, 1)
        return carry

    pairs_unroll = LPAIRS if near is None else half
    lax.fori_loop(0, half, restrict, 0, unroll=pairs_unroll)
    inner = pl.ds(2 * rows, half * rows)
    tmp_ref[inner, :] = flat_vcycle(tmp_ref[inner, :], (half, ys // 2, xs // 2), rows, 1, 2)

    def live(at, count):
        return jnp.where((at >= 0) & (at < count), 1.0, 0.0)

    def third(z):
        e = [tmp_ref[pl.ds(pl.multiple_of((z + k) * rows, rows), rows), :] for k in (1, 2, 3)]
        here = W * e[1]
        base = ((1.0 - 4.0 * W) / W) * here + x_sides(here, 1)
        for c in range(2):
            flat = base + y_beyond(here, c)
            for k in range(2):
                new = b_ref[2 * z + 2 + k, c] + (flat + W * e[2 * k])
                a_ref[2 * z + 2 + k, c] = new if near is None else live(z, half) * new

    def fourth(z):
        here, sides = around(a_ref, z + 2)
        for c in range(2):
            new = KEEP * here[c] + W * sides[c] + q_ref[z + 2, c]
            if near is not None:
                new = live(z, zs) * new
            v_ref[z + 1, pl.ds(HALO + c, rows, stride=2), :] = new

    def loop(step, start, count, unroll):
        def body(i, carry):
            step(start + i)
            return carry

        lax.fori_loop(0, count, body, 0, unroll=unroll)

    if near is None:
        loop(third, 0, half, LPAIRS)
        loop(fourth, 0, zs, LEVEL)
    else:
        loop(third, near - 1, 3, 3)
        loop(fourth, 2 * near - 1, 4, 4)


def pack_kernel(
    potential_hbm, store_hbm, out_ref, even_ref, odd_ref, potential_ref, store_ref, sems
):
    copies = [
        pltpu.make_async_copy(potential_hbm, potential_ref, sems.at[0]),
        pltpu.make_async_copy(store_hbm, store_ref, sems.at[1]),
    ]
    for copy in copies:
        copy.start()
    matrix = splitting_matrix()
    for copy in copies:
        copy.wait()
    depth, width, columns = potential_ref.shape
    slots = store_ref.shape[0]
    part = width // 2
    split = mm(potential_ref[...].reshape(depth * width, columns), matrix)
    even_ref[...] = split[:, :LANES]
    odd_ref[...] = split[:, LANES:]
    for z in range(depth):
        for c in range(4):
            ref = odd_ref if c & 1 else even_ref
            spot = pl.ds((4 * z + c) * part, part)
            out_ref[spot, :] = ref[pl.ds(z * width + (c >> 1), part, stride=2), :]
    base = depth * width * 2
    for slot in range(slots):
        for side in range(2):
            spot = pl.ds(base + side * depth, depth)
            out_ref[spot, pl.ds(slot * width, width)] = store_ref[slot, side]


OFFSETS = (0, 4, 3, 1, 2, 7, 5, 6)
EARLY = 5


def block_rows(ref, start, count):
    return ref[pl.ds(start, count), :]


def ends(load, first, second, part, low_half):
    head = jnp.where(low_half, load(first, 8), pltpu.roll(load(second, 8), 4, 0))
    tail = jnp.where(
        low_half, pltpu.roll(load(first + part - 8, 8), 4, 0), load(second + part - 8, 8)
    )
    return head, tail


def store_ends(ref, pencil, out_refs, at, depth, part):
    even_ref, odd_ref = out_refs
    is_even = (pencil % 2) == 0
    low_half = row_iota((8, LANES)) < 4
    for z in range(depth):
        for t in range(2):
            head, tail = ends(
                partial(block_rows, ref),
                (4 * z + 2 * t) * part, (4 * z + 2 * t + 1) * part, part, low_half,
            )
            even_ref[at + 2 * z + t] = jnp.where(is_even, tail, head)
            odd_ref[at + 2 * z + t] = jnp.where(is_even, head, tail)


def early_edges_kernel(scalar_ref, *refs, depth, width):
    blocks, out_refs = refs[:EARLY], refs[EARLY:]
    for k, ref in enumerate(blocks):
        store_ends(ref, scalar_ref[1], out_refs, 2 * depth * k, depth, width // 2)


def late_edges_kernel(scalar_ref, *refs, depth, width):
    slabs = len(OFFSETS)
    even_ref, odd_ref, faces_ref, store_ref, rows_ref = refs[slabs:]
    slab = scalar_ref[0]
    pencil = scalar_ref[1]
    planes = slabs * depth
    part = width // 2
    is_even = (pencil % 2) == 0
    low_half = row_iota((8, LANES)) < 4
    base = depth * width * 2
    late = refs[EARLY:slabs]
    for k, ref in enumerate(late):
        store_ends(ref, pencil, (even_ref, odd_ref), 2 * depth * k, depth, part)
    for offset, ref in zip(OFFSETS, refs):
        store_ref[slab ^ offset] = block_rows(ref, base, 8)
    rest = LANES - 2 * planes
    rows_ref[pl.ds(2 * planes, rest), :] = jnp.zeros((rest, LANES), jnp.float32)
    for s in range(slabs):
        tile = store_ref[scalar_ref[2 + s]]
        slot = scalar_ref[2 + slabs + s]
        picked = pltpu.roll(tile, (LANES - slot * width) & (LANES - 1), 1)
        rows_ref[pl.ds(s * depth, depth), :] = picked[:depth]
        rows_ref[pl.ds(planes + s * depth, depth), :] = picked[depth:]
    rows_ref[...] = rows_ref[...].T
    faces_ref[pl.ds(0, part), :] = rows_ref[pl.ds(0, part, stride=2), :]
    faces_ref[pl.ds(part, part), :] = rows_ref[pl.ds(1, part, stride=2), :]
    head, tail = ends(partial(block_rows, faces_ref), 0, part, part, low_half)
    even_ref[2 * depth * len(late)] = jnp.where(is_even, tail, head)
    odd_ref[2 * depth * len(late)] = jnp.where(is_even, head, tail)


def halo_tiles(even_ref, odd_ref, index, is_even, low_half):
    first = even_ref[index]
    second = odd_ref[index]
    above = jnp.where(is_even, first, second)
    below = jnp.where(is_even, second, first)
    return (
        jnp.where(low_half, above, pltpu.roll(below, 4, 0)),
        jnp.where(low_half, pltpu.roll(above, 4, 0), below),
    )


def join_planes(load, out_ref, left_ref, right_ref, depth, width):
    part = width // 2
    for z in range(depth):
        for c in range(4):
            ref = right_ref if c & 1 else left_ref
            ref[pl.ds(z * width + (c >> 1), part, stride=2), :] = load(z, c)
    rows = depth * width
    both = jnp.concatenate([left_ref[pl.ds(0, rows), :], right_ref[pl.ds(0, rows), :]], axis=1)
    out_ref[...] = mm(both, merging_matrix()).reshape(depth, width, 2 * LANES)


def hessian_parts(below, here, above):
    rise = [a - b for a, b in zip(above, below)]
    y_sum, y_rise, yz_rise = [], [], []
    for c in range(4):
        odd = c >> 1
        same, other = here[c ^ 2], y_other(here[c ^ 2], odd)
        y_sum.append(same + other)
        y_rise.append(other - same if odd else same - other)
        same, other = rise[c ^ 2], y_other(rise[c ^ 2], odd)
        yz_rise.append(other - same if odd else same - other)
    out = []
    for c in range(4):
        odd = c & 1
        same, other = here[c ^ 1], x_other(here[c ^ 1], odd)
        twice = 2.0 * here[c]
        pxx = same + other - twice
        pyy = y_sum[c] - twice
        pzz = below[c] + above[c] - twice
        same, other = rise[c ^ 1], x_other(rise[c ^ 1], odd)
        pxz = other - same if odd else same - other
        same, other = y_rise[c ^ 1], x_other(y_rise[c ^ 1], odd)
        pxy = other - same if odd else same - other
        cross = pxy * pxy + pxz * pxz + yz_rise[c] * yz_rise[c]
        out.append(pxx * pyy + (pxx + pyy) * pzz - 0.0625 * cross)
    return out


def face_part(face, c, z, planes):
    lane = lane_iota(face.shape)
    if c & 1:
        turned = pltpu.roll(face, LANES - 1 - planes - z, 1)
        return jnp.where(lane == LANES - 1, turned, 0.0)
    turned = pltpu.roll(face, (LANES - z) & (LANES - 1), 1)
    return jnp.where(lane == 0, turned, 0.0)


def fill_block(p_ref, at, ref, edge_refs, tile, pencil, depth, part):
    is_even = (pencil % 2) == 0
    low_half = row_iota((8, LANES)) < 4
    for z in range(depth):
        for c in range(4):
            p_ref[at + z, c, pl.ds(0, part), :] = block_rows(ref, (4 * z + c) * part, part)
        for t in range(2):
            first, second = halo_tiles(*edge_refs, tile + 2 * z + t, is_even, low_half)
            p_ref[at + z, 2 * t, pl.ds(part, 8), :] = first
            p_ref[at + z, 2 * t + 1, pl.ds(part, 8), :] = second


def near_half_kernel(scalar_ref, *refs, depth, width, pencils):
    near = [k for k in range(EARLY) if OFFSETS[k] < 4]
    blocks = refs[: len(near)]
    even_ref, odd_ref, faces_ref, p_ref, s_ref, q_ref = refs[len(near) :]
    slab = scalar_ref[0]
    pencil = scalar_ref[1]
    part = width // 2
    half = 4 * depth
    first_plane = (slab // 4) * half
    mask = halo_mask(pencil, pencils)
    blank = jnp.zeros(p_ref.shape[1:], jnp.float32)
    p_ref[0] = blank
    p_ref[half + 1] = blank
    for k, ref in zip(near, blocks):
        at = ((slab ^ OFFSETS[k]) % 4) * depth + 1
        fill_block(p_ref, at, ref, (even_ref, odd_ref), 2 * depth * k, pencil, depth, part)

    def body(j, carry):
        source = hessian_parts(parts(p_ref, j), parts(p_ref, j + 1), parts(p_ref, j + 2))
        for c in range(4):
            s_ref[j, c] = source[c][:part]
            face = faces_ref[pl.ds((c >> 1) * part, part), :]
            face = face_part(face, c, first_plane + j, 2 * half)
            q_ref[j, c, pl.ds(0, part), :] = W * (face - source[c][:part])
            q_ref[j, c, pl.ds(part, 8), :] = (-W * mask) * source[c][part:]
        return carry

    lax.fori_loop(0, half, body, 0, unroll=HESS)


def far_half_kernel(scalar_ref, *refs, depth, width, pencils):
    far = [k for k in range(len(OFFSETS)) if OFFSETS[k] >= 4]
    blocks = refs[: len(far)]
    early_refs = refs[len(far) : len(far) + 2]
    late_refs = refs[len(far) + 2 : len(far) + 4]
    faces_ref, pn_ref, sn_ref, qn_ref = refs[len(far) + 4 : len(far) + 8]
    s_ref, q_ref, u_ref, coarse_ref = refs[len(far) + 8 : len(far) + 12]
    p_ref, f_ref = refs[len(far) + 12 :]
    slab = scalar_ref[0]
    pencil = scalar_ref[1]
    part = width // 2
    half = 4 * depth
    planes = 2 * half
    lower = slab < 4
    near_first = jnp.where(lower, 0, half)
    far_first = half - near_first
    is_even = (pencil % 2) == 0
    low_half = row_iota((8, LANES)) < 4
    mask = halo_mask(pencil, pencils)
    blank = jnp.zeros(p_ref.shape[1:], jnp.float32)
    for ref in (q_ref, u_ref):
        for z in (0, 1, planes + 2, planes + 3):
            ref[z] = blank
    p_ref[jnp.where(lower, half + 1, 0)] = blank
    p_ref[jnp.where(lower, 0, half + 1)] = pn_ref[jnp.where(lower, half, 1)]
    for k, ref in zip(far, blocks):
        at = ((slab ^ OFFSETS[k]) % 4) * depth + 1
        early = k < EARLY
        tile = 2 * depth * (k if early else k - EARLY)
        edge_refs = early_refs if early else late_refs
        fill_block(p_ref, at, ref, edge_refs, tile, pencil, depth, part)
    face_tile = 2 * depth * (len(OFFSETS) - EARLY)
    first, second = halo_tiles(*late_refs, face_tile, is_even, low_half)
    f_ref[0, pl.ds(0, part), :] = faces_ref[pl.ds(0, part), :]
    f_ref[0, pl.ds(part, 8), :] = first
    f_ref[1, pl.ds(0, part), :] = faces_ref[pl.ds(part, part), :]
    f_ref[1, pl.ds(part, 8), :] = second

    def finish(source, z):
        for c in range(4):
            face = face_part(f_ref[c >> 1], c, z, planes)
            put(q_ref, z + 2, c, W * (face - source[c]), mask)

    def copy(j, carry):
        z = near_first + j
        for c in range(4):
            face = face_part(f_ref[c >> 1, pl.ds(part, 8), :], c, z, planes)
            q_ref[z + 2, c, pl.ds(0, part), :] = qn_ref[j, c, pl.ds(0, part), :]
            q_ref[z + 2, c, pl.ds(part, 8), :] = (
                qn_ref[j, c, pl.ds(part, 8), :] + (W * mask) * face
            )
        return carry

    lax.fori_loop(0, half, copy, 0, unroll=UNROLL)

    def body(j, carry):
        source = hessian_parts(parts(p_ref, j), parts(p_ref, j + 1), parts(p_ref, j + 2))
        finish(source, far_first + j)
        return carry

    lax.fori_loop(0, half, body, 0, unroll=HESS)
    seam = jnp.where(lower, half, 1)
    here = parts(pn_ref, seam)
    inner = parts(pn_ref, jnp.where(lower, half - 1, 2))
    outer = parts(p_ref, jnp.where(lower, 1, half))
    below = [jnp.where(lower, a, b) for a, b in zip(inner, outer)]
    above = [jnp.where(lower, b, a) for a, b in zip(inner, outer)]
    source = hessian_parts(below, here, above)
    finish(source, near_first + seam - 1)
    own = (slab % 4) * depth
    for z in range(depth):
        is_seam = own + z == seam - 1
        for c in range(4):
            s_ref[z, c] = jnp.where(is_seam, source[c][:part], sn_ref[own + z, c])
    def second_sweep(z, carry):
        here = parts(q_ref, z + 2)
        for c in range(4):
            sides = neighbours(q_ref[z + 1, c], here, q_ref[z + 3, c], c)
            put(u_ref, z + 2, c, (1.0 + KEEP) * here[c] + W * sides, mask)
        return carry

    lax.fori_loop(0, planes, second_sweep, 0, unroll=UNROLL)
    restrict_window(u_ref, q_ref, coarse_ref, planes, part)


def restrict_window(u_ref, q_ref, coarse_ref, planes, part):
    def restrict(z, carry):
        total = None
        for at in (2 * z + 2, 2 * z + 3):
            here = parts(u_ref, at)
            for c in range(4):
                new = swept(u_ref[at - 1, c], here, u_ref[at + 1, c], q_ref[at, c], c)
                change = new[:part] - here[c][:part]
                total = change if total is None else total + change
        coarse_ref[pl.ds(pl.multiple_of(z * part, part), part), :] = 0.5 * total
        return carry

    lax.fori_loop(0, planes // 2, restrict, 0, unroll=PAIRS)


def between_kernel(scalar_ref, q_ref, u_ref, s_ref, source_hbm, swept_ref, *refs, pencils):
    left_ref, right_ref, source_ref, sem = refs
    depth, width, _ = source_ref.shape
    planes = q_ref.shape[0] - 4
    mask = halo_mask(scalar_ref[1], pencils)
    join_planes(lambda z, c: s_ref[z, c], source_ref, left_ref, right_ref, depth, width)
    copy_out = pltpu.make_async_copy(source_ref, source_hbm, sem)
    copy_out.start()

    def sweep(z, carry):
        here = parts(u_ref, z + 2)
        for c in range(4):
            new = swept(u_ref[z + 1, c], here, u_ref[z + 3, c], q_ref[z + 2, c], c)
            put(swept_ref, z + 2, c, new, mask)
        return carry

    lax.fori_loop(0, planes, sweep, 0, unroll=UNROLL)
    copy_out.wait()


def window_kernel(scalar_ref, qwin_ref, uwin_ref, win_ref, *, pencils):
    mask = halo_mask(scalar_ref[1], pencils)
    for z in range(win_ref.shape[0]):
        here = parts(uwin_ref, z + 1)
        for c in range(4):
            new = swept(uwin_ref[z, c], here, uwin_ref[z + 2, c], qwin_ref[z, c], c)
            put(win_ref, z, c, new, mask)


def coarse_window(v_ref, z, pencil, part):
    start = pl.multiple_of(pencil * part, part)
    own = v_ref[z, pl.ds(start + HALO, part), :]
    above = v_ref[z, pl.ds(start + HALO + part, 8), :]
    below = v_ref[z, pl.ds(start, 8), :]
    tile = jnp.where(row_iota((8, LANES)) < 4, above, below)
    return jnp.concatenate([own, tile], axis=0)


def middle_kernel(
    scalar_ref, c0_ref, c1_ref, c2_ref, c3_ref, q_ref, swept_ref,
    qwin_ref, uwin_ref, coarse_ref,
    v_ref, q1_ref, a1_ref, b1_ref, tmp_ref, a_ref, b_ref, *, depth, width, pencils, shape
):
    slab = scalar_ref[0]
    pencil = scalar_ref[1]
    planes = a_ref.shape[0] - 4
    part = width // 2
    mask = halo_mask(pencil, pencils)
    piece_refs = (c0_ref, c1_ref, c2_ref, c3_ref)
    solve_level_one(piece_refs, pencil, v_ref, q1_ref, a1_ref, b1_ref, tmp_ref, shape)
    blank = jnp.zeros(a_ref.shape[1:], jnp.float32)
    for ref in (a_ref, b_ref):
        for z in (0, 1, planes + 2, planes + 3):
            ref[z] = blank

    def third_sweep(z, carry):
        v = [coarse_window(v_ref, z + k, pencil, part) for k in range(3)]
        for k, children in enumerate(swept_children(*v)):
            at = 2 * z + 2 + k
            for c in range(4):
                put(a_ref, at, c, swept_ref[at, c] + children[c], mask)
        return carry

    lax.fori_loop(0, planes // 2, third_sweep, 0, unroll=PAIRS)

    def sweep(src, dst):
        def body(z, carry):
            here = parts(src, z + 2)
            for c in range(4):
                new = swept(src[z + 1, c], here, src[z + 3, c], q_ref[z + 2, c], c)
                put(dst, z + 2, c, new, mask)
            return carry

        lax.fori_loop(0, planes, body, 0, unroll=UNROLL)

    sweep(a_ref, b_ref)
    sweep(b_ref, a_ref)
    sweep(a_ref, b_ref)
    restrict_window(b_ref, q_ref, coarse_ref, planes, part)
    for z in range(depth + 2):
        qwin_ref[z] = q_ref[slab * depth + z + 1]
    for z in range(depth + 4):
        uwin_ref[z] = b_ref[slab * depth + z]


def last_kernel(
    scalar_ref, c0_ref, c1_ref, c2_ref, c3_ref, qwin_ref, win_ref, out_hbm,
    v_ref, q1_ref, a1_ref, b1_ref, tmp_ref, a_ref, left_ref, right_ref, out_ref, sems,
    *, depth, width, pencils, shape
):
    slab = scalar_ref[0]
    pencil = scalar_ref[1]
    planes = shape[0] * 2
    part = width // 2
    mask = halo_mask(pencil, pencils)
    piece_refs = (c0_ref, c1_ref, c2_ref, c3_ref)
    solve_level_one(piece_refs, pencil, v_ref, q1_ref, a1_ref, b1_ref, tmp_ref, shape, slab)
    blank = jnp.zeros((part + 8, LANES), jnp.float32)
    v = [coarse_window(v_ref, slab * (depth // 2) + k, pencil, part) for k in range(4)]
    v = [blank] + v + [blank]
    for k in range(4):
        for side, children in enumerate(swept_children(*v[k : k + 3])):
            z = 2 * k + side - 1
            if 0 <= z < depth + 2:
                at = slab * depth - 1 + z
                live = jnp.where((at >= 0) & (at < planes), 1.0, 0.0)
                for c in range(4):
                    put(a_ref, z, c, live * (win_ref[z, c] + children[c]), mask)
    matrix = merging_matrix()
    copies = []
    for z in range(depth):
        here = parts(a_ref, z + 1)
        for c in range(4):
            new = swept(a_ref[z, c], here, a_ref[z + 2, c], qwin_ref[z + 1, c], c)
            ref = right_ref if c & 1 else left_ref
            ref[z, pl.ds(c >> 1, part, stride=2), :] = new[:part]
        out_ref[z] = mm(jnp.concatenate([left_ref[z], right_ref[z]], axis=1), matrix)
        copies.append(pltpu.make_async_copy(out_ref.at[z], out_hbm.at[z], sems.at[z]))
        copies[-1].start()
    for copy in copies:
        copy.wait()


def vmem():
    return pl.BlockSpec(memory_space=pltpu.VMEM)


def smem():
    return pl.BlockSpec(memory_space=pltpu.SMEM)


def arr(*shape):
    return jax.ShapeDtypeStruct(shape, jnp.float32)


def buf(*shape):
    return pltpu.VMEM(shape, jnp.float32)


def call(kernel, name, scalars, args, outs, scratch=(), space=pltpu.VMEM, out_space=None):
    out_specs = jax.tree.map(lambda _: vmem(), outs)
    if out_space is not None:
        out_specs = tuple(pl.BlockSpec(memory_space=one) for one in out_space)
    return pl.pallas_call(
        kernel,
        out_shape=outs,
        in_specs=[smem()] * len(scalars) + [pl.BlockSpec(memory_space=space)] * len(args),
        out_specs=out_specs,
        scratch_shapes=list(scratch),
        compiler_params=pltpu.CompilerParams(vmem_limit_bytes=16 << 20),
        name=name,
    )(*scalars, *args)


def windowed(potential, parent_store, face_owner, face_offset):
    depth, width, columns = potential.shape
    slabs = lax.axis_size("slab")
    pencils = lax.axis_size("pencil")
    planes, height = slabs * depth, pencils * width
    part = width // 2
    rows = part + 8
    where = jnp.stack([lax.axis_index("slab"), lax.axis_index("pencil")]).astype(jnp.int32)
    scalars = jnp.concatenate([where, face_owner, face_offset])
    own = call(
        pack_kernel,
        "pack",
        [],
        [pltpu.with_memory_space_constraint(x, pltpu.HBM) for x in (potential, parent_store)],
        arr(depth * width * 2 + 8, LANES),
        [
            buf(depth * width, LANES),
            buf(depth * width, LANES),
            buf(*potential.shape),
            buf(*parent_store.shape),
            pltpu.SemaphoreType.DMA((2,)),
        ],
        space=pltpu.HBM,
    )

    def swap(x, bits):
        return lax.ppermute(x, "slab", [(i, i ^ bits) for i in range(slabs)])

    near = [swap(own, bits) for bits in OFFSETS[1:5]]
    blocks = [own, *near] + [swap(near[0], bits) for bits in OFFSETS[2:5]]
    low_pairs = [(i, i + 1) for i in range(0, pencils - 1, 2)]
    high_pairs = [(i, i + 1) for i in range(1, pencils - 1, 2)]

    def beside(even, odd):
        return (
            lax.ppermute(even, "pencil", low_pairs + [(j, i) for i, j in low_pairs]),
            lax.ppermute(odd, "pencil", high_pairs + [(j, i) for i, j in high_pairs]),
        )

    message = arr(2 * depth * EARLY, 8, LANES)
    early = call(
        partial(early_edges_kernel, depth=depth, width=width),
        "early_edges",
        [scalars],
        blocks[:EARLY],
        (message, message),
    )
    early = beside(*early)
    message = arr(2 * depth * (slabs - EARLY) + 1, 8, LANES)
    even, odd, faces = call(
        partial(late_edges_kernel, depth=depth, width=width),
        "late_edges",
        [scalars],
        blocks,
        (message, message, arr(width, LANES)),
        [buf(slabs, 8, LANES), buf(LANES, LANES)],
    )
    late = beside(even, odd)
    shape = (planes // 2, height // 2, columns // 2)
    coarse_part = arr(planes // 2 * part, LANES)
    field = (planes + 4, 4, rows, LANES)
    half = planes // 2
    near = call(
        partial(near_half_kernel, depth=depth, width=width, pencils=pencils),
        "near_half",
        [scalars],
        [b for b, offset in zip(blocks, OFFSETS) if offset < 4] + [*early, faces],
        (arr(half + 2, 4, rows, LANES), arr(half, 4, part, LANES), arr(half, 4, rows, LANES)),
    )
    own_source, q, u, coarse = call(
        partial(far_half_kernel, depth=depth, width=width, pencils=pencils),
        "far_half",
        [scalars],
        [b for b, offset in zip(blocks, OFFSETS) if offset >= 4] + [*early, *late, faces, *near],
        (arr(depth, 4, part, LANES), arr(*field), arr(*field), coarse_part),
        [buf(half + 2, 4, rows, LANES), buf(2, rows, LANES)],
    )

    def pair(x, bits):
        return lax.ppermute(x, "pencil", [(i, i ^ bits) for i in range(pencils)])

    def gather(x, meanwhile):
        beside, across = pair(x, 1), pair(x, 2)
        made = meanwhile()
        across, made = lax.optimization_barrier((across, made))
        return [x, beside, across, pair(across, 1)], made

    between = lambda: call(
        partial(between_kernel, pencils=pencils),
        "between",
        [scalars],
        [q, u, own_source],
        (arr(depth, width, columns), arr(*field)),
        [
            buf(depth * width, LANES),
            buf(depth * width, LANES),
            buf(depth, width, columns),
            pltpu.SemaphoreType.DMA,
        ],
        out_space=[pl.ANY, pltpu.VMEM],
    )
    pieces, (source, swept_once) = gather(coarse, between)
    level = (shape[0] + 4, 2, shape[1] // 2, LANES)
    level_scratch = [
        buf(shape[0] + 2, shape[1] + 2 * HALO, LANES),
        buf(*level),
        buf(*level),
        buf(*level),
        buf((shape[0] // 2 + 4) * shape[1] // 2, LANES),
    ]
    sizes = dict(depth=depth, width=width, pencils=pencils, shape=shape)
    qwin, uwin, coarse = call(
        partial(middle_kernel, **sizes),
        "middle",
        [scalars],
        [*pieces, q, swept_once],
        (arr(depth + 2, 4, rows, LANES), arr(depth + 4, 4, rows, LANES), coarse_part),
        level_scratch + [buf(*field), buf(*field)],
    )
    window = lambda: call(
        partial(window_kernel, pencils=pencils),
        "window",
        [scalars],
        [qwin, uwin],
        arr(depth + 2, 4, rows, LANES),
    )
    pieces, win = gather(coarse, window)
    (solved,) = call(
        partial(last_kernel, **sizes),
        "last",
        [scalars],
        [*pieces, qwin, win],
        (arr(depth, width, columns),),
        level_scratch
        + [
            buf(depth + 2, 4, rows, LANES),
            buf(depth, width, LANES),
            buf(depth, width, LANES),
            buf(depth, width, columns),
            pltpu.SemaphoreType.DMA((depth,)),
        ],
        out_space=[pl.ANY],
    )
    return solved, source


def fits_window(potential, parent_store):
    depth, width, columns = potential.shape
    slabs = lax.axis_size("slab")
    pencils = lax.axis_size("pencil")
    planes = slabs * depth
    return (
        slabs == 8
        and depth == 4
        and columns == 2 * LANES
        and width == 32
        and parent_store.shape[0] * width == LANES
        and 2 * planes < LANES
        and pencils == 4
    )


def padded(cells, sides, width):
    for axis, dim in sides:
        count = lax.axis_size(axis)
        ends = count - 1
        head = lax.slice_in_dim(cells, 0, width, axis=dim)
        tail = lax.slice_in_dim(cells, cells.shape[dim] - width, cells.shape[dim], axis=dim)
        cells = jnp.concatenate(
            [
                lax.ppermute(tail, axis, [(i, (i + 1) % count) for i in range(ends)]),
                cells,
                lax.ppermute(head, axis, [((i + 1) % count, i) for i in range(ends)]),
            ],
            axis=dim,
        )
    return cells


def hessian_source(p):
    c = p[1:-1, 1:-1, 1:-1]
    pxx = p[1:-1, 1:-1, 2:] + p[1:-1, 1:-1, :-2] - 2.0 * c
    pyy = p[1:-1, 2:, 1:-1] + p[1:-1, :-2, 1:-1] - 2.0 * c
    pzz = p[2:, 1:-1, 1:-1] + p[:-2, 1:-1, 1:-1] - 2.0 * c
    pxy = 0.25 * (p[1:-1, 2:, 2:] - p[1:-1, :-2, 2:] - p[1:-1, 2:, :-2] + p[1:-1, :-2, :-2])
    pxz = 0.25 * (p[2:, 1:-1, 2:] - p[:-2, 1:-1, 2:] - p[2:, 1:-1, :-2] + p[:-2, 1:-1, :-2])
    pyz = 0.25 * (p[2:, 2:, 1:-1] - p[:-2, 2:, 1:-1] - p[2:, :-2, 1:-1] + p[:-2, :-2, 1:-1])
    return pxx * pyy + pxx * pzz + pyy * pzz - pxy * pxy - pxz * pxz - pyz * pyz


def apply_padded(p, level):
    c = p[1:-1, 1:-1, 1:-1]
    near = p[2:, 1:-1, 1:-1] + p[:-2, 1:-1, 1:-1]
    near = near + p[1:-1, 2:, 1:-1] + p[1:-1, :-2, 1:-1]
    near = near + p[1:-1, 1:-1, 2:] + p[1:-1, 1:-1, :-2]
    return (6.0 * c - near) * 0.25**level


def step_weight(level):
    return OMEGA / 6.0 * 4.0**level


def sweep_whole(u, rhs, level):
    return u + step_weight(level) * (rhs - apply_padded(jnp.pad(u, 1), level))


def restrict(r):
    a, b, c = r.shape
    return r.reshape(a // 2, 2, b // 2, 2, c // 2, 2).mean(axis=(1, 3, 5))


def prolong(e):
    a, b, c = e.shape
    return jnp.broadcast_to(e[:, None, :, None, :, None], (a, 2, b, 2, c, 2)).reshape(
        2 * a, 2 * b, 2 * c
    )


def vcycle(u, rhs, level):
    if is_coarsest(rhs.shape):
        for sweep_count in range(8):
            u = sweep_whole(u, rhs, level)
        return u
    u = sweep_whole(u, rhs, level)
    u = sweep_whole(u, rhs, level)
    resid = rhs - apply_padded(jnp.pad(u, 1), level)
    coarse = restrict(resid)
    correction = vcycle(jnp.zeros_like(coarse), coarse, level + 1)
    u = u + prolong(correction)
    u = sweep_whole(u, rhs, level)
    u = sweep_whole(u, rhs, level)
    return u


def widen_x(p):
    return jnp.pad(p, ((0, 0), (0, 0), (1, 1)))


def rim_one(u):
    return widen_x(padded(u, (("slab", 0), ("pencil", 1)), 1))


def coarse_solve(rhs, level):
    width = rhs.shape[1]
    columns = rhs.shape[2]
    whole = lax.all_gather(rhs, ("slab", "pencil"), axis=0, tiled=True)
    whole = whole.reshape(lax.axis_size("slab"), lax.axis_size("pencil") * width, columns)
    solved = vcycle(jnp.zeros_like(whole), whole, level)
    start_y = lax.axis_index("pencil") * width
    return lax.dynamic_slice(
        solved, (lax.axis_index("slab"), start_y, jnp.int32(0)), (1, width, columns)
    )


def split_vcycle(u, rhs, level, from_zero):
    if rhs.shape[0] == 1:
        return coarse_solve(rhs, level)
    weight = step_weight(level)
    if from_zero:
        u = weight * rhs
    else:
        u = u + weight * (rhs - apply_padded(rim_one(u), level))
    u = u + weight * (rhs - apply_padded(rim_one(u), level))
    resid = rhs - apply_padded(rim_one(u), level)
    correction = split_vcycle(None, restrict(resid), level + 1, True)
    u = u + prolong(correction)
    u = u + weight * (rhs - apply_padded(rim_one(u), level))
    u = u + weight * (rhs - apply_padded(rim_one(u), level))
    return u


def plain(potential, parent_store, face_owner, face_offset):
    depth, width, columns = potential.shape
    grown = widen_x(padded(potential, (("slab", 0), ("pencil", 1)), 1))
    source = hessian_source(grown)
    slab_index = lax.axis_index("slab")
    wanted = face_owner[slab_index] * parent_store.shape[0] + face_offset[slab_index]
    piece = lax.all_gather(parent_store, "slab", axis=0, tiled=True)
    labels = jnp.arange(piece.shape[0], dtype=jnp.int32)
    match = labels == wanted
    faces = jnp.sum(jnp.where(match[:, None, None, None], piece, 0.0), axis=0)
    rhs = -source
    rhs = rhs.at[:, :, 0].add(faces[0])
    rhs = rhs.at[:, :, columns - 1].add(faces[1])
    solved = jnp.zeros_like(rhs)
    for cycle in range(CYCLES):
        solved = split_vcycle(solved, rhs, 0, cycle == 0)
    return (solved, source)


def on_device(potential, parent_store, face_owner, face_offset):
    if fits_window(potential, parent_store):
        return windowed(potential, parent_store, face_owner, face_offset)
    return plain(potential, parent_store, face_owner, face_offset)


def solution(mesh):
    in_specs = (P("slab", "pencil", None), P("slab", None, None, "pencil"), P(), P())
    out_specs = (P("slab", "pencil", None), P("slab", "pencil", None))
    return jax.shard_map(
        on_device, mesh=mesh, in_specs=in_specs, out_specs=out_specs, check_vma=False
    )
```

```python
from functools import partial

import jax
import jax.numpy as jnp
import numpy as np
from jax import lax
from jax.experimental import pallas as pl
from jax.experimental.pallas import tpu as pltpu
from jax.sharding import PartitionSpec as P

CYCLES = 2
OMEGA = 0.8
W = float(np.float32(OMEGA / 6.0))
KEEP = 1.0 - 6.0 * W
HALO = 8
LANES = 128
UNROLL = 16
PAIRS = 16
HESS = 16
LEVEL = 16
LPAIRS = 4


def is_coarsest(shape):
    return min(shape) <= 4 or any((d % 2 for d in shape))


def lane_iota(shape):
    return lax.broadcasted_iota(jnp.int32, shape, len(shape) - 1)


def row_iota(shape):
    return lax.broadcasted_iota(jnp.int32, shape, len(shape) - 2)


def x_other(values, odd):
    lane = lane_iota(values.shape)
    if odd:
        return jnp.where(lane == LANES - 1, 0.0, pltpu.roll(values, LANES - 1, 1))
    return jnp.where(lane == 0, 0.0, pltpu.roll(values, 1, 1))


def y_other(values, odd):
    return pltpu.roll(values, values.shape[0] - 1 if odd else 1, 0)


def neighbours(below, here, above, c):
    across, along = here[c ^ 1], here[c ^ 2]
    near = (below + above) + (across + x_other(across, c & 1))
    return near + (along + y_other(along, c >> 1))


def swept(below, here, above, q, c):
    return KEEP * here[c] + W * neighbours(below, here, above, c) + q


def swept_children(below, here, above):
    here = W * here
    base = ((1.0 - 3.0 * W) / W) * here
    beyond = [W * below, W * above]
    across = [base + x_other(here, odd) for odd in range(2)]
    along = [y_other(here, odd) for odd in range(2)]
    flat = [across[c & 1] + along[c >> 1] for c in range(4)]
    return [[one + beyond[k] for one in flat] for k in range(2)]


def parts(ref, z):
    return [ref[z, c] for c in range(4)]


def halo_mask(pencil, pencils):
    row = row_iota((8, LANES))
    above = jnp.where(pencil < pencils - 1, 1.0, 0.0)
    below = jnp.where(pencil > 0, 1.0, 0.0)
    return jnp.where(row < 4, above, below)


def put(ref, z, c, values, mask):
    own = values.shape[0] - 8
    ref[z, c, pl.ds(0, own), :] = values[:own]
    ref[z, c, pl.ds(own, 8), :] = values[own:] * mask


def index_pair(rows, columns):
    return (
        lax.broadcasted_iota(jnp.int32, (rows, columns), 0),
        lax.broadcasted_iota(jnp.int32, (rows, columns), 1),
    )


def chosen(where, value):
    return jnp.where(where, value, 0.0).astype(jnp.bfloat16)


def splitting_matrix():
    i, j = index_pair(2 * LANES, 2 * LANES)
    return chosen(i == 2 * (j & (LANES - 1)) + (j >= LANES).astype(jnp.int32), 1.0)


def merging_matrix():
    i, j = index_pair(2 * LANES, 2 * LANES)
    return chosen(j == 2 * (i & (LANES - 1)) + (i >= LANES).astype(jnp.int32), 1.0)


def mm(a, b):
    high = a.astype(jnp.bfloat16)
    rest = a - high.astype(jnp.float32)
    middle = rest.astype(jnp.bfloat16)
    low = (rest - middle.astype(jnp.float32)).astype(jnp.bfloat16)

    def dot(x):
        return jnp.dot(x, b, preferred_element_type=jnp.float32)

    return dot(high) + (dot(middle) + dot(low))


def pair_sum(values, distance, axis):
    size = values.shape[axis]
    at = lax.broadcasted_iota(jnp.int32, values.shape, axis)
    ahead = pltpu.roll(values, size - distance, axis)
    behind = pltpu.roll(values, distance, axis)
    return values + jnp.where((at & distance) == 0, ahead, behind)


def x_sides(values, distance):
    lane = lane_iota(values.shape)
    left = jnp.where(lane < distance, 0.0, pltpu.roll(values, distance, 1))
    right = jnp.where(lane >= LANES - distance, 0.0, pltpu.roll(values, LANES - distance, 1))
    return left + right


def flat_sweep(u, q, rows, yd, xd):
    total = u.shape[0]
    zero = jnp.zeros((rows, LANES), jnp.float32)
    below = jnp.concatenate([zero, u[: total - rows]], axis=0)
    above = jnp.concatenate([u[rows:], zero], axis=0)
    y = row_iota(u.shape) & (rows - 1)
    down = jnp.where(y < yd, 0.0, pltpu.roll(u, yd, 0))
    up = jnp.where(y >= rows - yd, 0.0, pltpu.roll(u, total - yd, 0))
    return KEEP * u + W * ((below + above) + (down + up) + x_sides(u, xd)) + q


def flat_vcycle(q, shape, rows, yd, xd):
    if is_coarsest(shape):
        u = q
        for _ in range(7):
            u = flat_sweep(u, q, rows, yd, xd)
        return u
    zs, ys, xs = shape
    u = flat_sweep(q, q, rows, yd, xd)
    change = flat_sweep(u, q, rows, yd, xd) - u
    pairs = [
        change[2 * z * rows : (2 * z + 1) * rows] + change[(2 * z + 1) * rows : (2 * z + 2) * rows]
        for z in range(zs // 2)
    ]
    coarse = 0.5 * pair_sum(pair_sum(jnp.concatenate(pairs, axis=0), yd, 0), xd, 1)
    e = flat_vcycle(coarse, (zs // 2, ys // 2, xs // 2), rows, 2 * yd, 2 * xd)
    planes = []
    for z in range(zs // 2):
        planes += [e[z * rows : (z + 1) * rows]] * 2
    u = u + jnp.concatenate(planes, axis=0)
    u = flat_sweep(u, q, rows, yd, xd)
    return flat_sweep(u, q, rows, yd, xd)


def solve_level_one(piece_refs, pencil, v_ref, q_ref, a_ref, b_ref, tmp_ref, shape, near=None):
    zs, ys, xs = shape
    rows = ys // 2
    half = zs // 2
    piece = rows // len(piece_refs)
    row = row_iota((rows, LANES))
    blank = jnp.zeros((rows, LANES), jnp.float32)
    for ref in (q_ref, a_ref, b_ref):
        for z in (0, 1, zs + 2, zs + 3):
            for c in range(2):
                ref[z, c] = blank
    for z in (0, 1, half + 2, half + 3):
        tmp_ref[pl.ds(z * rows, rows), :] = blank
    edge = jnp.zeros((HALO, LANES), jnp.float32)
    for z in range(zs + 2):
        v_ref[z, pl.ds(0, HALO), :] = edge
        v_ref[z, pl.ds(HALO + ys, HALO), :] = edge
    if near is None:
        for z in (0, zs + 1):
            for c in range(2):
                v_ref[z, pl.ds(HALO + c * rows, rows), :] = blank
    for z in range(zs):
        for c in range(2):
            for k, ref in enumerate(piece_refs):
                spot = pl.ds(2 * piece * z + c, piece, stride=2)
                to = pl.ds(pl.multiple_of((pencil ^ k) * piece, piece), piece)
                q_ref[z + 2, c, to, :] = ref[spot, :]

    def y_beyond(other, c):
        if c:
            return jnp.where(row == rows - 1, 0.0, pltpu.roll(other, rows - 1, 0))
        return jnp.where(row == 0, 0.0, pltpu.roll(other, 1, 0))

    def around(src, z):
        here = [src[z, 0], src[z, 1]]
        near = []
        for c in range(2):
            other = here[1 - c]
            sides = (other + y_beyond(other, c)) + x_sides(here[c], 1)
            near.append((src[z - 1, c] + src[z + 1, c]) + sides)
        return here, near

    def second(z, carry):
        here, sides = around(q_ref, z)
        for c in range(2):
            a_ref[z, c] = (1.0 + KEEP) * here[c] + W * sides[c]
        return carry

    lax.fori_loop(2, zs + 2, second, 0, unroll=LEVEL)

    def restrict(z, carry):
        total = None
        for at in (2 * z + 2, 2 * z + 3):
            here, sides = around(a_ref, at)
            for c in range(2):
                new = KEEP * here[c] + W * sides[c] + q_ref[at, c]
                b_ref[at, c] = new
                change = new - here[c]
                total = change if total is None else total + change
        spot = pl.ds(pl.multiple_of((z + 2) * rows, rows), rows)
        tmp_ref[spot, :] = 0.5 * pair_sum(total, 1, 1)
        return carry

    pairs_unroll = LPAIRS if near is None else half
    lax.fori_loop(0, half, restrict, 0, unroll=pairs_unroll)
    inner = pl.ds(2 * rows, half * rows)
    tmp_ref[inner, :] = flat_vcycle(tmp_ref[inner, :], (half, ys // 2, xs // 2), rows, 1, 2)

    def live(at, count):
        return jnp.where((at >= 0) & (at < count), 1.0, 0.0)

    def third(z):
        e = [tmp_ref[pl.ds(pl.multiple_of((z + k) * rows, rows), rows), :] for k in (1, 2, 3)]
        here = W * e[1]
        base = ((1.0 - 4.0 * W) / W) * here + x_sides(here, 1)
        for c in range(2):
            flat = base + y_beyond(here, c)
            for k in range(2):
                new = b_ref[2 * z + 2 + k, c] + (flat + W * e[2 * k])
                a_ref[2 * z + 2 + k, c] = new if near is None else live(z, half) * new

    def fourth(z):
        here, sides = around(a_ref, z + 2)
        for c in range(2):
            new = KEEP * here[c] + W * sides[c] + q_ref[z + 2, c]
            if near is not None:
                new = live(z, zs) * new
            v_ref[z + 1, pl.ds(HALO + c, rows, stride=2), :] = new

    def loop(step, start, count, unroll):
        def body(i, carry):
            step(start + i)
            return carry

        lax.fori_loop(0, count, body, 0, unroll=unroll)

    if near is None:
        loop(third, 0, half, LPAIRS)
        loop(fourth, 0, zs, LEVEL)
    else:
        loop(third, near - 1, 3, 3)
        loop(fourth, 2 * near - 1, 4, 4)


def pack_kernel(
    potential_hbm, store_hbm, out_ref, even_ref, odd_ref, potential_ref, store_ref, sems
):
    copies = [
        pltpu.make_async_copy(potential_hbm, potential_ref, sems.at[0]),
        pltpu.make_async_copy(store_hbm, store_ref, sems.at[1]),
    ]
    for copy in copies:
        copy.start()
    matrix = splitting_matrix()
    for copy in copies:
        copy.wait()
    depth, width, columns = potential_ref.shape
    slots = store_ref.shape[0]
    part = width // 2
    split = mm(potential_ref[...].reshape(depth * width, columns), matrix)
    even_ref[...] = split[:, :LANES]
    odd_ref[...] = split[:, LANES:]
    for z in range(depth):
        for c in range(4):
            ref = odd_ref if c & 1 else even_ref
            spot = pl.ds((4 * z + c) * part, part)
            out_ref[spot, :] = ref[pl.ds(z * width + (c >> 1), part, stride=2), :]
    base = depth * width * 2
    for slot in range(slots):
        for side in range(2):
            spot = pl.ds(base + side * depth, depth)
            out_ref[spot, pl.ds(slot * width, width)] = store_ref[slot, side]


OFFSETS = (0, 4, 3, 1, 2, 7, 5, 6)
EARLY = 5


def block_rows(ref, start, count):
    return ref[pl.ds(start, count), :]


def ends(load, first, second, part, low_half):
    head = jnp.where(low_half, load(first, 8), pltpu.roll(load(second, 8), 4, 0))
    tail = jnp.where(
        low_half, pltpu.roll(load(first + part - 8, 8), 4, 0), load(second + part - 8, 8)
    )
    return head, tail


def store_ends(ref, pencil, out_refs, at, depth, part):
    even_ref, odd_ref = out_refs
    is_even = (pencil % 2) == 0
    low_half = row_iota((8, LANES)) < 4
    for z in range(depth):
        for t in range(2):
            head, tail = ends(
                partial(block_rows, ref),
                (4 * z + 2 * t) * part, (4 * z + 2 * t + 1) * part, part, low_half,
            )
            even_ref[at + 2 * z + t] = jnp.where(is_even, tail, head)
            odd_ref[at + 2 * z + t] = jnp.where(is_even, head, tail)


def early_edges_kernel(scalar_ref, *refs, depth, width):
    blocks, out_refs = refs[:EARLY], refs[EARLY:]
    for k, ref in enumerate(blocks):
        store_ends(ref, scalar_ref[1], out_refs, 2 * depth * k, depth, width // 2)


def late_edges_kernel(scalar_ref, *refs, depth, width):
    slabs = len(OFFSETS)
    even_ref, odd_ref, faces_ref, store_ref, rows_ref = refs[slabs:]
    slab = scalar_ref[0]
    pencil = scalar_ref[1]
    planes = slabs * depth
    part = width // 2
    is_even = (pencil % 2) == 0
    low_half = row_iota((8, LANES)) < 4
    base = depth * width * 2
    late = refs[EARLY:slabs]
    for k, ref in enumerate(late):
        store_ends(ref, pencil, (even_ref, odd_ref), 2 * depth * k, depth, part)
    for offset, ref in zip(OFFSETS, refs):
        store_ref[slab ^ offset] = block_rows(ref, base, 8)
    rest = LANES - 2 * planes
    rows_ref[pl.ds(2 * planes, rest), :] = jnp.zeros((rest, LANES), jnp.float32)
    for s in range(slabs):
        tile = store_ref[scalar_ref[2 + s]]
        slot = scalar_ref[2 + slabs + s]
        picked = pltpu.roll(tile, (LANES - slot * width) & (LANES - 1), 1)
        rows_ref[pl.ds(s * depth, depth), :] = picked[:depth]
        rows_ref[pl.ds(planes + s * depth, depth), :] = picked[depth:]
    rows_ref[...] = rows_ref[...].T
    faces_ref[pl.ds(0, part), :] = rows_ref[pl.ds(0, part, stride=2), :]
    faces_ref[pl.ds(part, part), :] = rows_ref[pl.ds(1, part, stride=2), :]
    head, tail = ends(partial(block_rows, faces_ref), 0, part, part, low_half)
    even_ref[2 * depth * len(late)] = jnp.where(is_even, tail, head)
    odd_ref[2 * depth * len(late)] = jnp.where(is_even, head, tail)


def halo_tiles(even_ref, odd_ref, index, is_even, low_half):
    first = even_ref[index]
    second = odd_ref[index]
    above = jnp.where(is_even, first, second)
    below = jnp.where(is_even, second, first)
    return (
        jnp.where(low_half, above, pltpu.roll(below, 4, 0)),
        jnp.where(low_half, pltpu.roll(above, 4, 0), below),
    )


def join_planes(load, out_ref, left_ref, right_ref, depth, width):
    part = width // 2
    for z in range(depth):
        for c in range(4):
            ref = right_ref if c & 1 else left_ref
            ref[pl.ds(z * width + (c >> 1), part, stride=2), :] = load(z, c)
    rows = depth * width
    both = jnp.concatenate([left_ref[pl.ds(0, rows), :], right_ref[pl.ds(0, rows), :]], axis=1)
    out_ref[...] = mm(both, merging_matrix()).reshape(depth, width, 2 * LANES)


def hessian_parts(below, here, above):
    rise = [a - b for a, b in zip(above, below)]
    y_sum, y_rise, yz_rise = [], [], []
    for c in range(4):
        odd = c >> 1
        same, other = here[c ^ 2], y_other(here[c ^ 2], odd)
        y_sum.append(same + other)
        y_rise.append(other - same if odd else same - other)
        same, other = rise[c ^ 2], y_other(rise[c ^ 2], odd)
        yz_rise.append(other - same if odd else same - other)
    out = []
    for c in range(4):
        odd = c & 1
        same, other = here[c ^ 1], x_other(here[c ^ 1], odd)
        twice = 2.0 * here[c]
        pxx = same + other - twice
        pyy = y_sum[c] - twice
        pzz = below[c] + above[c] - twice
        same, other = rise[c ^ 1], x_other(rise[c ^ 1], odd)
        pxz = other - same if odd else same - other
        same, other = y_rise[c ^ 1], x_other(y_rise[c ^ 1], odd)
        pxy = other - same if odd else same - other
        cross = pxy * pxy + pxz * pxz + yz_rise[c] * yz_rise[c]
        out.append(pxx * pyy + (pxx + pyy) * pzz - 0.0625 * cross)
    return out


def face_part(face, c, z, planes):
    lane = lane_iota(face.shape)
    if c & 1:
        turned = pltpu.roll(face, LANES - 1 - planes - z, 1)
        return jnp.where(lane == LANES - 1, turned, 0.0)
    turned = pltpu.roll(face, (LANES - z) & (LANES - 1), 1)
    return jnp.where(lane == 0, turned, 0.0)


def fill_block(p_ref, at, ref, edge_refs, tile, pencil, depth, part):
    is_even = (pencil % 2) == 0
    low_half = row_iota((8, LANES)) < 4
    for z in range(depth):
        for c in range(4):
            p_ref[at + z, c, pl.ds(0, part), :] = block_rows(ref, (4 * z + c) * part, part)
        for t in range(2):
            first, second = halo_tiles(*edge_refs, tile + 2 * z + t, is_even, low_half)
            p_ref[at + z, 2 * t, pl.ds(part, 8), :] = first
            p_ref[at + z, 2 * t + 1, pl.ds(part, 8), :] = second


def near_half_kernel(scalar_ref, *refs, depth, width, pencils):
    near = [k for k in range(EARLY) if OFFSETS[k] < 4]
    blocks = refs[: len(near)]
    even_ref, odd_ref, faces_ref, p_ref, s_ref, q_ref = refs[len(near) :]
    slab = scalar_ref[0]
    pencil = scalar_ref[1]
    part = width // 2
    half = 4 * depth
    first_plane = (slab // 4) * half
    mask = halo_mask(pencil, pencils)
    blank = jnp.zeros(p_ref.shape[1:], jnp.float32)
    p_ref[0] = blank
    p_ref[half + 1] = blank
    for k, ref in zip(near, blocks):
        at = ((slab ^ OFFSETS[k]) % 4) * depth + 1
        fill_block(p_ref, at, ref, (even_ref, odd_ref), 2 * depth * k, pencil, depth, part)

    def body(j, carry):
        source = hessian_parts(parts(p_ref, j), parts(p_ref, j + 1), parts(p_ref, j + 2))
        for c in range(4):
            s_ref[j, c] = source[c][:part]
            face = faces_ref[pl.ds((c >> 1) * part, part), :]
            face = face_part(face, c, first_plane + j, 2 * half)
            q_ref[j, c, pl.ds(0, part), :] = W * (face - source[c][:part])
            q_ref[j, c, pl.ds(part, 8), :] = (-W * mask) * source[c][part:]
        return carry

    lax.fori_loop(0, half, body, 0, unroll=HESS)


def far_half_kernel(scalar_ref, *refs, depth, width, pencils):
    far = [k for k in range(len(OFFSETS)) if OFFSETS[k] >= 4]
    blocks = refs[: len(far)]
    early_refs = refs[len(far) : len(far) + 2]
    late_refs = refs[len(far) + 2 : len(far) + 4]
    faces_ref, pn_ref, sn_ref, qn_ref = refs[len(far) + 4 : len(far) + 8]
    s_ref, q_ref, u_ref, coarse_ref = refs[len(far) + 8 : len(far) + 12]
    p_ref, f_ref = refs[len(far) + 12 :]
    slab = scalar_ref[0]
    pencil = scalar_ref[1]
    part = width // 2
    half = 4 * depth
    planes = 2 * half
    lower = slab < 4
    near_first = jnp.where(lower, 0, half)
    far_first = half - near_first
    is_even = (pencil % 2) == 0
    low_half = row_iota((8, LANES)) < 4
    mask = halo_mask(pencil, pencils)
    blank = jnp.zeros(p_ref.shape[1:], jnp.float32)
    for ref in (q_ref, u_ref):
        for z in (0, 1, planes + 2, planes + 3):
            ref[z] = blank
    p_ref[jnp.where(lower, half + 1, 0)] = blank
    p_ref[jnp.where(lower, 0, half + 1)] = pn_ref[jnp.where(lower, half, 1)]
    for k, ref in zip(far, blocks):
        at = ((slab ^ OFFSETS[k]) % 4) * depth + 1
        early = k < EARLY
        tile = 2 * depth * (k if early else k - EARLY)
        edge_refs = early_refs if early else late_refs
        fill_block(p_ref, at, ref, edge_refs, tile, pencil, depth, part)
    face_tile = 2 * depth * (len(OFFSETS) - EARLY)
    first, second = halo_tiles(*late_refs, face_tile, is_even, low_half)
    f_ref[0, pl.ds(0, part), :] = faces_ref[pl.ds(0, part), :]
    f_ref[0, pl.ds(part, 8), :] = first
    f_ref[1, pl.ds(0, part), :] = faces_ref[pl.ds(part, part), :]
    f_ref[1, pl.ds(part, 8), :] = second

    def finish(source, z):
        for c in range(4):
            face = face_part(f_ref[c >> 1], c, z, planes)
            put(q_ref, z + 2, c, W * (face - source[c]), mask)

    def copy(j, carry):
        z = near_first + j
        for c in range(4):
            face = face_part(f_ref[c >> 1, pl.ds(part, 8), :], c, z, planes)
            q_ref[z + 2, c, pl.ds(0, part), :] = qn_ref[j, c, pl.ds(0, part), :]
            q_ref[z + 2, c, pl.ds(part, 8), :] = (
                qn_ref[j, c, pl.ds(part, 8), :] + (W * mask) * face
            )
        return carry

    lax.fori_loop(0, half, copy, 0, unroll=UNROLL)

    def body(j, carry):
        source = hessian_parts(parts(p_ref, j), parts(p_ref, j + 1), parts(p_ref, j + 2))
        finish(source, far_first + j)
        return carry

    lax.fori_loop(0, half, body, 0, unroll=HESS)
    seam = jnp.where(lower, half, 1)
    here = parts(pn_ref, seam)
    inner = parts(pn_ref, jnp.where(lower, half - 1, 2))
    outer = parts(p_ref, jnp.where(lower, 1, half))
    below = [jnp.where(lower, a, b) for a, b in zip(inner, outer)]
    above = [jnp.where(lower, b, a) for a, b in zip(inner, outer)]
    source = hessian_parts(below, here, above)
    finish(source, near_first + seam - 1)
    own = (slab % 4) * depth
    for z in range(depth):
        is_seam = own + z == seam - 1
        for c in range(4):
            s_ref[z, c] = jnp.where(is_seam, source[c][:part], sn_ref[own + z, c])
    def second_sweep(z, carry):
        here = parts(q_ref, z + 2)
        for c in range(4):
            sides = neighbours(q_ref[z + 1, c], here, q_ref[z + 3, c], c)
            put(u_ref, z + 2, c, (1.0 + KEEP) * here[c] + W * sides, mask)
        return carry

    lax.fori_loop(0, planes, second_sweep, 0, unroll=UNROLL)
    restrict_window(u_ref, q_ref, coarse_ref, planes, part)


def restrict_window(u_ref, q_ref, coarse_ref, planes, part):
    def restrict(z, carry):
        total = None
        for at in (2 * z + 2, 2 * z + 3):
            here = parts(u_ref, at)
            for c in range(4):
                new = swept(u_ref[at - 1, c], here, u_ref[at + 1, c], q_ref[at, c], c)
                change = new[:part] - here[c][:part]
                total = change if total is None else total + change
        coarse_ref[pl.ds(pl.multiple_of(z * part, part), part), :] = 0.5 * total
        return carry

    lax.fori_loop(0, planes // 2, restrict, 0, unroll=PAIRS)


def between_kernel(scalar_ref, q_ref, u_ref, s_ref, source_hbm, swept_ref, *refs, pencils):
    left_ref, right_ref, source_ref, sem = refs
    depth, width, _ = source_ref.shape
    planes = q_ref.shape[0] - 4
    mask = halo_mask(scalar_ref[1], pencils)
    join_planes(lambda z, c: s_ref[z, c], source_ref, left_ref, right_ref, depth, width)
    copy_out = pltpu.make_async_copy(source_ref, source_hbm, sem)
    copy_out.start()

    def sweep(z, carry):
        here = parts(u_ref, z + 2)
        for c in range(4):
            new = swept(u_ref[z + 1, c], here, u_ref[z + 3, c], q_ref[z + 2, c], c)
            put(swept_ref, z + 2, c, new, mask)
        return carry

    lax.fori_loop(0, planes, sweep, 0, unroll=UNROLL)
    copy_out.wait()


def window_kernel(scalar_ref, qwin_ref, uwin_ref, win_ref, *, pencils):
    mask = halo_mask(scalar_ref[1], pencils)
    for z in range(win_ref.shape[0]):
        here = parts(uwin_ref, z + 1)
        for c in range(4):
            new = swept(uwin_ref[z, c], here, uwin_ref[z + 2, c], qwin_ref[z, c], c)
            put(win_ref, z, c, new, mask)


def coarse_window(v_ref, z, pencil, part):
    start = pl.multiple_of(pencil * part, part)
    own = v_ref[z, pl.ds(start + HALO, part), :]
    above = v_ref[z, pl.ds(start + HALO + part, 8), :]
    below = v_ref[z, pl.ds(start, 8), :]
    tile = jnp.where(row_iota((8, LANES)) < 4, above, below)
    return jnp.concatenate([own, tile], axis=0)


def middle_kernel(
    scalar_ref, c0_ref, c1_ref, c2_ref, c3_ref, q_ref, swept_ref,
    qwin_ref, uwin_ref, coarse_ref,
    v_ref, q1_ref, a1_ref, b1_ref, tmp_ref, a_ref, b_ref, *, depth, width, pencils, shape
):
    slab = scalar_ref[0]
    pencil = scalar_ref[1]
    planes = a_ref.shape[0] - 4
    part = width // 2
    mask = halo_mask(pencil, pencils)
    piece_refs = (c0_ref, c1_ref, c2_ref, c3_ref)
    solve_level_one(piece_refs, pencil, v_ref, q1_ref, a1_ref, b1_ref, tmp_ref, shape)
    blank = jnp.zeros(a_ref.shape[1:], jnp.float32)
    for ref in (a_ref, b_ref):
        for z in (0, 1, planes + 2, planes + 3):
            ref[z] = blank

    def third_sweep(z, carry):
        v = [coarse_window(v_ref, z + k, pencil, part) for k in range(3)]
        for k, children in enumerate(swept_children(*v)):
            at = 2 * z + 2 + k
            for c in range(4):
                put(a_ref, at, c, swept_ref[at, c] + children[c], mask)
        return carry

    lax.fori_loop(0, planes // 2, third_sweep, 0, unroll=PAIRS)

    def sweep(src, dst):
        def body(z, carry):
            here = parts(src, z + 2)
            for c in range(4):
                new = swept(src[z + 1, c], here, src[z + 3, c], q_ref[z + 2, c], c)
                put(dst, z + 2, c, new, mask)
            return carry

        lax.fori_loop(0, planes, body, 0, unroll=UNROLL)

    sweep(a_ref, b_ref)
    sweep(b_ref, a_ref)
    sweep(a_ref, b_ref)
    restrict_window(b_ref, q_ref, coarse_ref, planes, part)
    for z in range(depth + 2):
        qwin_ref[z] = q_ref[slab * depth + z + 1]
    for z in range(depth + 4):
        uwin_ref[z] = b_ref[slab * depth + z]


def last_kernel(
    scalar_ref, c0_ref, c1_ref, c2_ref, c3_ref, qwin_ref, win_ref, out_hbm,
    v_ref, q1_ref, a1_ref, b1_ref, tmp_ref, a_ref, left_ref, right_ref, out_ref, sems,
    *, depth, width, pencils, shape
):
    slab = scalar_ref[0]
    pencil = scalar_ref[1]
    planes = shape[0] * 2
    part = width // 2
    mask = halo_mask(pencil, pencils)
    piece_refs = (c0_ref, c1_ref, c2_ref, c3_ref)
    solve_level_one(piece_refs, pencil, v_ref, q1_ref, a1_ref, b1_ref, tmp_ref, shape, slab)
    blank = jnp.zeros((part + 8, LANES), jnp.float32)
    v = [coarse_window(v_ref, slab * (depth // 2) + k, pencil, part) for k in range(4)]
    v = [blank] + v + [blank]
    for k in range(4):
        for side, children in enumerate(swept_children(*v[k : k + 3])):
            z = 2 * k + side - 1
            if 0 <= z < depth + 2:
                at = slab * depth - 1 + z
                live = jnp.where((at >= 0) & (at < planes), 1.0, 0.0)
                for c in range(4):
                    put(a_ref, z, c, live * (win_ref[z, c] + children[c]), mask)
    matrix = merging_matrix()
    copies = []
    for z in range(depth):
        here = parts(a_ref, z + 1)
        for c in range(4):
            new = swept(a_ref[z, c], here, a_ref[z + 2, c], qwin_ref[z + 1, c], c)
            ref = right_ref if c & 1 else left_ref
            ref[z, pl.ds(c >> 1, part, stride=2), :] = new[:part]
        out_ref[z] = mm(jnp.concatenate([left_ref[z], right_ref[z]], axis=1), matrix)
        copies.append(pltpu.make_async_copy(out_ref.at[z], out_hbm.at[z], sems.at[z]))
        copies[-1].start()
    for copy in copies:
        copy.wait()


def vmem():
    return pl.BlockSpec(memory_space=pltpu.VMEM)


def smem():
    return pl.BlockSpec(memory_space=pltpu.SMEM)


def arr(*shape):
    return jax.ShapeDtypeStruct(shape, jnp.float32)


def buf(*shape):
    return pltpu.VMEM(shape, jnp.float32)


def call(kernel, name, scalars, args, outs, scratch=(), space=pltpu.VMEM, out_space=None):
    out_specs = jax.tree.map(lambda _: vmem(), outs)
    if out_space is not None:
        out_specs = tuple(pl.BlockSpec(memory_space=one) for one in out_space)
    return pl.pallas_call(
        kernel,
        out_shape=outs,
        in_specs=[smem()] * len(scalars) + [pl.BlockSpec(memory_space=space)] * len(args),
        out_specs=out_specs,
        scratch_shapes=list(scratch),
        compiler_params=pltpu.CompilerParams(vmem_limit_bytes=16 << 20),
        name=name,
    )(*scalars, *args)


def windowed(potential, parent_store, face_owner, face_offset):
    depth, width, columns = potential.shape
    slabs = lax.axis_size("slab")
    pencils = lax.axis_size("pencil")
    planes, height = slabs * depth, pencils * width
    part = width // 2
    rows = part + 8
    where = jnp.stack([lax.axis_index("slab"), lax.axis_index("pencil")]).astype(jnp.int32)
    scalars = jnp.concatenate([where, face_owner, face_offset])
    own = call(
        pack_kernel,
        "pack",
        [],
        [pltpu.with_memory_space_constraint(x, pltpu.HBM) for x in (potential, parent_store)],
        arr(depth * width * 2 + 8, LANES),
        [
            buf(depth * width, LANES),
            buf(depth * width, LANES),
            buf(*potential.shape),
            buf(*parent_store.shape),
            pltpu.SemaphoreType.DMA((2,)),
        ],
        space=pltpu.HBM,
    )

    def swap(x, bits):
        return lax.ppermute(x, "slab", [(i, i ^ bits) for i in range(slabs)])

    near = [swap(own, bits) for bits in OFFSETS[1:5]]
    blocks = [own, *near] + [swap(near[0], bits) for bits in OFFSETS[2:5]]
    low_pairs = [(i, i + 1) for i in range(0, pencils - 1, 2)]
    high_pairs = [(i, i + 1) for i in range(1, pencils - 1, 2)]

    def beside(even, odd):
        return (
            lax.ppermute(even, "pencil", low_pairs + [(j, i) for i, j in low_pairs]),
            lax.ppermute(odd, "pencil", high_pairs + [(j, i) for i, j in high_pairs]),
        )

    message = arr(2 * depth * EARLY, 8, LANES)
    early = call(
        partial(early_edges_kernel, depth=depth, width=width),
        "early_edges",
        [scalars],
        blocks[:EARLY],
        (message, message),
    )
    early = beside(*early)
    message = arr(2 * depth * (slabs - EARLY) + 1, 8, LANES)
    even, odd, faces = call(
        partial(late_edges_kernel, depth=depth, width=width),
        "late_edges",
        [scalars],
        blocks,
        (message, message, arr(width, LANES)),
        [buf(slabs, 8, LANES), buf(LANES, LANES)],
    )
    late = beside(even, odd)
    shape = (planes // 2, height // 2, columns // 2)
    coarse_part = arr(planes // 2 * part, LANES)
    field = (planes + 4, 4, rows, LANES)
    half = planes // 2
    near = call(
        partial(near_half_kernel, depth=depth, width=width, pencils=pencils),
        "near_half",
        [scalars],
        [b for b, offset in zip(blocks, OFFSETS) if offset < 4] + [*early, faces],
        (arr(half + 2, 4, rows, LANES), arr(half, 4, part, LANES), arr(half, 4, rows, LANES)),
    )
    own_source, q, u, coarse = call(
        partial(far_half_kernel, depth=depth, width=width, pencils=pencils),
        "far_half",
        [scalars],
        [b for b, offset in zip(blocks, OFFSETS) if offset >= 4] + [*early, *late, faces, *near],
        (arr(depth, 4, part, LANES), arr(*field), arr(*field), coarse_part),
        [buf(half + 2, 4, rows, LANES), buf(2, rows, LANES)],
    )

    def pair(x, bits):
        return lax.ppermute(x, "pencil", [(i, i ^ bits) for i in range(pencils)])

    def gather(x, meanwhile):
        beside, across = pair(x, 1), pair(x, 2)
        made = meanwhile()
        across, made = lax.optimization_barrier((across, made))
        return [x, beside, across, pair(across, 1)], made

    between = lambda: call(
        partial(between_kernel, pencils=pencils),
        "between",
        [scalars],
        [q, u, own_source],
        (arr(depth, width, columns), arr(*field)),
        [
            buf(depth * width, LANES),
            buf(depth * width, LANES),
            buf(depth, width, columns),
            pltpu.SemaphoreType.DMA,
        ],
        out_space=[pl.ANY, pltpu.VMEM],
    )
    pieces, (source, swept_once) = gather(coarse, between)
    level = (shape[0] + 4, 2, shape[1] // 2, LANES)
    level_scratch = [
        buf(shape[0] + 2, shape[1] + 2 * HALO, LANES),
        buf(*level),
        buf(*level),
        buf(*level),
        buf((shape[0] // 2 + 4) * shape[1] // 2, LANES),
    ]
    sizes = dict(depth=depth, width=width, pencils=pencils, shape=shape)
    qwin, uwin, coarse = call(
        partial(middle_kernel, **sizes),
        "middle",
        [scalars],
        [*pieces, q, swept_once],
        (arr(depth + 2, 4, rows, LANES), arr(depth + 4, 4, rows, LANES), coarse_part),
        level_scratch + [buf(*field), buf(*field)],
    )
    window = lambda: call(
        partial(window_kernel, pencils=pencils),
        "window",
        [scalars],
        [qwin, uwin],
        arr(depth + 2, 4, rows, LANES),
    )
    pieces, win = gather(coarse, window)
    (solved,) = call(
        partial(last_kernel, **sizes),
        "last",
        [scalars],
        [*pieces, qwin, win],
        (arr(depth, width, columns),),
        level_scratch
        + [
            buf(depth + 2, 4, rows, LANES),
            buf(depth, width, LANES),
            buf(depth, width, LANES),
            buf(depth, width, columns),
            pltpu.SemaphoreType.DMA((depth,)),
        ],
        out_space=[pl.ANY],
    )
    return solved, source


def fits_window(potential, parent_store):
    depth, width, columns = potential.shape
    slabs = lax.axis_size("slab")
    pencils = lax.axis_size("pencil")
    planes = slabs * depth
    return (
        slabs == 8
        and depth == 4
        and columns == 2 * LANES
        and width == 32
        and parent_store.shape[0] * width == LANES
        and 2 * planes < LANES
        and pencils == 4
    )


def padded(cells, sides, width):
    for axis, dim in sides:
        count = lax.axis_size(axis)
        ends = count - 1
        head = lax.slice_in_dim(cells, 0, width, axis=dim)
        tail = lax.slice_in_dim(cells, cells.shape[dim] - width, cells.shape[dim], axis=dim)
        cells = jnp.concatenate(
            [
                lax.ppermute(tail, axis, [(i, (i + 1) % count) for i in range(ends)]),
                cells,
                lax.ppermute(head, axis, [((i + 1) % count, i) for i in range(ends)]),
            ],
            axis=dim,
        )
    return cells


def hessian_source(p):
    c = p[1:-1, 1:-1, 1:-1]
    pxx = p[1:-1, 1:-1, 2:] + p[1:-1, 1:-1, :-2] - 2.0 * c
    pyy = p[1:-1, 2:, 1:-1] + p[1:-1, :-2, 1:-1] - 2.0 * c
    pzz = p[2:, 1:-1, 1:-1] + p[:-2, 1:-1, 1:-1] - 2.0 * c
    pxy = 0.25 * (p[1:-1, 2:, 2:] - p[1:-1, :-2, 2:] - p[1:-1, 2:, :-2] + p[1:-1, :-2, :-2])
    pxz = 0.25 * (p[2:, 1:-1, 2:] - p[:-2, 1:-1, 2:] - p[2:, 1:-1, :-2] + p[:-2, 1:-1, :-2])
    pyz = 0.25 * (p[2:, 2:, 1:-1] - p[:-2, 2:, 1:-1] - p[2:, :-2, 1:-1] + p[:-2, :-2, 1:-1])
    return pxx * pyy + pxx * pzz + pyy * pzz - pxy * pxy - pxz * pxz - pyz * pyz


def apply_padded(p, level):
    c = p[1:-1, 1:-1, 1:-1]
    near = p[2:, 1:-1, 1:-1] + p[:-2, 1:-1, 1:-1]
    near = near + p[1:-1, 2:, 1:-1] + p[1:-1, :-2, 1:-1]
    near = near + p[1:-1, 1:-1, 2:] + p[1:-1, 1:-1, :-2]
    return (6.0 * c - near) * 0.25**level


def step_weight(level):
    return OMEGA / 6.0 * 4.0**level


def sweep_whole(u, rhs, level):
    return u + step_weight(level) * (rhs - apply_padded(jnp.pad(u, 1), level))


def restrict(r):
    a, b, c = r.shape
    return r.reshape(a // 2, 2, b // 2, 2, c // 2, 2).mean(axis=(1, 3, 5))


def prolong(e):
    a, b, c = e.shape
    return jnp.broadcast_to(e[:, None, :, None, :, None], (a, 2, b, 2, c, 2)).reshape(
        2 * a, 2 * b, 2 * c
    )


def vcycle(u, rhs, level):
    if is_coarsest(rhs.shape):
        for sweep_count in range(8):
            u = sweep_whole(u, rhs, level)
        return u
    u = sweep_whole(u, rhs, level)
    u = sweep_whole(u, rhs, level)
    resid = rhs - apply_padded(jnp.pad(u, 1), level)
    coarse = restrict(resid)
    correction = vcycle(jnp.zeros_like(coarse), coarse, level + 1)
    u = u + prolong(correction)
    u = sweep_whole(u, rhs, level)
    u = sweep_whole(u, rhs, level)
    return u


def widen_x(p):
    return jnp.pad(p, ((0, 0), (0, 0), (1, 1)))


def rim_one(u):
    return widen_x(padded(u, (("slab", 0), ("pencil", 1)), 1))


def coarse_solve(rhs, level):
    width = rhs.shape[1]
    columns = rhs.shape[2]
    whole = lax.all_gather(rhs, ("slab", "pencil"), axis=0, tiled=True)
    whole = whole.reshape(lax.axis_size("slab"), lax.axis_size("pencil") * width, columns)
    solved = vcycle(jnp.zeros_like(whole), whole, level)
    start_y = lax.axis_index("pencil") * width
    return lax.dynamic_slice(
        solved, (lax.axis_index("slab"), start_y, jnp.int32(0)), (1, width, columns)
    )


def split_vcycle(u, rhs, level, from_zero):
    if rhs.shape[0] == 1:
        return coarse_solve(rhs, level)
    weight = step_weight(level)
    if from_zero:
        u = weight * rhs
    else:
        u = u + weight * (rhs - apply_padded(rim_one(u), level))
    u = u + weight * (rhs - apply_padded(rim_one(u), level))
    resid = rhs - apply_padded(rim_one(u), level)
    correction = split_vcycle(None, restrict(resid), level + 1, True)
    u = u + prolong(correction)
    u = u + weight * (rhs - apply_padded(rim_one(u), level))
    u = u + weight * (rhs - apply_padded(rim_one(u), level))
    return u


def plain(potential, parent_store, face_owner, face_offset):
    depth, width, columns = potential.shape
    grown = widen_x(padded(potential, (("slab", 0), ("pencil", 1)), 1))
    source = hessian_source(grown)
    slab_index = lax.axis_index("slab")
    wanted = face_owner[slab_index] * parent_store.shape[0] + face_offset[slab_index]
    piece = lax.all_gather(parent_store, "slab", axis=0, tiled=True)
    labels = jnp.arange(piece.shape[0], dtype=jnp.int32)
    match = labels == wanted
    faces = jnp.sum(jnp.where(match[:, None, None, None], piece, 0.0), axis=0)
    rhs = -source
    rhs = rhs.at[:, :, 0].add(faces[0])
    rhs = rhs.at[:, :, columns - 1].add(faces[1])
    solved = jnp.zeros_like(rhs)
    for cycle in range(CYCLES):
        solved = split_vcycle(solved, rhs, 0, cycle == 0)
    return (solved, source)


def on_device(potential, parent_store, face_owner, face_offset):
    if fits_window(potential, parent_store):
        return windowed(potential, parent_store, face_owner, face_offset)
    return plain(potential, parent_store, face_owner, face_offset)


def solution(mesh):
    in_specs = (P("slab", "pencil", None), P("slab", None, None, "pencil"), P(), P())
    out_specs = (P("slab", "pencil", None), P("slab", "pencil", None))
    return jax.shard_map(
        on_device, mesh=mesh, in_specs=in_specs, out_specs=out_specs, check_vma=False
    )
```

```python
from functools import partial

import jax
import jax.numpy as jnp
import numpy as np
from jax import lax
from jax.experimental import pallas as pl
from jax.experimental.pallas import tpu as pltpu
from jax.sharding import PartitionSpec as P

CYCLES = 2
OMEGA = 0.8
W = float(np.float32(OMEGA / 6.0))
KEEP = 1.0 - 6.0 * W
HALO = 8
LANES = 128
UNROLL = 16
PAIRS = 16
HESS = 16
LEVEL = 16
LPAIRS = 4


def is_coarsest(shape):
    return min(shape) <= 4 or any((d % 2 for d in shape))


def lane_iota(shape):
    return lax.broadcasted_iota(jnp.int32, shape, len(shape) - 1)


def row_iota(shape):
    return lax.broadcasted_iota(jnp.int32, shape, len(shape) - 2)


def x_other(values, odd):
    lane = lane_iota(values.shape)
    if odd:
        return jnp.where(lane == LANES - 1, 0.0, pltpu.roll(values, LANES - 1, 1))
    return jnp.where(lane == 0, 0.0, pltpu.roll(values, 1, 1))


def y_other(values, odd):
    return pltpu.roll(values, values.shape[0] - 1 if odd else 1, 0)


def neighbours(below, here, above, c):
    across, along = here[c ^ 1], here[c ^ 2]
    near = (below + above) + (across + x_other(across, c & 1))
    return near + (along + y_other(along, c >> 1))


def swept(below, here, above, q, c):
    return KEEP * here[c] + W * neighbours(below, here, above, c) + q


def swept_children(below, here, above):
    here = W * here
    base = ((1.0 - 3.0 * W) / W) * here
    beyond = [W * below, W * above]
    across = [base + x_other(here, odd) for odd in range(2)]
    along = [y_other(here, odd) for odd in range(2)]
    flat = [across[c & 1] + along[c >> 1] for c in range(4)]
    return [[one + beyond[k] for one in flat] for k in range(2)]


def parts(ref, z):
    return [ref[z, c] for c in range(4)]


def halo_mask(pencil, pencils):
    row = row_iota((8, LANES))
    above = jnp.where(pencil < pencils - 1, 1.0, 0.0)
    below = jnp.where(pencil > 0, 1.0, 0.0)
    return jnp.where(row < 4, above, below)


def put(ref, z, c, values, mask):
    own = values.shape[0] - 8
    ref[z, c, pl.ds(0, own), :] = values[:own]
    ref[z, c, pl.ds(own, 8), :] = values[own:] * mask


def index_pair(rows, columns):
    return (
        lax.broadcasted_iota(jnp.int32, (rows, columns), 0),
        lax.broadcasted_iota(jnp.int32, (rows, columns), 1),
    )


def chosen(where, value):
    return jnp.where(where, value, 0.0).astype(jnp.bfloat16)


def splitting_matrix():
    i, j = index_pair(2 * LANES, 2 * LANES)
    return chosen(i == 2 * (j & (LANES - 1)) + (j >= LANES).astype(jnp.int32), 1.0)


def merging_matrix():
    i, j = index_pair(2 * LANES, 2 * LANES)
    return chosen(j == 2 * (i & (LANES - 1)) + (i >= LANES).astype(jnp.int32), 1.0)


def mm(a, b):
    high = a.astype(jnp.bfloat16)
    rest = a - high.astype(jnp.float32)
    middle = rest.astype(jnp.bfloat16)
    low = (rest - middle.astype(jnp.float32)).astype(jnp.bfloat16)

    def dot(x):
        return jnp.dot(x, b, preferred_element_type=jnp.float32)

    return dot(high) + (dot(middle) + dot(low))


def pair_sum(values, distance, axis):
    size = values.shape[axis]
    at = lax.broadcasted_iota(jnp.int32, values.shape, axis)
    ahead = pltpu.roll(values, size - distance, axis)
    behind = pltpu.roll(values, distance, axis)
    return values + jnp.where((at & distance) == 0, ahead, behind)


def x_sides(values, distance):
    lane = lane_iota(values.shape)
    left = jnp.where(lane < distance, 0.0, pltpu.roll(values, distance, 1))
    right = jnp.where(lane >= LANES - distance, 0.0, pltpu.roll(values, LANES - distance, 1))
    return left + right


def flat_sweep(u, q, rows, yd, xd):
    total = u.shape[0]
    zero = jnp.zeros((rows, LANES), jnp.float32)
    below = jnp.concatenate([zero, u[: total - rows]], axis=0)
    above = jnp.concatenate([u[rows:], zero], axis=0)
    y = row_iota(u.shape) & (rows - 1)
    down = jnp.where(y < yd, 0.0, pltpu.roll(u, yd, 0))
    up = jnp.where(y >= rows - yd, 0.0, pltpu.roll(u, total - yd, 0))
    return KEEP * u + W * ((below + above) + (down + up) + x_sides(u, xd)) + q


def flat_vcycle(q, shape, rows, yd, xd):
    if is_coarsest(shape):
        u = q
        for _ in range(7):
            u = flat_sweep(u, q, rows, yd, xd)
        return u
    zs, ys, xs = shape
    u = flat_sweep(q, q, rows, yd, xd)
    change = flat_sweep(u, q, rows, yd, xd) - u
    pairs = [
        change[2 * z * rows : (2 * z + 1) * rows] + change[(2 * z + 1) * rows : (2 * z + 2) * rows]
        for z in range(zs // 2)
    ]
    coarse = 0.5 * pair_sum(pair_sum(jnp.concatenate(pairs, axis=0), yd, 0), xd, 1)
    e = flat_vcycle(coarse, (zs // 2, ys // 2, xs // 2), rows, 2 * yd, 2 * xd)
    planes = []
    for z in range(zs // 2):
        planes += [e[z * rows : (z + 1) * rows]] * 2
    u = u + jnp.concatenate(planes, axis=0)
    u = flat_sweep(u, q, rows, yd, xd)
    return flat_sweep(u, q, rows, yd, xd)


def solve_level_one(piece_refs, pencil, v_ref, q_ref, a_ref, b_ref, tmp_ref, shape, near=None):
    zs, ys, xs = shape
    rows = ys // 2
    half = zs // 2
    piece = rows // len(piece_refs)
    row = row_iota((rows, LANES))
    blank = jnp.zeros((rows, LANES), jnp.float32)
    for ref in (q_ref, a_ref, b_ref):
        for z in (0, 1, zs + 2, zs + 3):
            for c in range(2):
                ref[z, c] = blank
    for z in (0, 1, half + 2, half + 3):
        tmp_ref[pl.ds(z * rows, rows), :] = blank
    edge = jnp.zeros((HALO, LANES), jnp.float32)
    for z in range(zs + 2):
        v_ref[z, pl.ds(0, HALO), :] = edge
        v_ref[z, pl.ds(HALO + ys, HALO), :] = edge
    if near is None:
        for z in (0, zs + 1):
            for c in range(2):
                v_ref[z, pl.ds(HALO + c * rows, rows), :] = blank
    for z in range(zs):
        for c in range(2):
            for k, ref in enumerate(piece_refs):
                spot = pl.ds(2 * piece * z + c, piece, stride=2)
                to = pl.ds(pl.multiple_of((pencil ^ k) * piece, piece), piece)
                q_ref[z + 2, c, to, :] = ref[spot, :]

    def y_beyond(other, c):
        if c:
            return jnp.where(row == rows - 1, 0.0, pltpu.roll(other, rows - 1, 0))
        return jnp.where(row == 0, 0.0, pltpu.roll(other, 1, 0))

    def around(src, z):
        here = [src[z, 0], src[z, 1]]
        near = []
        for c in range(2):
            other = here[1 - c]
            sides = (other + y_beyond(other, c)) + x_sides(here[c], 1)
            near.append((src[z - 1, c] + src[z + 1, c]) + sides)
        return here, near

    def second(z, carry):
        here, sides = around(q_ref, z)
        for c in range(2):
            a_ref[z, c] = (1.0 + KEEP) * here[c] + W * sides[c]
        return carry

    lax.fori_loop(2, zs + 2, second, 0, unroll=LEVEL)

    def restrict(z, carry):
        total = None
        for at in (2 * z + 2, 2 * z + 3):
            here, sides = around(a_ref, at)
            for c in range(2):
                new = KEEP * here[c] + W * sides[c] + q_ref[at, c]
                b_ref[at, c] = new
                change = new - here[c]
                total = change if total is None else total + change
        spot = pl.ds(pl.multiple_of((z + 2) * rows, rows), rows)
        tmp_ref[spot, :] = 0.5 * pair_sum(total, 1, 1)
        return carry

    pairs_unroll = LPAIRS if near is None else half
    lax.fori_loop(0, half, restrict, 0, unroll=pairs_unroll)
    inner = pl.ds(2 * rows, half * rows)
    tmp_ref[inner, :] = flat_vcycle(tmp_ref[inner, :], (half, ys // 2, xs // 2), rows, 1, 2)

    def live(at, count):
        return jnp.where((at >= 0) & (at < count), 1.0, 0.0)

    def third(z):
        e = [tmp_ref[pl.ds(pl.multiple_of((z + k) * rows, rows), rows), :] for k in (1, 2, 3)]
        here = W * e[1]
        base = ((1.0 - 4.0 * W) / W) * here + x_sides(here, 1)
        for c in range(2):
            flat = base + y_beyond(here, c)
            for k in range(2):
                new = b_ref[2 * z + 2 + k, c] + (flat + W * e[2 * k])
                a_ref[2 * z + 2 + k, c] = new if near is None else live(z, half) * new

    def fourth(z):
        here, sides = around(a_ref, z + 2)
        for c in range(2):
            new = KEEP * here[c] + W * sides[c] + q_ref[z + 2, c]
            if near is not None:
                new = live(z, zs) * new
            v_ref[z + 1, pl.ds(HALO + c, rows, stride=2), :] = new

    def loop(step, start, count, unroll):
        def body(i, carry):
            step(start + i)
            return carry

        lax.fori_loop(0, count, body, 0, unroll=unroll)

    if near is None:
        loop(third, 0, half, LPAIRS)
        loop(fourth, 0, zs, LEVEL)
    else:
        loop(third, near - 1, 3, 3)
        loop(fourth, 2 * near - 1, 4, 4)


def pack_kernel(
    potential_hbm, store_hbm, out_ref, even_ref, odd_ref, potential_ref, store_ref, sems
):
    copies = [
        pltpu.make_async_copy(potential_hbm, potential_ref, sems.at[0]),
        pltpu.make_async_copy(store_hbm, store_ref, sems.at[1]),
    ]
    for copy in copies:
        copy.start()
    matrix = splitting_matrix()
    for copy in copies:
        copy.wait()
    depth, width, columns = potential_ref.shape
    slots = store_ref.shape[0]
    part = width // 2
    split = mm(potential_ref[...].reshape(depth * width, columns), matrix)
    even_ref[...] = split[:, :LANES]
    odd_ref[...] = split[:, LANES:]
    for z in range(depth):
        for c in range(4):
            ref = odd_ref if c & 1 else even_ref
            spot = pl.ds((4 * z + c) * part, part)
            out_ref[spot, :] = ref[pl.ds(z * width + (c >> 1), part, stride=2), :]
    base = depth * width * 2
    for slot in range(slots):
        for side in range(2):
            spot = pl.ds(base + side * depth, depth)
            out_ref[spot, pl.ds(slot * width, width)] = store_ref[slot, side]


OFFSETS = (0, 4, 3, 1, 2, 7, 5, 6)
EARLY = 5


def block_rows(ref, start, count):
    return ref[pl.ds(start, count), :]


def ends(load, first, second, part, low_half):
    head = jnp.where(low_half, load(first, 8), pltpu.roll(load(second, 8), 4, 0))
    tail = jnp.where(
        low_half, pltpu.roll(load(first + part - 8, 8), 4, 0), load(second + part - 8, 8)
    )
    return head, tail


def store_ends(ref, pencil, out_refs, at, depth, part):
    even_ref, odd_ref = out_refs
    is_even = (pencil % 2) == 0
    low_half = row_iota((8, LANES)) < 4
    for z in range(depth):
        for t in range(2):
            head, tail = ends(
                partial(block_rows, ref),
                (4 * z + 2 * t) * part, (4 * z + 2 * t + 1) * part, part, low_half,
            )
            even_ref[at + 2 * z + t] = jnp.where(is_even, tail, head)
            odd_ref[at + 2 * z + t] = jnp.where(is_even, head, tail)


def early_edges_kernel(scalar_ref, *refs, depth, width):
    blocks, out_refs = refs[:EARLY], refs[EARLY:]
    for k, ref in enumerate(blocks):
        store_ends(ref, scalar_ref[1], out_refs, 2 * depth * k, depth, width // 2)


def late_edges_kernel(scalar_ref, *refs, depth, width):
    slabs = len(OFFSETS)
    even_ref, odd_ref, faces_ref, store_ref, rows_ref = refs[slabs:]
    slab = scalar_ref[0]
    pencil = scalar_ref[1]
    planes = slabs * depth
    part = width // 2
    is_even = (pencil % 2) == 0
    low_half = row_iota((8, LANES)) < 4
    base = depth * width * 2
    late = refs[EARLY:slabs]
    for k, ref in enumerate(late):
        store_ends(ref, pencil, (even_ref, odd_ref), 2 * depth * k, depth, part)
    for offset, ref in zip(OFFSETS, refs):
        store_ref[slab ^ offset] = block_rows(ref, base, 8)
    rest = LANES - 2 * planes
    rows_ref[pl.ds(2 * planes, rest), :] = jnp.zeros((rest, LANES), jnp.float32)
    for s in range(slabs):
        tile = store_ref[scalar_ref[2 + s]]
        slot = scalar_ref[2 + slabs + s]
        picked = pltpu.roll(tile, (LANES - slot * width) & (LANES - 1), 1)
        rows_ref[pl.ds(s * depth, depth), :] = picked[:depth]
        rows_ref[pl.ds(planes + s * depth, depth), :] = picked[depth:]
    rows_ref[...] = rows_ref[...].T
    faces_ref[pl.ds(0, part), :] = rows_ref[pl.ds(0, part, stride=2), :]
    faces_ref[pl.ds(part, part), :] = rows_ref[pl.ds(1, part, stride=2), :]
    head, tail = ends(partial(block_rows, faces_ref), 0, part, part, low_half)
    even_ref[2 * depth * len(late)] = jnp.where(is_even, tail, head)
    odd_ref[2 * depth * len(late)] = jnp.where(is_even, head, tail)


def halo_tiles(even_ref, odd_ref, index, is_even, low_half):
    first = even_ref[index]
    second = odd_ref[index]
    above = jnp.where(is_even, first, second)
    below = jnp.where(is_even, second, first)
    return (
        jnp.where(low_half, above, pltpu.roll(below, 4, 0)),
        jnp.where(low_half, pltpu.roll(above, 4, 0), below),
    )


def join_planes(load, out_ref, left_ref, right_ref, depth, width):
    part = width // 2
    for z in range(depth):
        for c in range(4):
            ref = right_ref if c & 1 else left_ref
            ref[pl.ds(z * width + (c >> 1), part, stride=2), :] = load(z, c)
    rows = depth * width
    both = jnp.concatenate([left_ref[pl.ds(0, rows), :], right_ref[pl.ds(0, rows), :]], axis=1)
    out_ref[...] = mm(both, merging_matrix()).reshape(depth, width, 2 * LANES)


def hessian_parts(below, here, above):
    rise = [a - b for a, b in zip(above, below)]
    y_sum, y_rise, yz_rise = [], [], []
    for c in range(4):
        odd = c >> 1
        same, other = here[c ^ 2], y_other(here[c ^ 2], odd)
        y_sum.append(same + other)
        y_rise.append(other - same if odd else same - other)
        same, other = rise[c ^ 2], y_other(rise[c ^ 2], odd)
        yz_rise.append(other - same if odd else same - other)
    out = []
    for c in range(4):
        odd = c & 1
        same, other = here[c ^ 1], x_other(here[c ^ 1], odd)
        twice = 2.0 * here[c]
        pxx = same + other - twice
        pyy = y_sum[c] - twice
        pzz = below[c] + above[c] - twice
        same, other = rise[c ^ 1], x_other(rise[c ^ 1], odd)
        pxz = other - same if odd else same - other
        same, other = y_rise[c ^ 1], x_other(y_rise[c ^ 1], odd)
        pxy = other - same if odd else same - other
        cross = pxy * pxy + pxz * pxz + yz_rise[c] * yz_rise[c]
        out.append(pxx * pyy + (pxx + pyy) * pzz - 0.0625 * cross)
    return out


def face_part(face, c, z, planes):
    lane = lane_iota(face.shape)
    if c & 1:
        turned = pltpu.roll(face, LANES - 1 - planes - z, 1)
        return jnp.where(lane == LANES - 1, turned, 0.0)
    turned = pltpu.roll(face, (LANES - z) & (LANES - 1), 1)
    return jnp.where(lane == 0, turned, 0.0)


def fill_rows(p_ref, at, ref, depth, part):
    for z in range(depth):
        for c in range(4):
            p_ref[at + z, c, pl.ds(0, part), :] = block_rows(ref, (4 * z + c) * part, part)


def fill_halo(p_ref, at, edge_refs, tile, pencil, depth, part):
    is_even = (pencil % 2) == 0
    low_half = row_iota((8, LANES)) < 4
    for z in range(depth):
        for t in range(2):
            first, second = halo_tiles(*edge_refs, tile + 2 * z + t, is_even, low_half)
            p_ref[at + z, 2 * t, pl.ds(part, 8), :] = first
            p_ref[at + z, 2 * t + 1, pl.ds(part, 8), :] = second


def near_half_kernel(scalar_ref, *refs, depth, width, pencils):
    near = [k for k in range(EARLY) if OFFSETS[k] < 4]
    even_ref, odd_ref, faces_ref, p_ref, s_ref, q_ref, far_ref = refs[len(OFFSETS) :]
    slab = scalar_ref[0]
    pencil = scalar_ref[1]
    part = width // 2
    half = 4 * depth
    first_plane = (slab // 4) * half
    mask = halo_mask(pencil, pencils)
    blank = jnp.zeros(p_ref.shape[1:], jnp.float32)
    p_ref[0] = blank
    p_ref[half + 1] = blank
    for k, ref in enumerate(refs[: len(OFFSETS)]):
        at = ((slab ^ OFFSETS[k]) % 4) * depth + 1
        fill_rows(p_ref if k in near else far_ref, at, ref, depth, part)
        if k in near:
            fill_halo(p_ref, at, (even_ref, odd_ref), 2 * depth * k, pencil, depth, part)

    def body(j, carry):
        source = hessian_parts(parts(p_ref, j), parts(p_ref, j + 1), parts(p_ref, j + 2))
        for c in range(4):
            s_ref[j, c] = source[c][:part]
            face = faces_ref[pl.ds((c >> 1) * part, part), :]
            face = face_part(face, c, first_plane + j, 2 * half)
            at = first_plane + j + 2
            q_ref[at, c, pl.ds(0, part), :] = W * (face - source[c][:part])
            q_ref[at, c, pl.ds(part, 8), :] = (-W * mask) * source[c][part:]
        return carry

    lax.fori_loop(0, half, body, 0, unroll=HESS)


def far_half_kernel(scalar_ref, *refs, depth, width, pencils):
    far = [k for k in range(len(OFFSETS)) if OFFSETS[k] >= 4]
    early_refs, late_refs = refs[:2], refs[2:4]
    faces_ref, pn_ref, sn_ref = refs[4:7]
    s_ref, q_ref, u_ref, coarse_ref, p_ref, f_ref = refs[9:]
    slab = scalar_ref[0]
    pencil = scalar_ref[1]
    part = width // 2
    half = 4 * depth
    planes = 2 * half
    lower = slab < 4
    near_first = jnp.where(lower, 0, half)
    far_first = half - near_first
    is_even = (pencil % 2) == 0
    low_half = row_iota((8, LANES)) < 4
    mask = halo_mask(pencil, pencils)
    blank = jnp.zeros(p_ref.shape[1:], jnp.float32)
    for ref in (q_ref, u_ref):
        for z in (0, 1, planes + 2, planes + 3):
            ref[z] = blank
    p_ref[jnp.where(lower, half + 1, 0)] = blank
    p_ref[jnp.where(lower, 0, half + 1)] = pn_ref[jnp.where(lower, half, 1)]
    for k in far:
        at = ((slab ^ OFFSETS[k]) % 4) * depth + 1
        early = k < EARLY
        tile = 2 * depth * (k if early else k - EARLY)
        edge_refs = early_refs if early else late_refs
        fill_halo(p_ref, at, edge_refs, tile, pencil, depth, part)
    face_tile = 2 * depth * (len(OFFSETS) - EARLY)
    first, second = halo_tiles(*late_refs, face_tile, is_even, low_half)
    f_ref[0, pl.ds(0, part), :] = faces_ref[pl.ds(0, part), :]
    f_ref[0, pl.ds(part, 8), :] = first
    f_ref[1, pl.ds(0, part), :] = faces_ref[pl.ds(part, part), :]
    f_ref[1, pl.ds(part, 8), :] = second

    def finish(source, z):
        for c in range(4):
            face = face_part(f_ref[c >> 1], c, z, planes)
            put(q_ref, z + 2, c, W * (face - source[c]), mask)

    def copy(j, carry):
        z = near_first + j
        for c in range(4):
            face = face_part(f_ref[c >> 1, pl.ds(part, 8), :], c, z, planes)
            tile = pl.ds(part, 8)
            q_ref[z + 2, c, tile, :] = q_ref[z + 2, c, tile, :] + (W * mask) * face
        return carry

    lax.fori_loop(0, half, copy, 0, unroll=UNROLL)

    def body(j, carry):
        source = hessian_parts(parts(p_ref, j), parts(p_ref, j + 1), parts(p_ref, j + 2))
        finish(source, far_first + j)
        return carry

    lax.fori_loop(0, half, body, 0, unroll=HESS)
    seam = jnp.where(lower, half, 1)
    here = parts(pn_ref, seam)
    inner = parts(pn_ref, jnp.where(lower, half - 1, 2))
    outer = parts(p_ref, jnp.where(lower, 1, half))
    below = [jnp.where(lower, a, b) for a, b in zip(inner, outer)]
    above = [jnp.where(lower, b, a) for a, b in zip(inner, outer)]
    source = hessian_parts(below, here, above)
    finish(source, near_first + seam - 1)
    own = (slab % 4) * depth
    for z in range(depth):
        is_seam = own + z == seam - 1
        for c in range(4):
            s_ref[z, c] = jnp.where(is_seam, source[c][:part], sn_ref[own + z, c])
    def second_sweep(z, carry):
        here = parts(q_ref, z + 2)
        for c in range(4):
            sides = neighbours(q_ref[z + 1, c], here, q_ref[z + 3, c], c)
            put(u_ref, z + 2, c, (1.0 + KEEP) * here[c] + W * sides, mask)
        return carry

    lax.fori_loop(0, planes, second_sweep, 0, unroll=UNROLL)
    restrict_window(u_ref, q_ref, coarse_ref, planes, part)


def restrict_window(u_ref, q_ref, coarse_ref, planes, part):
    def restrict(z, carry):
        total = None
        for at in (2 * z + 2, 2 * z + 3):
            here = parts(u_ref, at)
            for c in range(4):
                new = swept(u_ref[at - 1, c], here, u_ref[at + 1, c], q_ref[at, c], c)
                change = new[:part] - here[c][:part]
                total = change if total is None else total + change
        coarse_ref[pl.ds(pl.multiple_of(z * part, part), part), :] = 0.5 * total
        return carry

    lax.fori_loop(0, planes // 2, restrict, 0, unroll=PAIRS)


def between_kernel(scalar_ref, q_ref, u_ref, s_ref, source_hbm, swept_ref, *refs, pencils):
    left_ref, right_ref, source_ref, sem = refs
    depth, width, _ = source_ref.shape
    planes = q_ref.shape[0] - 4
    mask = halo_mask(scalar_ref[1], pencils)
    join_planes(lambda z, c: s_ref[z, c], source_ref, left_ref, right_ref, depth, width)
    copy_out = pltpu.make_async_copy(source_ref, source_hbm, sem)
    copy_out.start()

    def sweep(z, carry):
        here = parts(u_ref, z + 2)
        for c in range(4):
            new = swept(u_ref[z + 1, c], here, u_ref[z + 3, c], q_ref[z + 2, c], c)
            put(swept_ref, z + 2, c, new, mask)
        return carry

    lax.fori_loop(0, planes, sweep, 0, unroll=UNROLL)
    copy_out.wait()


def window_kernel(scalar_ref, qwin_ref, uwin_ref, win_ref, *, pencils):
    mask = halo_mask(scalar_ref[1], pencils)
    for z in range(win_ref.shape[0]):
        here = parts(uwin_ref, z + 1)
        for c in range(4):
            new = swept(uwin_ref[z, c], here, uwin_ref[z + 2, c], qwin_ref[z, c], c)
            put(win_ref, z, c, new, mask)


def coarse_window(v_ref, z, pencil, part):
    start = pl.multiple_of(pencil * part, part)
    own = v_ref[z, pl.ds(start + HALO, part), :]
    above = v_ref[z, pl.ds(start + HALO + part, 8), :]
    below = v_ref[z, pl.ds(start, 8), :]
    tile = jnp.where(row_iota((8, LANES)) < 4, above, below)
    return jnp.concatenate([own, tile], axis=0)


def middle_kernel(
    scalar_ref, c0_ref, c1_ref, c2_ref, c3_ref, q_ref, swept_ref,
    qwin_ref, uwin_ref, coarse_ref,
    v_ref, q1_ref, a1_ref, b1_ref, tmp_ref, a_ref, b_ref, *, depth, width, pencils, shape
):
    slab = scalar_ref[0]
    pencil = scalar_ref[1]
    planes = a_ref.shape[0] - 4
    part = width // 2
    mask = halo_mask(pencil, pencils)
    piece_refs = (c0_ref, c1_ref, c2_ref, c3_ref)
    solve_level_one(piece_refs, pencil, v_ref, q1_ref, a1_ref, b1_ref, tmp_ref, shape)
    blank = jnp.zeros(a_ref.shape[1:], jnp.float32)
    for ref in (a_ref, b_ref):
        for z in (0, 1, planes + 2, planes + 3):
            ref[z] = blank

    def third_sweep(z, carry):
        v = [coarse_window(v_ref, z + k, pencil, part) for k in range(3)]
        for k, children in enumerate(swept_children(*v)):
            at = 2 * z + 2 + k
            for c in range(4):
                put(a_ref, at, c, swept_ref[at, c] + children[c], mask)
        return carry

    lax.fori_loop(0, planes // 2, third_sweep, 0, unroll=PAIRS)

    def sweep(src, dst):
        def body(z, carry):
            here = parts(src, z + 2)
            for c in range(4):
                new = swept(src[z + 1, c], here, src[z + 3, c], q_ref[z + 2, c], c)
                put(dst, z + 2, c, new, mask)
            return carry

        lax.fori_loop(0, planes, body, 0, unroll=UNROLL)

    sweep(a_ref, b_ref)
    sweep(b_ref, a_ref)
    sweep(a_ref, b_ref)
    restrict_window(b_ref, q_ref, coarse_ref, planes, part)
    for z in range(depth + 2):
        qwin_ref[z] = q_ref[slab * depth + z + 1]
    for z in range(depth + 4):
        uwin_ref[z] = b_ref[slab * depth + z]


def last_kernel(
    scalar_ref, c0_ref, c1_ref, c2_ref, c3_ref, qwin_ref, win_ref, out_hbm,
    v_ref, q1_ref, a1_ref, b1_ref, tmp_ref, a_ref, left_ref, right_ref, out_ref, sems,
    *, depth, width, pencils, shape
):
    slab = scalar_ref[0]
    pencil = scalar_ref[1]
    planes = shape[0] * 2
    part = width // 2
    mask = halo_mask(pencil, pencils)
    piece_refs = (c0_ref, c1_ref, c2_ref, c3_ref)
    solve_level_one(piece_refs, pencil, v_ref, q1_ref, a1_ref, b1_ref, tmp_ref, shape, slab)
    blank = jnp.zeros((part + 8, LANES), jnp.float32)
    v = [coarse_window(v_ref, slab * (depth // 2) + k, pencil, part) for k in range(4)]
    v = [blank] + v + [blank]
    for k in range(4):
        for side, children in enumerate(swept_children(*v[k : k + 3])):
            z = 2 * k + side - 1
            if 0 <= z < depth + 2:
                at = slab * depth - 1 + z
                live = jnp.where((at >= 0) & (at < planes), 1.0, 0.0)
                for c in range(4):
                    put(a_ref, z, c, live * (win_ref[z, c] + children[c]), mask)
    matrix = merging_matrix()
    copies = []
    for z in range(depth):
        here = parts(a_ref, z + 1)
        for c in range(4):
            new = swept(a_ref[z, c], here, a_ref[z + 2, c], qwin_ref[z + 1, c], c)
            ref = right_ref if c & 1 else left_ref
            ref[z, pl.ds(c >> 1, part, stride=2), :] = new[:part]
        out_ref[z] = mm(jnp.concatenate([left_ref[z], right_ref[z]], axis=1), matrix)
        copies.append(pltpu.make_async_copy(out_ref.at[z], out_hbm.at[z], sems.at[z]))
        copies[-1].start()
    for copy in copies:
        copy.wait()


def vmem():
    return pl.BlockSpec(memory_space=pltpu.VMEM)


def smem():
    return pl.BlockSpec(memory_space=pltpu.SMEM)


def arr(*shape):
    return jax.ShapeDtypeStruct(shape, jnp.float32)


def buf(*shape):
    return pltpu.VMEM(shape, jnp.float32)


def call(kernel, name, scalars, args, outs, scratch=(), space=pltpu.VMEM, out_space=None, aliases={}):
    out_specs = jax.tree.map(lambda _: vmem(), outs)
    if out_space is not None:
        out_specs = tuple(pl.BlockSpec(memory_space=one) for one in out_space)
    return pl.pallas_call(
        kernel,
        out_shape=outs,
        in_specs=[smem()] * len(scalars) + [pl.BlockSpec(memory_space=space)] * len(args),
        out_specs=out_specs,
        scratch_shapes=list(scratch),
        compiler_params=pltpu.CompilerParams(vmem_limit_bytes=16 << 20),
        name=name,
        input_output_aliases=aliases,
    )(*scalars, *args)


def windowed(potential, parent_store, face_owner, face_offset):
    depth, width, columns = potential.shape
    slabs = lax.axis_size("slab")
    pencils = lax.axis_size("pencil")
    planes, height = slabs * depth, pencils * width
    part = width // 2
    rows = part + 8
    where = jnp.stack([lax.axis_index("slab"), lax.axis_index("pencil")]).astype(jnp.int32)
    scalars = jnp.concatenate([where, face_owner, face_offset])
    own = call(
        pack_kernel,
        "pack",
        [],
        [pltpu.with_memory_space_constraint(x, pltpu.HBM) for x in (potential, parent_store)],
        arr(depth * width * 2 + 8, LANES),
        [
            buf(depth * width, LANES),
            buf(depth * width, LANES),
            buf(*potential.shape),
            buf(*parent_store.shape),
            pltpu.SemaphoreType.DMA((2,)),
        ],
        space=pltpu.HBM,
    )

    def swap(x, bits):
        return lax.ppermute(x, "slab", [(i, i ^ bits) for i in range(slabs)])

    near = [swap(own, bits) for bits in OFFSETS[1:5]]
    blocks = [own, *near] + [swap(near[0], bits) for bits in OFFSETS[2:5]]
    low_pairs = [(i, i + 1) for i in range(0, pencils - 1, 2)]
    high_pairs = [(i, i + 1) for i in range(1, pencils - 1, 2)]

    def beside(even, odd):
        return (
            lax.ppermute(even, "pencil", low_pairs + [(j, i) for i, j in low_pairs]),
            lax.ppermute(odd, "pencil", high_pairs + [(j, i) for i, j in high_pairs]),
        )

    message = arr(2 * depth * EARLY, 8, LANES)
    early = call(
        partial(early_edges_kernel, depth=depth, width=width),
        "early_edges",
        [scalars],
        blocks[:EARLY],
        (message, message),
    )
    early = beside(*early)
    message = arr(2 * depth * (slabs - EARLY) + 1, 8, LANES)
    even, odd, faces = call(
        partial(late_edges_kernel, depth=depth, width=width),
        "late_edges",
        [scalars],
        blocks,
        (message, message, arr(width, LANES)),
        [buf(slabs, 8, LANES), buf(LANES, LANES)],
    )
    late = beside(even, odd)
    shape = (planes // 2, height // 2, columns // 2)
    coarse_part = arr(planes // 2 * part, LANES)
    field = (planes + 4, 4, rows, LANES)
    half = planes // 2
    near = call(
        partial(near_half_kernel, depth=depth, width=width, pencils=pencils),
        "near_half",
        [scalars],
        [*blocks, *early, faces],
        (
            arr(half + 2, 4, rows, LANES),
            arr(half, 4, part, LANES),
            arr(*field),
            arr(half + 2, 4, rows, LANES),
        ),
    )
    own_source, q, u, coarse, _ = call(
        partial(far_half_kernel, depth=depth, width=width, pencils=pencils),
        "far_half",
        [scalars],
        [*early, *late, faces, *near],
        (
            arr(depth, 4, part, LANES),
            arr(*field),
            arr(*field),
            coarse_part,
            arr(half + 2, 4, rows, LANES),
        ),
        [buf(2, rows, LANES)],
        aliases={8: 1, 9: 4},
    )

    def pair(x, bits):
        return lax.ppermute(x, "pencil", [(i, i ^ bits) for i in range(pencils)])

    def gather(x, meanwhile):
        beside, across = pair(x, 1), pair(x, 2)
        made = meanwhile()
        across, made = lax.optimization_barrier((across, made))
        return [x, beside, across, pair(across, 1)], made

    between = lambda: call(
        partial(between_kernel, pencils=pencils),
        "between",
        [scalars],
        [q, u, own_source],
        (arr(depth, width, columns), arr(*field)),
        [
            buf(depth * width, LANES),
            buf(depth * width, LANES),
            buf(depth, width, columns),
            pltpu.SemaphoreType.DMA,
        ],
        out_space=[pl.ANY, pltpu.VMEM],
    )
    pieces, (source, swept_once) = gather(coarse, between)
    level = (shape[0] + 4, 2, shape[1] // 2, LANES)
    level_scratch = [
        buf(shape[0] + 2, shape[1] + 2 * HALO, LANES),
        buf(*level),
        buf(*level),
        buf(*level),
        buf((shape[0] // 2 + 4) * shape[1] // 2, LANES),
    ]
    sizes = dict(depth=depth, width=width, pencils=pencils, shape=shape)
    qwin, uwin, coarse = call(
        partial(middle_kernel, **sizes),
        "middle",
        [scalars],
        [*pieces, q, swept_once],
        (arr(depth + 2, 4, rows, LANES), arr(depth + 4, 4, rows, LANES), coarse_part),
        level_scratch + [buf(*field), buf(*field)],
    )
    window = lambda: call(
        partial(window_kernel, pencils=pencils),
        "window",
        [scalars],
        [qwin, uwin],
        arr(depth + 2, 4, rows, LANES),
    )
    pieces, win = gather(coarse, window)
    (solved,) = call(
        partial(last_kernel, **sizes),
        "last",
        [scalars],
        [*pieces, qwin, win],
        (arr(depth, width, columns),),
        level_scratch
        + [
            buf(depth + 2, 4, rows, LANES),
            buf(depth, width, LANES),
            buf(depth, width, LANES),
            buf(depth, width, columns),
            pltpu.SemaphoreType.DMA((depth,)),
        ],
        out_space=[pl.ANY],
    )
    return solved, source


def fits_window(potential, parent_store):
    depth, width, columns = potential.shape
    slabs = lax.axis_size("slab")
    pencils = lax.axis_size("pencil")
    planes = slabs * depth
    return (
        slabs == 8
        and depth == 4
        and columns == 2 * LANES
        and width == 32
        and parent_store.shape[0] * width == LANES
        and 2 * planes < LANES
        and pencils == 4
    )


def padded(cells, sides, width):
    for axis, dim in sides:
        count = lax.axis_size(axis)
        ends = count - 1
        head = lax.slice_in_dim(cells, 0, width, axis=dim)
        tail = lax.slice_in_dim(cells, cells.shape[dim] - width, cells.shape[dim], axis=dim)
        cells = jnp.concatenate(
            [
                lax.ppermute(tail, axis, [(i, (i + 1) % count) for i in range(ends)]),
                cells,
                lax.ppermute(head, axis, [((i + 1) % count, i) for i in range(ends)]),
            ],
            axis=dim,
        )
    return cells


def hessian_source(p):
    c = p[1:-1, 1:-1, 1:-1]
    pxx = p[1:-1, 1:-1, 2:] + p[1:-1, 1:-1, :-2] - 2.0 * c
    pyy = p[1:-1, 2:, 1:-1] + p[1:-1, :-2, 1:-1] - 2.0 * c
    pzz = p[2:, 1:-1, 1:-1] + p[:-2, 1:-1, 1:-1] - 2.0 * c
    pxy = 0.25 * (p[1:-1, 2:, 2:] - p[1:-1, :-2, 2:] - p[1:-1, 2:, :-2] + p[1:-1, :-2, :-2])
    pxz = 0.25 * (p[2:, 1:-1, 2:] - p[:-2, 1:-1, 2:] - p[2:, 1:-1, :-2] + p[:-2, 1:-1, :-2])
    pyz = 0.25 * (p[2:, 2:, 1:-1] - p[:-2, 2:, 1:-1] - p[2:, :-2, 1:-1] + p[:-2, :-2, 1:-1])
    return pxx * pyy + pxx * pzz + pyy * pzz - pxy * pxy - pxz * pxz - pyz * pyz


def apply_padded(p, level):
    c = p[1:-1, 1:-1, 1:-1]
    near = p[2:, 1:-1, 1:-1] + p[:-2, 1:-1, 1:-1]
    near = near + p[1:-1, 2:, 1:-1] + p[1:-1, :-2, 1:-1]
    near = near + p[1:-1, 1:-1, 2:] + p[1:-1, 1:-1, :-2]
    return (6.0 * c - near) * 0.25**level


def step_weight(level):
    return OMEGA / 6.0 * 4.0**level


def sweep_whole(u, rhs, level):
    return u + step_weight(level) * (rhs - apply_padded(jnp.pad(u, 1), level))


def restrict(r):
    a, b, c = r.shape
    return r.reshape(a // 2, 2, b // 2, 2, c // 2, 2).mean(axis=(1, 3, 5))


def prolong(e):
    a, b, c = e.shape
    return jnp.broadcast_to(e[:, None, :, None, :, None], (a, 2, b, 2, c, 2)).reshape(
        2 * a, 2 * b, 2 * c
    )


def vcycle(u, rhs, level):
    if is_coarsest(rhs.shape):
        for sweep_count in range(8):
            u = sweep_whole(u, rhs, level)
        return u
    u = sweep_whole(u, rhs, level)
    u = sweep_whole(u, rhs, level)
    resid = rhs - apply_padded(jnp.pad(u, 1), level)
    coarse = restrict(resid)
    correction = vcycle(jnp.zeros_like(coarse), coarse, level + 1)
    u = u + prolong(correction)
    u = sweep_whole(u, rhs, level)
    u = sweep_whole(u, rhs, level)
    return u


def widen_x(p):
    return jnp.pad(p, ((0, 0), (0, 0), (1, 1)))


def rim_one(u):
    return widen_x(padded(u, (("slab", 0), ("pencil", 1)), 1))


def coarse_solve(rhs, level):
    width = rhs.shape[1]
    columns = rhs.shape[2]
    whole = lax.all_gather(rhs, ("slab", "pencil"), axis=0, tiled=True)
    whole = whole.reshape(lax.axis_size("slab"), lax.axis_size("pencil") * width, columns)
    solved = vcycle(jnp.zeros_like(whole), whole, level)
    start_y = lax.axis_index("pencil") * width
    return lax.dynamic_slice(
        solved, (lax.axis_index("slab"), start_y, jnp.int32(0)), (1, width, columns)
    )


def split_vcycle(u, rhs, level, from_zero):
    if rhs.shape[0] == 1:
        return coarse_solve(rhs, level)
    weight = step_weight(level)
    if from_zero:
        u = weight * rhs
    else:
        u = u + weight * (rhs - apply_padded(rim_one(u), level))
    u = u + weight * (rhs - apply_padded(rim_one(u), level))
    resid = rhs - apply_padded(rim_one(u), level)
    correction = split_vcycle(None, restrict(resid), level + 1, True)
    u = u + prolong(correction)
    u = u + weight * (rhs - apply_padded(rim_one(u), level))
    u = u + weight * (rhs - apply_padded(rim_one(u), level))
    return u


def plain(potential, parent_store, face_owner, face_offset):
    depth, width, columns = potential.shape
    grown = widen_x(padded(potential, (("slab", 0), ("pencil", 1)), 1))
    source = hessian_source(grown)
    slab_index = lax.axis_index("slab")
    wanted = face_owner[slab_index] * parent_store.shape[0] + face_offset[slab_index]
    piece = lax.all_gather(parent_store, "slab", axis=0, tiled=True)
    labels = jnp.arange(piece.shape[0], dtype=jnp.int32)
    match = labels == wanted
    faces = jnp.sum(jnp.where(match[:, None, None, None], piece, 0.0), axis=0)
    rhs = -source
    rhs = rhs.at[:, :, 0].add(faces[0])
    rhs = rhs.at[:, :, columns - 1].add(faces[1])
    solved = jnp.zeros_like(rhs)
    for cycle in range(CYCLES):
        solved = split_vcycle(solved, rhs, 0, cycle == 0)
    return (solved, source)


def on_device(potential, parent_store, face_owner, face_offset):
    if fits_window(potential, parent_store):
        return windowed(potential, parent_store, face_owner, face_offset)
    return plain(potential, parent_store, face_owner, face_offset)


def solution(mesh):
    in_specs = (P("slab", "pencil", None), P("slab", None, None, "pencil"), P(), P())
    out_specs = (P("slab", "pencil", None), P("slab", "pencil", None))
    return jax.shard_map(
        on_device, mesh=mesh, in_specs=in_specs, out_specs=out_specs, check_vma=False
    )
```

```python
from functools import partial

import jax
import jax.numpy as jnp
import numpy as np
from jax import lax
from jax.experimental import pallas as pl
from jax.experimental.pallas import tpu as pltpu
from jax.sharding import PartitionSpec as P

CYCLES = 2
OMEGA = 0.8
W = float(np.float32(OMEGA / 6.0))
KEEP = 1.0 - 6.0 * W
HALO = 8
LANES = 128
UNROLL = 16
PAIRS = 16
HESS = 16
LEVEL = 16
LPAIRS = 8


def is_coarsest(shape):
    return min(shape) <= 4 or any((d % 2 for d in shape))


def lane_iota(shape):
    return lax.broadcasted_iota(jnp.int32, shape, len(shape) - 1)


def row_iota(shape):
    return lax.broadcasted_iota(jnp.int32, shape, len(shape) - 2)


def x_other(values, odd):
    lane = lane_iota(values.shape)
    if odd:
        return jnp.where(lane == LANES - 1, 0.0, pltpu.roll(values, LANES - 1, 1))
    return jnp.where(lane == 0, 0.0, pltpu.roll(values, 1, 1))


def y_other(values, odd):
    return pltpu.roll(values, values.shape[0] - 1 if odd else 1, 0)


def neighbours(below, here, above, c):
    across, along = here[c ^ 1], here[c ^ 2]
    near = (below + above) + (across + x_other(across, c & 1))
    return near + (along + y_other(along, c >> 1))


def swept(below, here, above, q, c):
    return KEEP * here[c] + W * neighbours(below, here, above, c) + q


def swept_children(below, here, above):
    here = W * here
    base = ((1.0 - 3.0 * W) / W) * here
    beyond = [W * below, W * above]
    across = [base + x_other(here, odd) for odd in range(2)]
    along = [y_other(here, odd) for odd in range(2)]
    flat = [across[c & 1] + along[c >> 1] for c in range(4)]
    return [[one + beyond[k] for one in flat] for k in range(2)]


def parts(ref, z):
    return [ref[z, c] for c in range(4)]


def halo_mask(pencil, pencils):
    row = row_iota((8, LANES))
    above = jnp.where(pencil < pencils - 1, 1.0, 0.0)
    below = jnp.where(pencil > 0, 1.0, 0.0)
    return jnp.where(row < 4, above, below)


def put(ref, z, c, values, mask):
    own = values.shape[0] - 8
    ref[z, c, pl.ds(0, own), :] = values[:own]
    ref[z, c, pl.ds(own, 8), :] = values[own:] * mask


def index_pair(rows, columns):
    return (
        lax.broadcasted_iota(jnp.int32, (rows, columns), 0),
        lax.broadcasted_iota(jnp.int32, (rows, columns), 1),
    )


def chosen(where, value):
    return jnp.where(where, value, 0.0).astype(jnp.bfloat16)


def splitting_matrix():
    i, j = index_pair(2 * LANES, 2 * LANES)
    return chosen(i == 2 * (j & (LANES - 1)) + (j >= LANES).astype(jnp.int32), 1.0)


def merging_matrix():
    i, j = index_pair(2 * LANES, 2 * LANES)
    return chosen(j == 2 * (i & (LANES - 1)) + (i >= LANES).astype(jnp.int32), 1.0)


def mm(a, b):
    high = a.astype(jnp.bfloat16)
    rest = a - high.astype(jnp.float32)
    middle = rest.astype(jnp.bfloat16)
    low = (rest - middle.astype(jnp.float32)).astype(jnp.bfloat16)

    def dot(x):
        return jnp.dot(x, b, preferred_element_type=jnp.float32)

    return dot(high) + (dot(middle) + dot(low))


def pair_sum(values, distance, axis):
    size = values.shape[axis]
    at = lax.broadcasted_iota(jnp.int32, values.shape, axis)
    ahead = pltpu.roll(values, size - distance, axis)
    behind = pltpu.roll(values, distance, axis)
    return values + jnp.where((at & distance) == 0, ahead, behind)


def x_sides(values, distance):
    lane = lane_iota(values.shape)
    left = jnp.where(lane < distance, 0.0, pltpu.roll(values, distance, 1))
    right = jnp.where(lane >= LANES - distance, 0.0, pltpu.roll(values, LANES - distance, 1))
    return left + right


def flat_sweep(u, q, rows, yd, xd):
    total = u.shape[0]
    zero = jnp.zeros((rows, LANES), jnp.float32)
    below = jnp.concatenate([zero, u[: total - rows]], axis=0)
    above = jnp.concatenate([u[rows:], zero], axis=0)
    y = row_iota(u.shape) & (rows - 1)
    down = jnp.where(y < yd, 0.0, pltpu.roll(u, yd, 0))
    up = jnp.where(y >= rows - yd, 0.0, pltpu.roll(u, total - yd, 0))
    return KEEP * u + W * ((below + above) + (down + up) + x_sides(u, xd)) + q


def flat_vcycle(q, shape, rows, yd, xd):
    if is_coarsest(shape):
        u = q
        for _ in range(7):
            u = flat_sweep(u, q, rows, yd, xd)
        return u
    zs, ys, xs = shape
    u = flat_sweep(q, q, rows, yd, xd)
    change = flat_sweep(u, q, rows, yd, xd) - u
    pairs = [
        change[2 * z * rows : (2 * z + 1) * rows] + change[(2 * z + 1) * rows : (2 * z + 2) * rows]
        for z in range(zs // 2)
    ]
    coarse = 0.5 * pair_sum(pair_sum(jnp.concatenate(pairs, axis=0), yd, 0), xd, 1)
    e = flat_vcycle(coarse, (zs // 2, ys // 2, xs // 2), rows, 2 * yd, 2 * xd)
    planes = []
    for z in range(zs // 2):
        planes += [e[z * rows : (z + 1) * rows]] * 2
    u = u + jnp.concatenate(planes, axis=0)
    u = flat_sweep(u, q, rows, yd, xd)
    return flat_sweep(u, q, rows, yd, xd)


def solve_level_one(piece_refs, pencil, v_ref, q_ref, a_ref, b_ref, tmp_ref, shape, near=None):
    zs, ys, xs = shape
    rows = ys // 2
    half = zs // 2
    piece = rows // len(piece_refs)
    row = row_iota((rows, LANES))
    blank = jnp.zeros((rows, LANES), jnp.float32)
    for ref in (q_ref, a_ref, b_ref):
        for z in (0, 1, zs + 2, zs + 3):
            for c in range(2):
                ref[z, c] = blank
    for z in (0, 1, half + 2, half + 3):
        tmp_ref[pl.ds(z * rows, rows), :] = blank
    edge = jnp.zeros((HALO, LANES), jnp.float32)
    for z in range(zs + 2):
        v_ref[z, pl.ds(0, HALO), :] = edge
        v_ref[z, pl.ds(HALO + ys, HALO), :] = edge
    if near is None:
        for z in (0, zs + 1):
            for c in range(2):
                v_ref[z, pl.ds(HALO + c * rows, rows), :] = blank
    for z in range(zs):
        for c in range(2):
            for k, ref in enumerate(piece_refs):
                spot = pl.ds(2 * piece * z + c, piece, stride=2)
                to = pl.ds(pl.multiple_of((pencil ^ k) * piece, piece), piece)
                q_ref[z + 2, c, to, :] = ref[spot, :]

    def y_beyond(other, c):
        if c:
            return jnp.where(row == rows - 1, 0.0, pltpu.roll(other, rows - 1, 0))
        return jnp.where(row == 0, 0.0, pltpu.roll(other, 1, 0))

    def around(src, z):
        here = [src[z, 0], src[z, 1]]
        near = []
        for c in range(2):
            other = here[1 - c]
            sides = (other + y_beyond(other, c)) + x_sides(here[c], 1)
            near.append((src[z - 1, c] + src[z + 1, c]) + sides)
        return here, near

    def second(z, carry):
        here, sides = around(q_ref, z)
        for c in range(2):
            a_ref[z, c] = (1.0 + KEEP) * here[c] + W * sides[c]
        return carry

    lax.fori_loop(2, zs + 2, second, 0, unroll=LEVEL)

    def restrict(z, carry):
        total = None
        for at in (2 * z + 2, 2 * z + 3):
            here, sides = around(a_ref, at)
            for c in range(2):
                new = KEEP * here[c] + W * sides[c] + q_ref[at, c]
                b_ref[at, c] = new
                change = new - here[c]
                total = change if total is None else total + change
        spot = pl.ds(pl.multiple_of((z + 2) * rows, rows), rows)
        tmp_ref[spot, :] = 0.5 * pair_sum(total, 1, 1)
        return carry

    pairs_unroll = LPAIRS if near is None else half
    lax.fori_loop(0, half, restrict, 0, unroll=pairs_unroll)
    inner = pl.ds(2 * rows, half * rows)
    tmp_ref[inner, :] = flat_vcycle(tmp_ref[inner, :], (half, ys // 2, xs // 2), rows, 1, 2)

    def live(at, count):
        return jnp.where((at >= 0) & (at < count), 1.0, 0.0)

    def third(z):
        e = [tmp_ref[pl.ds(pl.multiple_of((z + k) * rows, rows), rows), :] for k in (1, 2, 3)]
        here = W * e[1]
        base = ((1.0 - 4.0 * W) / W) * here + x_sides(here, 1)
        for c in range(2):
            flat = base + y_beyond(here, c)
            for k in range(2):
                new = b_ref[2 * z + 2 + k, c] + (flat + W * e[2 * k])
                a_ref[2 * z + 2 + k, c] = new if near is None else live(z, half) * new

    def fourth(z):
        here, sides = around(a_ref, z + 2)
        for c in range(2):
            new = KEEP * here[c] + W * sides[c] + q_ref[z + 2, c]
            if near is not None:
                new = live(z, zs) * new
            v_ref[z + 1, pl.ds(HALO + c, rows, stride=2), :] = new

    def loop(step, start, count, unroll):
        def body(i, carry):
            step(start + i)
            return carry

        lax.fori_loop(0, count, body, 0, unroll=unroll)

    if near is None:
        loop(third, 0, half, LPAIRS)
        loop(fourth, 0, zs, LEVEL)
    else:
        loop(third, near - 1, 3, 3)
        loop(fourth, 2 * near - 1, 4, 4)


def pack_kernel(
    potential_hbm, store_hbm, out_ref, even_ref, odd_ref, potential_ref, store_ref, sems
):
    copies = [
        pltpu.make_async_copy(potential_hbm, potential_ref, sems.at[0]),
        pltpu.make_async_copy(store_hbm, store_ref, sems.at[1]),
    ]
    for copy in copies:
        copy.start()
    matrix = splitting_matrix()
    for copy in copies:
        copy.wait()
    depth, width, columns = potential_ref.shape
    slots = store_ref.shape[0]
    part = width // 2
    split = mm(potential_ref[...].reshape(depth * width, columns), matrix)
    even_ref[...] = split[:, :LANES]
    odd_ref[...] = split[:, LANES:]
    for z in range(depth):
        for c in range(4):
            ref = odd_ref if c & 1 else even_ref
            spot = pl.ds((4 * z + c) * part, part)
            out_ref[spot, :] = ref[pl.ds(z * width + (c >> 1), part, stride=2), :]
    base = depth * width * 2
    for slot in range(slots):
        for side in range(2):
            spot = pl.ds(base + side * depth, depth)
            out_ref[spot, pl.ds(slot * width, width)] = store_ref[slot, side]


OFFSETS = (0, 4, 3, 1, 2, 7, 5, 6)
EARLY = 5


def block_rows(ref, start, count):
    return ref[pl.ds(start, count), :]


def ends(load, first, second, part, low_half):
    head = jnp.where(low_half, load(first, 8), pltpu.roll(load(second, 8), 4, 0))
    tail = jnp.where(
        low_half, pltpu.roll(load(first + part - 8, 8), 4, 0), load(second + part - 8, 8)
    )
    return head, tail


def store_ends(ref, pencil, out_refs, at, depth, part):
    even_ref, odd_ref = out_refs
    is_even = (pencil % 2) == 0
    low_half = row_iota((8, LANES)) < 4
    for z in range(depth):
        for t in range(2):
            head, tail = ends(
                partial(block_rows, ref),
                (4 * z + 2 * t) * part, (4 * z + 2 * t + 1) * part, part, low_half,
            )
            even_ref[at + 2 * z + t] = jnp.where(is_even, tail, head)
            odd_ref[at + 2 * z + t] = jnp.where(is_even, head, tail)


def early_edges_kernel(scalar_ref, *refs, depth, width):
    blocks, out_refs = refs[:EARLY], refs[EARLY:]
    for k, ref in enumerate(blocks):
        store_ends(ref, scalar_ref[1], out_refs, 2 * depth * k, depth, width // 2)


def late_edges_kernel(scalar_ref, *refs, depth, width):
    slabs = len(OFFSETS)
    even_ref, odd_ref, faces_ref, store_ref, rows_ref = refs[slabs:]
    slab = scalar_ref[0]
    pencil = scalar_ref[1]
    planes = slabs * depth
    part = width // 2
    is_even = (pencil % 2) == 0
    low_half = row_iota((8, LANES)) < 4
    base = depth * width * 2
    late = refs[EARLY:slabs]
    for k, ref in enumerate(late):
        store_ends(ref, pencil, (even_ref, odd_ref), 2 * depth * k, depth, part)
    for offset, ref in zip(OFFSETS, refs):
        store_ref[slab ^ offset] = block_rows(ref, base, 8)
    rest = LANES - 2 * planes
    rows_ref[pl.ds(2 * planes, rest), :] = jnp.zeros((rest, LANES), jnp.float32)
    for s in range(slabs):
        tile = store_ref[scalar_ref[2 + s]]
        slot = scalar_ref[2 + slabs + s]
        picked = pltpu.roll(tile, (LANES - slot * width) & (LANES - 1), 1)
        rows_ref[pl.ds(s * depth, depth), :] = picked[:depth]
        rows_ref[pl.ds(planes + s * depth, depth), :] = picked[depth:]
    rows_ref[...] = rows_ref[...].T
    faces_ref[pl.ds(0, part), :] = rows_ref[pl.ds(0, part, stride=2), :]
    faces_ref[pl.ds(part, part), :] = rows_ref[pl.ds(1, part, stride=2), :]
    head, tail = ends(partial(block_rows, faces_ref), 0, part, part, low_half)
    even_ref[2 * depth * len(late)] = jnp.where(is_even, tail, head)
    odd_ref[2 * depth * len(late)] = jnp.where(is_even, head, tail)


def halo_tiles(even_ref, odd_ref, index, is_even, low_half):
    first = even_ref[index]
    second = odd_ref[index]
    above = jnp.where(is_even, first, second)
    below = jnp.where(is_even, second, first)
    return (
        jnp.where(low_half, above, pltpu.roll(below, 4, 0)),
        jnp.where(low_half, pltpu.roll(above, 4, 0), below),
    )


def join_planes(load, out_ref, left_ref, right_ref, depth, width):
    part = width // 2
    for z in range(depth):
        for c in range(4):
            ref = right_ref if c & 1 else left_ref
            ref[pl.ds(z * width + (c >> 1), part, stride=2), :] = load(z, c)
    rows = depth * width
    both = jnp.concatenate([left_ref[pl.ds(0, rows), :], right_ref[pl.ds(0, rows), :]], axis=1)
    out_ref[...] = mm(both, merging_matrix()).reshape(depth, width, 2 * LANES)


def hessian_parts(below, here, above):
    rise = [a - b for a, b in zip(above, below)]
    y_sum, y_rise, yz_rise = [], [], []
    for c in range(4):
        odd = c >> 1
        same, other = here[c ^ 2], y_other(here[c ^ 2], odd)
        y_sum.append(same + other)
        y_rise.append(other - same if odd else same - other)
        same, other = rise[c ^ 2], y_other(rise[c ^ 2], odd)
        yz_rise.append(other - same if odd else same - other)
    out = []
    for c in range(4):
        odd = c & 1
        same, other = here[c ^ 1], x_other(here[c ^ 1], odd)
        twice = 2.0 * here[c]
        pxx = same + other - twice
        pyy = y_sum[c] - twice
        pzz = below[c] + above[c] - twice
        same, other = rise[c ^ 1], x_other(rise[c ^ 1], odd)
        pxz = other - same if odd else same - other
        same, other = y_rise[c ^ 1], x_other(y_rise[c ^ 1], odd)
        pxy = other - same if odd else same - other
        cross = pxy * pxy + pxz * pxz + yz_rise[c] * yz_rise[c]
        out.append(pxx * pyy + (pxx + pyy) * pzz - 0.0625 * cross)
    return out


def face_part(face, c, z, planes):
    lane = lane_iota(face.shape)
    if c & 1:
        turned = pltpu.roll(face, LANES - 1 - planes - z, 1)
        return jnp.where(lane == LANES - 1, turned, 0.0)
    turned = pltpu.roll(face, (LANES - z) & (LANES - 1), 1)
    return jnp.where(lane == 0, turned, 0.0)


def fill_rows(p_ref, at, ref, depth, part):
    for z in range(depth):
        for c in range(4):
            p_ref[at + z, c, pl.ds(0, part), :] = block_rows(ref, (4 * z + c) * part, part)


def fill_halo(p_ref, at, edge_refs, tile, pencil, depth, part):
    is_even = (pencil % 2) == 0
    low_half = row_iota((8, LANES)) < 4
    for z in range(depth):
        for t in range(2):
            first, second = halo_tiles(*edge_refs, tile + 2 * z + t, is_even, low_half)
            p_ref[at + z, 2 * t, pl.ds(part, 8), :] = first
            p_ref[at + z, 2 * t + 1, pl.ds(part, 8), :] = second


def near_half_kernel(scalar_ref, *refs, depth, width, pencils):
    near = [k for k in range(EARLY) if OFFSETS[k] < 4]
    even_ref, odd_ref, faces_ref, p_ref, s_ref, q_ref, far_ref = refs[len(OFFSETS) :]
    slab = scalar_ref[0]
    pencil = scalar_ref[1]
    part = width // 2
    half = 4 * depth
    first_plane = (slab // 4) * half
    mask = halo_mask(pencil, pencils)
    blank = jnp.zeros(p_ref.shape[1:], jnp.float32)
    p_ref[0] = blank
    p_ref[half + 1] = blank
    for k, ref in enumerate(refs[: len(OFFSETS)]):
        at = ((slab ^ OFFSETS[k]) % 4) * depth + 1
        fill_rows(p_ref if k in near else far_ref, at, ref, depth, part)
        if k in near:
            fill_halo(p_ref, at, (even_ref, odd_ref), 2 * depth * k, pencil, depth, part)

    def body(j, carry):
        source = hessian_parts(parts(p_ref, j), parts(p_ref, j + 1), parts(p_ref, j + 2))
        for c in range(4):
            s_ref[j, c] = source[c][:part]
            face = faces_ref[pl.ds((c >> 1) * part, part), :]
            face = face_part(face, c, first_plane + j, 2 * half)
            at = first_plane + j + 2
            q_ref[at, c, pl.ds(0, part), :] = W * (face - source[c][:part])
            q_ref[at, c, pl.ds(part, 8), :] = (-W * mask) * source[c][part:]
        return carry

    lax.fori_loop(0, half, body, 0, unroll=HESS)


def far_half_kernel(scalar_ref, *refs, depth, width, pencils):
    far = [k for k in range(len(OFFSETS)) if OFFSETS[k] >= 4]
    early_refs, late_refs = refs[:2], refs[2:4]
    faces_ref, pn_ref, sn_ref = refs[4:7]
    s_ref, q_ref, u_ref, coarse_ref, p_ref, f_ref = refs[9:]
    slab = scalar_ref[0]
    pencil = scalar_ref[1]
    part = width // 2
    half = 4 * depth
    planes = 2 * half
    lower = slab < 4
    near_first = jnp.where(lower, 0, half)
    far_first = half - near_first
    is_even = (pencil % 2) == 0
    low_half = row_iota((8, LANES)) < 4
    mask = halo_mask(pencil, pencils)
    blank = jnp.zeros(p_ref.shape[1:], jnp.float32)
    for ref in (q_ref, u_ref):
        for z in (0, 1, planes + 2, planes + 3):
            ref[z] = blank
    p_ref[jnp.where(lower, half + 1, 0)] = blank
    p_ref[jnp.where(lower, 0, half + 1)] = pn_ref[jnp.where(lower, half, 1)]
    for k in far:
        at = ((slab ^ OFFSETS[k]) % 4) * depth + 1
        early = k < EARLY
        tile = 2 * depth * (k if early else k - EARLY)
        edge_refs = early_refs if early else late_refs
        fill_halo(p_ref, at, edge_refs, tile, pencil, depth, part)
    face_tile = 2 * depth * (len(OFFSETS) - EARLY)
    first, second = halo_tiles(*late_refs, face_tile, is_even, low_half)
    f_ref[0, pl.ds(0, part), :] = faces_ref[pl.ds(0, part), :]
    f_ref[0, pl.ds(part, 8), :] = first
    f_ref[1, pl.ds(0, part), :] = faces_ref[pl.ds(part, part), :]
    f_ref[1, pl.ds(part, 8), :] = second

    def finish(source, z):
        for c in range(4):
            face = face_part(f_ref[c >> 1], c, z, planes)
            put(q_ref, z + 2, c, W * (face - source[c]), mask)

    def copy(j, carry):
        z = near_first + j
        for c in range(4):
            face = face_part(f_ref[c >> 1, pl.ds(part, 8), :], c, z, planes)
            tile = pl.ds(part, 8)
            q_ref[z + 2, c, tile, :] = q_ref[z + 2, c, tile, :] + (W * mask) * face
        return carry

    lax.fori_loop(0, half, copy, 0, unroll=UNROLL)

    def body(j, carry):
        source = hessian_parts(parts(p_ref, j), parts(p_ref, j + 1), parts(p_ref, j + 2))
        finish(source, far_first + j)
        return carry

    lax.fori_loop(0, half, body, 0, unroll=HESS)
    seam = jnp.where(lower, half, 1)
    here = parts(pn_ref, seam)
    inner = parts(pn_ref, jnp.where(lower, half - 1, 2))
    outer = parts(p_ref, jnp.where(lower, 1, half))
    below = [jnp.where(lower, a, b) for a, b in zip(inner, outer)]
    above = [jnp.where(lower, b, a) for a, b in zip(inner, outer)]
    source = hessian_parts(below, here, above)
    finish(source, near_first + seam - 1)
    own = (slab % 4) * depth
    for z in range(depth):
        is_seam = own + z == seam - 1
        for c in range(4):
            s_ref[z, c] = jnp.where(is_seam, source[c][:part], sn_ref[own + z, c])
    def second_sweep(z, carry):
        here = parts(q_ref, z + 2)
        for c in range(4):
            sides = neighbours(q_ref[z + 1, c], here, q_ref[z + 3, c], c)
            put(u_ref, z + 2, c, (1.0 + KEEP) * here[c] + W * sides, mask)
        return carry

    lax.fori_loop(0, planes, second_sweep, 0, unroll=UNROLL)
    restrict_window(u_ref, q_ref, coarse_ref, planes, part)


def restrict_window(u_ref, q_ref, coarse_ref, planes, part):
    def restrict(z, carry):
        total = None
        for at in (2 * z + 2, 2 * z + 3):
            here = parts(u_ref, at)
            for c in range(4):
                new = swept(u_ref[at - 1, c], here, u_ref[at + 1, c], q_ref[at, c], c)
                change = new[:part] - here[c][:part]
                total = change if total is None else total + change
        coarse_ref[pl.ds(pl.multiple_of(z * part, part), part), :] = 0.5 * total
        return carry

    lax.fori_loop(0, planes // 2, restrict, 0, unroll=PAIRS)


def between_kernel(scalar_ref, q_ref, u_ref, s_ref, source_hbm, swept_ref, *refs, pencils):
    left_ref, right_ref, source_ref, sem = refs
    depth, width, _ = source_ref.shape
    planes = q_ref.shape[0] - 4
    mask = halo_mask(scalar_ref[1], pencils)
    join_planes(lambda z, c: s_ref[z, c], source_ref, left_ref, right_ref, depth, width)
    copy_out = pltpu.make_async_copy(source_ref, source_hbm, sem)
    copy_out.start()

    def sweep(z, carry):
        here = parts(u_ref, z + 2)
        for c in range(4):
            new = swept(u_ref[z + 1, c], here, u_ref[z + 3, c], q_ref[z + 2, c], c)
            put(swept_ref, z + 2, c, new, mask)
        return carry

    lax.fori_loop(0, planes, sweep, 0, unroll=UNROLL)
    copy_out.wait()


def window_kernel(scalar_ref, qwin_ref, uwin_ref, win_ref, *, pencils):
    mask = halo_mask(scalar_ref[1], pencils)
    for z in range(win_ref.shape[0]):
        here = parts(uwin_ref, z + 1)
        for c in range(4):
            new = swept(uwin_ref[z, c], here, uwin_ref[z + 2, c], qwin_ref[z, c], c)
            put(win_ref, z, c, new, mask)


def coarse_window(v_ref, z, pencil, part):
    start = pl.multiple_of(pencil * part, part)
    own = v_ref[z, pl.ds(start + HALO, part), :]
    above = v_ref[z, pl.ds(start + HALO + part, 8), :]
    below = v_ref[z, pl.ds(start, 8), :]
    tile = jnp.where(row_iota((8, LANES)) < 4, above, below)
    return jnp.concatenate([own, tile], axis=0)


def middle_kernel(
    scalar_ref, c0_ref, c1_ref, c2_ref, c3_ref, q_ref, swept_ref,
    qwin_ref, uwin_ref, coarse_ref,
    v_ref, q1_ref, a1_ref, b1_ref, tmp_ref, a_ref, b_ref, *, depth, width, pencils, shape
):
    slab = scalar_ref[0]
    pencil = scalar_ref[1]
    planes = a_ref.shape[0] - 4
    part = width // 2
    mask = halo_mask(pencil, pencils)
    piece_refs = (c0_ref, c1_ref, c2_ref, c3_ref)
    solve_level_one(piece_refs, pencil, v_ref, q1_ref, a1_ref, b1_ref, tmp_ref, shape)
    blank = jnp.zeros(a_ref.shape[1:], jnp.float32)
    for ref in (a_ref, b_ref):
        for z in (0, 1, planes + 2, planes + 3):
            ref[z] = blank

    def third_sweep(z, carry):
        v = [coarse_window(v_ref, z + k, pencil, part) for k in range(3)]
        for k, children in enumerate(swept_children(*v)):
            at = 2 * z + 2 + k
            for c in range(4):
                put(a_ref, at, c, swept_ref[at, c] + children[c], mask)
        return carry

    lax.fori_loop(0, planes // 2, third_sweep, 0, unroll=PAIRS)

    def sweep(src, dst):
        def body(z, carry):
            here = parts(src, z + 2)
            for c in range(4):
                new = swept(src[z + 1, c], here, src[z + 3, c], q_ref[z + 2, c], c)
                put(dst, z + 2, c, new, mask)
            return carry

        lax.fori_loop(0, planes, body, 0, unroll=UNROLL)

    sweep(a_ref, b_ref)
    sweep(b_ref, a_ref)
    sweep(a_ref, b_ref)
    restrict_window(b_ref, q_ref, coarse_ref, planes, part)
    for z in range(depth + 2):
        qwin_ref[z] = q_ref[slab * depth + z + 1]
    for z in range(depth + 4):
        uwin_ref[z] = b_ref[slab * depth + z]


def last_kernel(
    scalar_ref, c0_ref, c1_ref, c2_ref, c3_ref, qwin_ref, win_ref, out_hbm,
    v_ref, q1_ref, a1_ref, b1_ref, tmp_ref, a_ref, left_ref, right_ref, out_ref, sems,
    *, depth, width, pencils, shape
):
    slab = scalar_ref[0]
    pencil = scalar_ref[1]
    planes = shape[0] * 2
    part = width // 2
    mask = halo_mask(pencil, pencils)
    piece_refs = (c0_ref, c1_ref, c2_ref, c3_ref)
    solve_level_one(piece_refs, pencil, v_ref, q1_ref, a1_ref, b1_ref, tmp_ref, shape, slab)
    blank = jnp.zeros((part + 8, LANES), jnp.float32)
    v = [coarse_window(v_ref, slab * (depth // 2) + k, pencil, part) for k in range(4)]
    v = [blank] + v + [blank]
    for k in range(4):
        for side, children in enumerate(swept_children(*v[k : k + 3])):
            z = 2 * k + side - 1
            if 0 <= z < depth + 2:
                at = slab * depth - 1 + z
                live = jnp.where((at >= 0) & (at < planes), 1.0, 0.0)
                for c in range(4):
                    put(a_ref, z, c, live * (win_ref[z, c] + children[c]), mask)
    matrix = merging_matrix()
    copies = []
    for z in range(depth):
        here = parts(a_ref, z + 1)
        for c in range(4):
            new = swept(a_ref[z, c], here, a_ref[z + 2, c], qwin_ref[z + 1, c], c)
            ref = right_ref if c & 1 else left_ref
            ref[z, pl.ds(c >> 1, part, stride=2), :] = new[:part]
        out_ref[z] = mm(jnp.concatenate([left_ref[z], right_ref[z]], axis=1), matrix)
        copies.append(pltpu.make_async_copy(out_ref.at[z], out_hbm.at[z], sems.at[z]))
        copies[-1].start()
    for copy in copies:
        copy.wait()


def vmem():
    return pl.BlockSpec(memory_space=pltpu.VMEM)


def smem():
    return pl.BlockSpec(memory_space=pltpu.SMEM)


def arr(*shape):
    return jax.ShapeDtypeStruct(shape, jnp.float32)


def buf(*shape):
    return pltpu.VMEM(shape, jnp.float32)


def call(kernel, name, scalars, args, outs, scratch=(), space=pltpu.VMEM, out_space=None, aliases={}):
    out_specs = jax.tree.map(lambda _: vmem(), outs)
    if out_space is not None:
        out_specs = tuple(pl.BlockSpec(memory_space=one) for one in out_space)
    return pl.pallas_call(
        kernel,
        out_shape=outs,
        in_specs=[smem()] * len(scalars) + [pl.BlockSpec(memory_space=space)] * len(args),
        out_specs=out_specs,
        scratch_shapes=list(scratch),
        compiler_params=pltpu.CompilerParams(vmem_limit_bytes=16 << 20),
        name=name,
        input_output_aliases=aliases,
    )(*scalars, *args)


def windowed(potential, parent_store, face_owner, face_offset):
    depth, width, columns = potential.shape
    slabs = lax.axis_size("slab")
    pencils = lax.axis_size("pencil")
    planes, height = slabs * depth, pencils * width
    part = width // 2
    rows = part + 8
    where = jnp.stack([lax.axis_index("slab"), lax.axis_index("pencil")]).astype(jnp.int32)
    scalars = jnp.concatenate([where, face_owner, face_offset])
    own = call(
        pack_kernel,
        "pack",
        [],
        [pltpu.with_memory_space_constraint(x, pltpu.HBM) for x in (potential, parent_store)],
        arr(depth * width * 2 + 8, LANES),
        [
            buf(depth * width, LANES),
            buf(depth * width, LANES),
            buf(*potential.shape),
            buf(*parent_store.shape),
            pltpu.SemaphoreType.DMA((2,)),
        ],
        space=pltpu.HBM,
    )

    def swap(x, bits):
        return lax.ppermute(x, "slab", [(i, i ^ bits) for i in range(slabs)])

    near = [swap(own, bits) for bits in OFFSETS[1:5]]
    blocks = [own, *near] + [swap(near[0], bits) for bits in OFFSETS[2:5]]
    low_pairs = [(i, i + 1) for i in range(0, pencils - 1, 2)]
    high_pairs = [(i, i + 1) for i in range(1, pencils - 1, 2)]

    def beside(even, odd):
        return (
            lax.ppermute(even, "pencil", low_pairs + [(j, i) for i, j in low_pairs]),
            lax.ppermute(odd, "pencil", high_pairs + [(j, i) for i, j in high_pairs]),
        )

    message = arr(2 * depth * EARLY, 8, LANES)
    early = call(
        partial(early_edges_kernel, depth=depth, width=width),
        "early_edges",
        [scalars],
        blocks[:EARLY],
        (message, message),
    )
    early = beside(*early)
    message = arr(2 * depth * (slabs - EARLY) + 1, 8, LANES)
    even, odd, faces = call(
        partial(late_edges_kernel, depth=depth, width=width),
        "late_edges",
        [scalars],
        blocks,
        (message, message, arr(width, LANES)),
        [buf(slabs, 8, LANES), buf(LANES, LANES)],
    )
    late = beside(even, odd)
    shape = (planes // 2, height // 2, columns // 2)
    coarse_part = arr(planes // 2 * part, LANES)
    field = (planes + 4, 4, rows, LANES)
    half = planes // 2
    near = call(
        partial(near_half_kernel, depth=depth, width=width, pencils=pencils),
        "near_half",
        [scalars],
        [*blocks, *early, faces],
        (
            arr(half + 2, 4, rows, LANES),
            arr(half, 4, part, LANES),
            arr(*field),
            arr(half + 2, 4, rows, LANES),
        ),
    )
    own_source, q, u, coarse, _ = call(
        partial(far_half_kernel, depth=depth, width=width, pencils=pencils),
        "far_half",
        [scalars],
        [*early, *late, faces, *near],
        (
            arr(depth, 4, part, LANES),
            arr(*field),
            arr(*field),
            coarse_part,
            arr(half + 2, 4, rows, LANES),
        ),
        [buf(2, rows, LANES)],
        aliases={8: 1, 9: 4},
    )

    def pair(x, bits):
        return lax.ppermute(x, "pencil", [(i, i ^ bits) for i in range(pencils)])

    def gather(x, meanwhile):
        beside, across = pair(x, 1), pair(x, 2)
        made = meanwhile()
        across, made = lax.optimization_barrier((across, made))
        return [x, beside, across, pair(across, 1)], made

    between = lambda: call(
        partial(between_kernel, pencils=pencils),
        "between",
        [scalars],
        [q, u, own_source],
        (arr(depth, width, columns), arr(*field)),
        [
            buf(depth * width, LANES),
            buf(depth * width, LANES),
            buf(depth, width, columns),
            pltpu.SemaphoreType.DMA,
        ],
        out_space=[pl.ANY, pltpu.VMEM],
    )
    pieces, (source, swept_once) = gather(coarse, between)
    level = (shape[0] + 4, 2, shape[1] // 2, LANES)
    level_scratch = [
        buf(shape[0] + 2, shape[1] + 2 * HALO, LANES),
        buf(*level),
        buf(*level),
        buf(*level),
        buf((shape[0] // 2 + 4) * shape[1] // 2, LANES),
    ]
    sizes = dict(depth=depth, width=width, pencils=pencils, shape=shape)
    qwin, uwin, coarse = call(
        partial(middle_kernel, **sizes),
        "middle",
        [scalars],
        [*pieces, q, swept_once],
        (arr(depth + 2, 4, rows, LANES), arr(depth + 4, 4, rows, LANES), coarse_part),
        level_scratch + [buf(*field), buf(*field)],
    )
    window = lambda: call(
        partial(window_kernel, pencils=pencils),
        "window",
        [scalars],
        [qwin, uwin],
        arr(depth + 2, 4, rows, LANES),
    )
    pieces, win = gather(coarse, window)
    (solved,) = call(
        partial(last_kernel, **sizes),
        "last",
        [scalars],
        [*pieces, qwin, win],
        (arr(depth, width, columns),),
        level_scratch
        + [
            buf(depth + 2, 4, rows, LANES),
            buf(depth, width, LANES),
            buf(depth, width, LANES),
            buf(depth, width, columns),
            pltpu.SemaphoreType.DMA((depth,)),
        ],
        out_space=[pl.ANY],
    )
    return solved, source


def fits_window(potential, parent_store):
    depth, width, columns = potential.shape
    slabs = lax.axis_size("slab")
    pencils = lax.axis_size("pencil")
    planes = slabs * depth
    return (
        slabs == 8
        and depth == 4
        and columns == 2 * LANES
        and width == 32
        and parent_store.shape[0] * width == LANES
        and 2 * planes < LANES
        and pencils == 4
    )


def padded(cells, sides, width):
    for axis, dim in sides:
        count = lax.axis_size(axis)
        ends = count - 1
        head = lax.slice_in_dim(cells, 0, width, axis=dim)
        tail = lax.slice_in_dim(cells, cells.shape[dim] - width, cells.shape[dim], axis=dim)
        cells = jnp.concatenate(
            [
                lax.ppermute(tail, axis, [(i, (i + 1) % count) for i in range(ends)]),
                cells,
                lax.ppermute(head, axis, [((i + 1) % count, i) for i in range(ends)]),
            ],
            axis=dim,
        )
    return cells


def hessian_source(p):
    c = p[1:-1, 1:-1, 1:-1]
    pxx = p[1:-1, 1:-1, 2:] + p[1:-1, 1:-1, :-2] - 2.0 * c
    pyy = p[1:-1, 2:, 1:-1] + p[1:-1, :-2, 1:-1] - 2.0 * c
    pzz = p[2:, 1:-1, 1:-1] + p[:-2, 1:-1, 1:-1] - 2.0 * c
    pxy = 0.25 * (p[1:-1, 2:, 2:] - p[1:-1, :-2, 2:] - p[1:-1, 2:, :-2] + p[1:-1, :-2, :-2])
    pxz = 0.25 * (p[2:, 1:-1, 2:] - p[:-2, 1:-1, 2:] - p[2:, 1:-1, :-2] + p[:-2, 1:-1, :-2])
    pyz = 0.25 * (p[2:, 2:, 1:-1] - p[:-2, 2:, 1:-1] - p[2:, :-2, 1:-1] + p[:-2, :-2, 1:-1])
    return pxx * pyy + pxx * pzz + pyy * pzz - pxy * pxy - pxz * pxz - pyz * pyz


def apply_padded(p, level):
    c = p[1:-1, 1:-1, 1:-1]
    near = p[2:, 1:-1, 1:-1] + p[:-2, 1:-1, 1:-1]
    near = near + p[1:-1, 2:, 1:-1] + p[1:-1, :-2, 1:-1]
    near = near + p[1:-1, 1:-1, 2:] + p[1:-1, 1:-1, :-2]
    return (6.0 * c - near) * 0.25**level


def step_weight(level):
    return OMEGA / 6.0 * 4.0**level


def sweep_whole(u, rhs, level):
    return u + step_weight(level) * (rhs - apply_padded(jnp.pad(u, 1), level))


def restrict(r):
    a, b, c = r.shape
    return r.reshape(a // 2, 2, b // 2, 2, c // 2, 2).mean(axis=(1, 3, 5))


def prolong(e):
    a, b, c = e.shape
    return jnp.broadcast_to(e[:, None, :, None, :, None], (a, 2, b, 2, c, 2)).reshape(
        2 * a, 2 * b, 2 * c
    )


def vcycle(u, rhs, level):
    if is_coarsest(rhs.shape):
        for sweep_count in range(8):
            u = sweep_whole(u, rhs, level)
        return u
    u = sweep_whole(u, rhs, level)
    u = sweep_whole(u, rhs, level)
    resid = rhs - apply_padded(jnp.pad(u, 1), level)
    coarse = restrict(resid)
    correction = vcycle(jnp.zeros_like(coarse), coarse, level + 1)
    u = u + prolong(correction)
    u = sweep_whole(u, rhs, level)
    u = sweep_whole(u, rhs, level)
    return u


def widen_x(p):
    return jnp.pad(p, ((0, 0), (0, 0), (1, 1)))


def rim_one(u):
    return widen_x(padded(u, (("slab", 0), ("pencil", 1)), 1))


def coarse_solve(rhs, level):
    width = rhs.shape[1]
    columns = rhs.shape[2]
    whole = lax.all_gather(rhs, ("slab", "pencil"), axis=0, tiled=True)
    whole = whole.reshape(lax.axis_size("slab"), lax.axis_size("pencil") * width, columns)
    solved = vcycle(jnp.zeros_like(whole), whole, level)
    start_y = lax.axis_index("pencil") * width
    return lax.dynamic_slice(
        solved, (lax.axis_index("slab"), start_y, jnp.int32(0)), (1, width, columns)
    )


def split_vcycle(u, rhs, level, from_zero):
    if rhs.shape[0] == 1:
        return coarse_solve(rhs, level)
    weight = step_weight(level)
    if from_zero:
        u = weight * rhs
    else:
        u = u + weight * (rhs - apply_padded(rim_one(u), level))
    u = u + weight * (rhs - apply_padded(rim_one(u), level))
    resid = rhs - apply_padded(rim_one(u), level)
    correction = split_vcycle(None, restrict(resid), level + 1, True)
    u = u + prolong(correction)
    u = u + weight * (rhs - apply_padded(rim_one(u), level))
    u = u + weight * (rhs - apply_padded(rim_one(u), level))
    return u


def plain(potential, parent_store, face_owner, face_offset):
    depth, width, columns = potential.shape
    grown = widen_x(padded(potential, (("slab", 0), ("pencil", 1)), 1))
    source = hessian_source(grown)
    slab_index = lax.axis_index("slab")
    wanted = face_owner[slab_index] * parent_store.shape[0] + face_offset[slab_index]
    piece = lax.all_gather(parent_store, "slab", axis=0, tiled=True)
    labels = jnp.arange(piece.shape[0], dtype=jnp.int32)
    match = labels == wanted
    faces = jnp.sum(jnp.where(match[:, None, None, None], piece, 0.0), axis=0)
    rhs = -source
    rhs = rhs.at[:, :, 0].add(faces[0])
    rhs = rhs.at[:, :, columns - 1].add(faces[1])
    solved = jnp.zeros_like(rhs)
    for cycle in range(CYCLES):
        solved = split_vcycle(solved, rhs, 0, cycle == 0)
    return (solved, source)


def on_device(potential, parent_store, face_owner, face_offset):
    if fits_window(potential, parent_store):
        return windowed(potential, parent_store, face_owner, face_offset)
    return plain(potential, parent_store, face_owner, face_offset)


def solution(mesh):
    in_specs = (P("slab", "pencil", None), P("slab", None, None, "pencil"), P(), P())
    out_specs = (P("slab", "pencil", None), P("slab", "pencil", None))
    return jax.shard_map(
        on_device, mesh=mesh, in_specs=in_specs, out_specs=out_specs, check_vma=False
    )
```
